128 devices in a mesh: solver: 4 (over y), space: 32 (over z, x, core).
Axes of the slice: x: 4, y: 4, z: 4, core: 2. Of those that a mesh axis runs over, the one named last changes fastest.
Arguments:
- pressure_start: float32 [512, 256, 512], P(('solver', 'space')), may hold values from -6 to 6
- fluid_coef: float32 [512, 256, 512], P(('solver', 'space')), may hold values from 0.25 to 2
- fluid_rhs: float32 [512, 256, 512], P(('solver', 'space')), may hold values from -6 to 6
- wall_start: float32 [3, 8, 512, 256], P(None, None, ('solver', 'space')), may hold values from -4 to 4
- wall_stiff: float32 [8, 512, 256], P(None, ('solver', 'space')), may hold values from 0.5 to 4
- wall_load: float32 [3, 8, 512, 256], P(None, None, ('solver', 'space')), may hold values from -6 to 6
- normals: float32 [3, 131072], P(None, ('solver', 'space')), may hold values from -4 to 4
- fluid_owner: int32 [131072, 1], P(('solver', 'space')), may hold values from 0 to 127; in each aligned block of 1024 rows (0 to 1023, 1024 to 2047, ...) at most 16 rows name the same one
- fluid_cell: int32 [131072], P(('solver', 'space')), may hold values from 0 to 524287
- interface_start: float32 [6, 131072], P(None, ('solver', 'space')), may hold values from -6 to 6
- past_residual: float32 [32, 6, 131072], P(None, None, ('solver', 'space')), may hold values from -4 to 4
- past_output: float32 [32, 6, 131072], P(None, None, ('solver', 'space')), may hold values from -4 to 4
Outputs:
- interface_next: float32 [6, 131072], P(None, ('solver', 'space'))
- pressure: float32 [512, 256, 512], P(('solver', 'space'))
- wall: float32 [3, 8, 512, 256], P(None, None, ('solver', 'space'))
The draws below stay inside these ranges and needn't reach their ends.
Inputs may be any that keep to these rules, and one draw needn't show every extreme that they name: `fluid_owner`: among the 1024 interface points of one device, at most 16 have the same fluid owner.
All inputs are finite; a program needn't handle non-finite values.
Results may differ from the reference program's by a relative error of at most 0.00011.
Values sent between devices are 32-bit elements; how exact they have to be, the bound alone decides.
A program may use at most 64 MiB of HBM per device.

```python
import math
import jax
import jax.numpy as jnp
import numpy as np
from jax import lax

CX = 4
NY = 256
NZ = 512
SWEEPS = 4
S2 = 256
S3 = 8
KRYLOV = 2
COUPLE = 2
HIST = 32
NX = 512
NS1 = 512
IF_DEV = 1024
NI = 131072
MOST = 16
DEVICES = 128


def place_ends(entries, own_key, least, high):
    place = [jax.random.randint(jax.random.fold_in(own_key, axis), (), 0, length) for axis, length in enumerate(entries.shape)]
    widest = entries.shape.index(max(entries.shape))
    beside = place[:widest] + [(place[widest] + 1) % entries.shape[widest]] + place[widest + 1:]
    return entries.at[tuple(place)].set(least).at[tuple(beside)].set(high)


def level_of(own_key, dims, split, low, largest):
    loudness, own = 1.0, jax.random.fold_in(own_key, 6)
    for position, parts in split:
        draws = jnp.exp(jax.random.uniform(jax.random.fold_in(own, position), (parts,), jnp.float32, low / len(split), largest / len(split)))
        loudness = loudness * jnp.repeat(draws, dims[position] // parts).reshape([-1 if axis == position else 1 for axis in range(len(dims))])
    return loudness


def shared_out(stream_key, own, number, rows, amount, top, reach, lean):
    ranking = jax.random.permutation(stream_key, amount)
    heavy_load, usual = shares(amount, rows * top, reach, lean, True), shares(amount, rows * top, reach, lean, False)
    places = jnp.arange(amount)

    def named(tallies, turn):
        used = int((tallies > 0).sum())
        fixed = max(1, used // 4)
        shifted = fixed + (places - fixed + turn * (used - fixed)) % max(1, amount - fixed)
        return jnp.zeros((amount,), jnp.int32).at[ranking[jnp.where(places < fixed, places, shifted)]].set(jnp.asarray(tallies, jnp.int32))

    tallies = jnp.where(number % 4 == 0, named(heavy_load, number // 4), named(usual, number - number // 4 - 1))
    mixed = jax.random.permutation(jax.random.fold_in(own, 3), amount)
    donor, taker = mixed[0:amount // 2 * 2:2], mixed[1:amount // 2 * 2:2]
    margin = jnp.minimum(tallies[donor] - 1, reach - tallies[taker]) // 2
    margin = jnp.where((donor == ranking[0]) | (taker == ranking[0]) | (tallies[taker] == 0), 0, jnp.maximum(margin, 0))
    shifted = jax.random.randint(jax.random.fold_in(own, 4), (amount // 2,), 0, 1 << 20) % (margin + 1)
    tallies = tallies.at[donor].add(-shifted).at[taker].add(shifted)
    members = jnp.searchsorted(jnp.cumsum(tallies), jnp.arange(rows * top), side="right").astype(jnp.int32)
    grid = members.reshape(top, rows).T
    grid = grid[jax.random.permutation(jax.random.fold_in(own, 1), rows)]
    turn = jax.random.randint(jax.random.fold_in(own, 2), (rows, 1), 0, top)
    return jnp.take_along_axis(grid, (jnp.arange(top)[None, :] + turn) % top, axis=1)


def shares(amount, total, most, skew, full):
    loads = [(1 << 20) // math.isqrt(grade ** skew) + 1 for grade in range(1, amount + 1)]
    largest = most if full else min(most, max(-(-total // amount), total * loads[0] // sum(loads)))
    least = 1 if total - largest >= amount - 1 else 0
    holding, spare = [largest] + [least] * (amount - 1), total - largest - least * (amount - 1)
    while spare > 0:
        free = [i for i in range(1, amount) if holding[i] < largest] or [i for i in range(1, amount) if holding[i] < most]
        pool, left = sum([loads[i] for i in free]), spare
        for i in free:
            extra = min(most - holding[i], max(1, left * loads[i] // pool), spare)
            holding[i] = holding[i] + extra
            spare = spare - extra
    return np.array(holding)


def normal_values(key, shape, width, most, cuts=(), kind=jnp.bfloat16):
    gain = level_of(key, shape, cuts, -0.22, 0.18) if cuts else 1.0
    values = jax.random.normal(key, shape, jnp.float32) * width * gain
    return jnp.minimum(jnp.maximum(values, -most), most).astype(kind)


def setup_inputs(seed: int = 0) -> dict:
    key_list = jax.random.split(jax.random.key(seed), 13)
    pressure_start = normal_values(key_list[0], (NX, NY, NZ), 1.0, 6.0, ((0, 128),), jnp.float32)
    fluid_coef = jnp.clip(0.25 + 1.75 * jax.random.uniform(key_list[1], (NX, NY, NZ), jnp.float32) ** level_of(key_list[1], (NX, NY, NZ), ((0, 128),), -0.2, 0.2), 0.25, 2.0)
    fluid_rhs = normal_values(key_list[2], (NX, NY, NZ), 1.0, 6.0, ((0, 128),), jnp.float32)
    wall_start = normal_values(key_list[3], (3, S3, NS1, S2), 0.5, 4.0, ((2, 128),), jnp.float32)
    wall_stiff = jnp.clip(jnp.exp(math.log(4.0) - 2.0794415 * jax.random.uniform(key_list[4], (S3, NS1, S2), jnp.float32) ** level_of(key_list[4], (S3, NS1, S2), ((1, 128),), -0.2, 0.2)), 0.5, 4.0)
    wall_load = normal_values(key_list[5], (3, S3, NS1, S2), 1.0, 6.0, ((2, 128),), jnp.float32)
    normals = normal_values(key_list[6], (3, NI), 0.6, 4.0, ((1, 128),), jnp.float32)
    fluid_owner_keys = jax.random.split(jax.random.fold_in(key_list[7], 1), NI // IF_DEV)
    fluid_owner_turns = jax.random.permutation(jax.random.fold_in(key_list[7], 3), NI // IF_DEV)
    fluid_owner = jax.vmap(lambda own, number: shared_out(jax.random.fold_in(key_list[7], 2), own, number, IF_DEV, DEVICES, 1, MOST, 2))(fluid_owner_keys, fluid_owner_turns).reshape((NI, 1))
    fluid_cell = place_ends(jax.random.randint(key_list[8], (NI,), 0, CX * NY * NZ), jax.random.fold_in(key_list[8], 1), 0, (CX * NY * NZ) - 1).astype(jnp.int32)
    interface_start = normal_values(key_list[9], (6, NI), 1.0, 6.0, ((1, 128),), jnp.float32)
    past_residual = normal_values(key_list[10], (HIST, 6, NI), 0.5, 4.0, ((2, 128),), jnp.float32)
    past_output = normal_values(key_list[11], (HIST, 6, NI), 0.5, 4.0, ((2, 128),), jnp.float32)
    return {"pressure_start": pressure_start, "fluid_coef": fluid_coef, "fluid_rhs": fluid_rhs, "wall_start": wall_start, "wall_stiff": wall_stiff, "wall_load": wall_load, "normals": normals, "fluid_owner": fluid_owner, "fluid_cell": fluid_cell, "interface_start": interface_start, "past_residual": past_residual, "past_output": past_output}


OMEGA = 0.8
SOURCE_GAIN = 4.0
RIDGE = 0.1
TINY = 1e-06

def fluid_sweep(field, rhs, diag):
    padded = jnp.pad(field, 1)
    beside = padded[2:, 1:-1, 1:-1] + padded[:-2, 1:-1, 1:-1]
    beside = beside + padded[1:-1, 2:, 1:-1] + padded[1:-1, :-2, 1:-1]
    beside = beside + padded[1:-1, 1:-1, 2:] + padded[1:-1, 1:-1, :-2]
    return (1.0 - OMEGA) * field + OMEGA * (rhs + beside) / diag

def wall_apply(field, stiff):
    padded = jnp.pad(field, ((0, 0), (1, 1), (1, 1), (0, 0)))
    beside = padded[:, 2:, 1:-1] + padded[:, :-2, 1:-1] + padded[:, 1:-1, 2:] + padded[:, 1:-1, :-2]
    beside = beside + jnp.roll(field, 1, 3) + jnp.roll(field, -1, 3)
    return (6.0 + stiff) * field - beside

def wall_solve(force, stiff):
    solution = jnp.zeros_like(force)
    residual = force
    direction = force
    norm_now = jnp.sum(residual * residual)
    for step in range(KRYLOV):
        image = wall_apply(direction, stiff)
        alpha = norm_now / jnp.sum(direction * image)
        solution = solution + alpha * direction
        residual = residual - alpha * image
        if step + 1 < KRYLOV:
            norm_next = jnp.sum(residual * residual)
            direction = residual + norm_next / norm_now * direction
            norm_now = norm_next
    return solution

def reference(pressure_start, fluid_coef, fluid_rhs, wall_start, wall_stiff, wall_load, normals, fluid_owner, fluid_cell, interface_start, past_residual, past_output):
    highest = lax.Precision.HIGHEST
    where = (fluid_owner[:, 0] * (CX * NY * NZ) + fluid_cell).astype(jnp.int32)
    diag = 6.0 + fluid_coef
    base = wall_load - wall_apply(wall_start, wall_stiff)
    state = interface_start
    pressure = pressure_start
    stack_res = past_residual
    stack_out = past_output
    last_res = state
    last_out = state
    wall = wall_start
    for turn in range(COUPLE):
        displace = state[0:3]
        traction = state[3:6]
        flux = SOURCE_GAIN * jnp.sum(normals * displace, axis=0)
        source = jnp.zeros((NX * NY * NZ,), jnp.float32).at[where].add(flux).reshape(NX, NY, NZ)
        rhs = fluid_rhs + source
        for sweep in range(SWEEPS):
            pressure = fluid_sweep(pressure, rhs, diag)
        fluid_out = -pressure.reshape(-1)[where][None, :] * normals
        force = base.at[:, 0].add(traction.reshape(3, NS1, S2))
        wall = wall_start + wall_solve(force, wall_stiff)
        solid_out = wall[:, 0].reshape(3, NI)
        output = jnp.concatenate([solid_out, fluid_out], axis=0)
        resid = output - state
        if turn > 0:
            stack_res = jnp.concatenate([(resid - last_res)[None], stack_res[:-1]], axis=0)
            stack_out = jnp.concatenate([(output - last_out)[None], stack_out[:-1]], axis=0)
        last_res = resid
        last_out = output
        gram = jnp.einsum('aci,bci->ab', stack_res, stack_res, precision=highest)
        proj = jnp.einsum('aci,ci->a', stack_res, resid, precision=highest)
        ridge = RIDGE * jnp.trace(gram) / HIST + TINY
        factor = jnp.linalg.cholesky(gram + ridge * jnp.eye(HIST, dtype=jnp.float32))
        half = lax.linalg.triangular_solve(factor, proj[:, None], left_side=True, lower=True)
        coeffs = -lax.linalg.triangular_solve(factor, half, left_side=True, lower=True, transpose_a=True)[:, 0]
        state = output + jnp.einsum('a,aci->ci', coeffs, stack_out, precision=highest)
    return (state, pressure, wall)
```

```python
import functools

import jax
import jax.numpy as jnp
from jax import lax
from jax.experimental import pallas as pl
from jax.experimental.pallas import tpu as pltpu
from jax.sharding import PartitionSpec as P

SWEEPS = 4
COUPLE = 2
OMEGA = 0.8
SOURCE_GAIN = 4.0
RIDGE = 0.1
TINY = 1e-06
SLOTS = 16
LANES = 128
MESH = pl.DeviceIdType.MESH
F32 = jnp.float32
BF16 = jnp.bfloat16
BOTH = ("solver", "space")
CELLS, WEIGHTS, SOLID, FIRST, BACK, BACK2, LAST = range(7)
ROUNDS = 7


def iota(shape, dim):
    return lax.broadcasted_iota(jnp.int32, shape, dim)


def dot(a, b, contract, exact=False):
    return lax.dot_general(
        a,
        b,
        (((contract[0],), (contract[1],)), ((), ())),
        precision=lax.Precision.HIGHEST if exact else None,
        preferred_element_type=F32,
    )


def mask(flag):
    return jnp.where(flag, 1.0, 0.0).astype(F32)


def eliminate(m, size):
    row = iota(m.shape, 0)
    for k in range(size):
        pivot_row = m[k : k + 1, :] / m[k : k + 1, k : k + 1]
        m = jnp.where(row == k, pivot_row, m - m[:, k : k + 1] * pivot_row)
    return m


def kernel(cfg, *refs):
    (D, SP, LO, CX, NY, NZ, L3, W1, S2, IF, H, NCH, RC) = cfg
    HI = D // LO
    R, K = CX * NY, SLOTS * D
    (
        p_hbm, coef_hbm, rhs_hbm, ws_hbm, stiff_hbm, load_hbm, normal_hbm, owner_hbm, cell_hbm, x_hbm, v_hbm, w_hbm,
        state_out, p_out, wall_out,
        pa, pb, weight, rhs, total, halo_l, halo_r, at, a_mat, f_hi, f_lo, p_hi, p_lo,
        ws_v, stiff_v, load_v, normal, owner, cell, x0, vres, vout,
        owner_hot, rank_hot,
        m_cells, a_cells, m_weights, a_weights, m_solid, a_solid, m_back, a_back, m_back2, a_back2,
        m_first, a_first, m_last, a_last,
        ws_x, stiff_x, f1_x, f2_x, kf, base,
        g_send, g_one, g_mid, g_two, q_send, q_one, q_mid, q_two,
        u_rows, zcols,
        load_sem, all_send, all_recv, halo_send, halo_recv, wall_send, wall_recv, tree_send, tree_recv, out_sem,
    ) = refs
    me = lax.axis_index("solver") * SP + lax.axis_index("space")
    left, right = lax.rem(me + D - 1, D), lax.rem(me + 1, D)
    keep_l = jnp.where(me > 0, 1.0, 0.0).astype(F32)
    keep_r = jnp.where(me < D - 1, 1.0, 0.0).astype(F32)

    def at_device(d):
        return (d // SP, lax.rem(d, SP))

    def remote(src, dst, send, recv, d):
        return pltpu.make_async_remote_copy(
            src_ref=src,
            dst_ref=dst,
            send_sem=send,
            recv_sem=recv,
            device_id=at_device(d),
            device_id_type=MESH,
        )

    loads = [
        pltpu.make_async_copy(src, dst, load_sem.at[i])
        for i, (src, dst) in enumerate(
            (
                (owner_hbm, owner),
                (cell_hbm, cell),
                (normal_hbm, normal),
                (x_hbm, x0),
                (p_hbm, pa.at[:, pl.ds(8, NY), :]),
                (ws_hbm, ws_v),
                (stiff_hbm, stiff_v),
                (load_hbm, load_v),
                (v_hbm, vres),
                (w_hbm, vout),
                (coef_hbm, weight),
                (rhs_hbm, rhs),
            )
        )
    ]
    for copy in loads:
        copy.start()
    barrier = pltpu.get_barrier_semaphore()

    def greet(k, _):
        pl.semaphore_signal(
            barrier, inc=1, device_id=at_device(lax.rem(me + k, D)), device_id_type=MESH
        )
        return 0

    lax.fori_loop(1, D, greet, 0)

    def each(msg, arrived, r):
        def one(k, _):
            d = lax.rem(me + k, D)
            remote(msg.at[d], arrived.at[me], all_send.at[r], all_recv.at[r], d).start()
            return 0

        lax.fori_loop(1, D, one, 0)
        arrived[me] = msg[me]

    def same(row, arrived, r):
        def one(k, _):
            d = lax.rem(me + k, D)
            remote(row, arrived.at[me], all_send.at[r], all_recv.at[r], d).start()
            return 0

        lax.fori_loop(1, D, one, 0)
        arrived[me] = row[...]

    def all_arrived(arrived, r):
        part = arrived.at[pl.ds(0, D - 1)]
        remote(part, part, all_send.at[r], all_recv.at[r], right).wait_recv()

    def all_sent(arrived, r):
        part = arrived.at[pl.ds(0, D - 1)]
        remote(part, part, all_send.at[r], all_recv.at[r], right).wait_send()

    lo, hi = lax.rem(me, LO), me // LO

    def tree_one(send, one, r):
        for k in range(1, LO):
            d = hi * LO + lax.rem(lo + k, LO)
            remote(send, one.at[lo], tree_send.at[r], tree_recv.at[r], d).start()
        one[lo] = send[...]

    def tree_two(one, mid, two, r):
        part = one.at[pl.ds(0, LO - 1)]
        remote(part, part, tree_send.at[r], tree_recv.at[r], right).wait()
        mid[...] = jnp.sum(one[...], axis=0)
        for k in range(1, HI):
            d = lax.rem(hi + k, HI) * LO + lo
            remote(mid, two.at[hi], tree_send.at[r + 1], tree_recv.at[r + 1], d).start()
        two[hi] = mid[...]

    def tree_end(two, r):
        part = two.at[pl.ds(0, HI - 1)]
        remote(part, part, tree_send.at[r + 1], tree_recv.at[r + 1], right).wait()
        return jnp.sum(two[...], axis=0)

    for copy in loads[:4]:
        copy.wait()
    block = min(IF, LANES)
    before = mask(iota((block, block), 0) < iota((block, block), 1)).astype(BF16)
    ones = jnp.ones((block, block), BF16)
    carry = jnp.zeros((D, block), F32)
    for b in range(IF // block):
        cols = pl.ds(b * block, block)
        hot = mask(owner[:, cols] == iota((D, block), 0))
        owner_hot[:, cols] = hot
        hot16 = hot.astype(BF16)
        rank = jnp.sum(hot * (carry + dot(hot16, before, (1, 0))), axis=0, keepdims=True)
        carry = carry + dot(hot16, ones, (1, 0))
        slot = lax.rem(iota((LANES, block), 0), SLOTS).astype(F32)
        rank_hot[:, cols] = mask(slot == rank)
    x = x0[...]
    nrm = normal[...]
    flux = SOURCE_GAIN * jnp.sum(nrm * x[0:3], axis=0, keepdims=True)
    group = iota((LANES, IF), 0) // SLOTS
    named = (cell[...] + 1).astype(F32)
    packed = rank_hot[...] * jnp.where(group == 0, flux, jnp.where(group == 1, named, 0.0))
    m_cells[:, 0, :] = dot(owner_hot[...], packed, (1, 1), True)

    pl.semaphore_wait(barrier, D - 1)
    each(m_cells, a_cells, CELLS)

    def halo(buf, e, ch):
        rows = pl.ds(pl.multiple_of(ch * (NY // NCH), 8), NY // NCH)
        inner = pl.ds(pl.multiple_of(ch * (NY // NCH) + 8, 8), NY // NCH)
        to_left = remote(
            buf.at[0, inner, :], halo_r.at[e, rows, :], halo_send.at[e, 0, ch], halo_recv.at[e, 0, ch], left
        )
        to_right = remote(
            buf.at[CX - 1, inner, :], halo_l.at[e, rows, :], halo_send.at[e, 1, ch], halo_recv.at[e, 1, ch], right
        )
        return to_left, to_right

    loads[4].wait()
    for ch in range(NCH):
        for copy in halo(pa, 0, ch):
            copy.start()

    for copy in loads[5:8]:
        copy.wait()
    for w in range(W1):
        for c in range(3):
            ws_x[1 + w, c] = ws_v[c, :, w, :]
        stiff_x[1 + w] = stiff_v[:, w, :]

    def planes(buf, width, count, r):
        return (
            remote(buf.at[pl.ds(width, width)], buf.at[pl.ds(width + count, width)], wall_send.at[r, 0], wall_recv.at[r, 0], left),
            remote(buf.at[pl.ds(count, width)], buf.at[pl.ds(0, width)], wall_send.at[r, 1], wall_recv.at[r, 1], right),
        )

    wall_static = planes(ws_x, 1, W1, 0) + planes(stiff_x, 1, W1, 1)
    for copy in wall_static:
        copy.start()

    pad = jnp.zeros((CX, 8, NZ), F32)
    for buf in (pa, pb):
        buf[:, pl.ds(0, 8), :] = pad
        buf[:, pl.ds(NY + 8, 8), :] = pad

    loads[8].wait()
    loads[9].wait()
    zero3 = jnp.zeros((3, IF), F32)
    n_low = jnp.concatenate([zero3, nrm], axis=0)
    n_top = jnp.concatenate([SOURCE_GAIN * nrm, zero3], axis=0)
    per_row = LANES // SLOTS

    def weights(ref, factor, first):
        def some(q, _):
            for i in range(per_row):
                u = jnp.sum(ref[q * per_row + i] * factor, axis=0, keepdims=True)
                rows = pl.ds(i * SLOTS, SLOTS)
                u_rows[rows, :] = rank_hot[pl.ds(0, SLOTS), :] * u
            m_weights[:, first + q, :] = dot(owner_hot[...], u_rows[...], (1, 1), True)
            return 0

        for q in range(H // per_row):
            some(q, 0)

    weights(vres, n_low, 0)
    weights(vout, n_top, H // per_row)

    def layers(f):
        row = iota(f.shape, 1)
        up = jnp.where(row == 0, 0.0, pltpu.roll(f, 1, 1))
        down = jnp.where(row == L3 - 1, 0.0, pltpu.roll(f, L3 - 1, 1))
        return up + down + pltpu.roll(f, 1, 2) + pltpu.roll(f, S2 - 1, 2)

    def tangent(low, f, high, stiff):
        return (6.0 + stiff)[None] * f - (low + high + layers(f))

    for copy in wall_static:
        copy.wait()

    def force(x_now, dest):
        for w in range(W1):
            part = pl.ds(w * S2, S2)
            for c in range(3):
                b = base[w, c]
                t = x_now[3 + c : 4 + c, w * S2 : (w + 1) * S2]
                row = iota((L3, S2), 0)
                dest[2 + w, c] = b + jnp.where(row == 0, t, 0.0)

    for w in range(W1):
        low = ws_x[w] * (keep_l if w == 0 else 1.0)
        high = ws_x[w + 2] * (keep_r if w == W1 - 1 else 1.0)
        k_w = tangent(low, ws_x[w + 1], high, stiff_x[w + 1])
        for c in range(3):
            base[w, c] = load_v[c, :, w, :] - k_w[c]
    force(x, f1_x)
    wall_f1 = planes(f1_x, 2, W1, 2)
    for copy in wall_f1:
        copy.start()

    each(m_weights, a_weights, WEIGHTS)

    gram = jnp.zeros((H, H), F32)
    for c in range(6):
        v_c = vres[:, c, :]
        gram = gram + dot(v_c, v_c, (1, 1), True)
    g_send[0:H, 0:H] = gram
    loads[10].wait()
    loads[11].wait()

    def invert(i, _):
        rows = pl.ds(pl.multiple_of(i * RC, 8), RC)
        for xx in range(CX):
            weight[xx, rows, :] = OMEGA / (6.0 + weight[xx, rows, :])
        return 0

    lax.fori_loop(0, NY // RC, invert, 0)

    all_arrived(a_cells, CELLS)
    got = a_cells[:, 0, :]
    found = got[:, SLOTS : 2 * SLOTS].astype(jnp.int32) - 1
    row_of = found >> (NZ.bit_length() - 1)
    zcols[:, 0:SLOTS] = jnp.bitwise_and(found, NZ - 1)
    flipped = got.T[SLOTS : 2 * SLOTS, :].astype(jnp.int32) - 1
    row_flat = flipped >> (NZ.bit_length() - 1)

    def mark(xx, _):
        for j in range(SLOTS):
            hit = iota((NY, D), 0) + xx * NY == row_flat[j : j + 1, :]
            at[pl.ds(pl.multiple_of(xx * NY, 8), NY), j * D : (j + 1) * D] = mask(hit).astype(BF16)
        return 0

    lax.fori_loop(0, CX, mark, 0)

    def scatter(flux_now):
        for j in range(SLOTS):
            f_j = flux_now[:, j : j + 1]
            top = f_j.astype(BF16).astype(F32)
            here = zcols[:, j : j + 1] == iota((D, NZ), 1)
            f_hi[j * D : (j + 1) * D, :] = jnp.where(here, top, 0.0).astype(BF16)
            f_lo[j * D : (j + 1) * D, :] = jnp.where(here, f_j - top, 0.0).astype(BF16)
        half = max(NY // 2, 8)

        def place(i, _):
            rows = pl.ds(pl.multiple_of(i * half, 8), half)
            hot = at[rows, :]
            found_here = dot(hot, f_hi[...], (1, 0)) + dot(hot, f_lo[...], (1, 0))
            total[rows, :] = rhs[rows, :] + found_here
            return 0

        lax.fori_loop(0, R // half, place, 0)

    scatter(got)

    def update(src, dst, xx, y0, up, down):
        ext = src[xx, pl.ds(y0, RC + 16), :]
        c = ext[8 : 8 + RC]
        beside = pltpu.roll(ext, 1, 0)[8 : 8 + RC] + pltpu.roll(ext, RC + 15, 0)[8 : 8 + RC]
        lane = iota((RC, NZ), 1)
        beside = beside + jnp.where(lane == 0, 0.0, pltpu.roll(c, 1, 1))
        beside = beside + jnp.where(lane == NZ - 1, 0.0, pltpu.roll(c, NZ - 1, 1))
        rows = pl.ds(pl.multiple_of(xx * NY + y0, 8), RC)
        new = (1.0 - OMEGA) * c + weight[xx, pl.ds(y0, RC), :] * (total[rows, :] + up + down + beside)
        dst[xx, pl.ds(pl.multiple_of(y0 + 8, 8), RC), :] = new

    chunk = NY // NCH

    def sweep(e, src, dst, send):
        if e >= 1:
            for ch in range(NCH):
                for copy in halo(dst, e - 1, ch):
                    copy.wait_send()

        def edge(ch, _):
            to_left, to_right = halo(src, e, ch)
            to_left.wait_recv()
            to_right.wait_recv()

            def part(i, _):
                y0 = pl.multiple_of(ch * chunk + i * RC, 8)
                up = halo_l[e, pl.ds(y0, RC), :] * keep_l
                down = src[1, pl.ds(pl.multiple_of(y0 + 8, 8), RC), :]
                update(src, dst, 0, y0, up, down)
                up = src[CX - 2, pl.ds(pl.multiple_of(y0 + 8, 8), RC), :]
                down = halo_r[e, pl.ds(y0, RC), :] * keep_r
                update(src, dst, CX - 1, y0, up, down)
                return 0

            lax.fori_loop(0, chunk // RC, part, 0)
            if send:
                for copy in halo(dst, e + 1, ch):
                    copy.start()
            return 0

        lax.fori_loop(0, NCH, edge, 0)

        def inner(i, _):
            y0 = pl.multiple_of(i * RC, 8)
            for xx in range(1, CX - 1):
                up = src[xx - 1, pl.ds(pl.multiple_of(y0 + 8, 8), RC), :]
                down = src[xx + 1, pl.ds(pl.multiple_of(y0 + 8, 8), RC), :]
                update(src, dst, xx, y0, up, down)
            return 0

        lax.fori_loop(0, NY // RC, inner, 0)

    def moments(f_x, copies, dest, first):
        for copy in copies:
            copy.wait()
        ext = []
        for i in range(W1 + 4):
            f = f_x[i]
            ext.append(f * keep_l if i < 2 else f * keep_r if i >= W1 + 2 else f)
        image = []
        for i in range(W1 + 2):
            image.append(tangent(ext[i], ext[i + 1], ext[i + 2], stiff_x[i]))
        image[0] = image[0] * keep_l
        image[-1] = image[-1] * keep_r
        sums = [jnp.zeros((L3, S2), F32) for _ in range(4)]
        for w in range(W1):
            f, k1 = ext[w + 2], image[w + 1]
            k2 = tangent(image[w], k1, image[w + 2], stiff_x[w + 1])
            kf[w] = k1
            for n, (one, two) in enumerate(((f, f), (f, k1), (k1, k1), (k1, k2))):
                sums[n] = sums[n] + jnp.sum(one * two, axis=0)
        for n in range(4):
            s = jnp.sum(sums[n], axis=0, keepdims=True)
            width = min(S2, LANES)
            s = sum(s[:, i * width : (i + 1) * width] for i in range(S2 // width))
            dest[first + n : first + n + 1, 0:width] = s

    def wall_update(f_x, rows):
        width = min(S2, LANES)
        m0, m1, m2, m3 = (jnp.sum(rows[n : n + 1, 0:width], axis=1, keepdims=True) for n in range(4))
        alpha0 = m0 / m1
        left_over = m0 - 2.0 * alpha0 * m1 + alpha0 * alpha0 * m2
        grow = 1.0 + left_over / m0
        alpha1 = left_over / (grow * grow * m1 - 2.0 * grow * alpha0 * m2 + alpha0 * alpha0 * m3)
        on_f, on_k = alpha0 + alpha1 * grow, alpha1 * alpha0
        new = []
        for w in range(W1):
            new.append(ws_x[w + 1] + on_f[None] * f_x[w + 2] - on_k[None] * kf[w])
        rows_out = [
            jnp.concatenate([new[w][c, 0:1, :] for w in range(W1)], axis=1) for c in range(3)
        ]
        return new, jnp.concatenate(rows_out, axis=0)

    def sample():
        def cut(i, _):
            for xx in range(CX):
                v = pa[xx, pl.ds(pl.multiple_of(i * RC + 8, 8), RC), :]
                top = v.astype(BF16)
                rows = pl.ds(pl.multiple_of(xx * NY + i * RC, 8), RC)
                p_hi[rows, :] = top
                p_lo[rows, :] = (v - top.astype(F32)).astype(BF16)
            return 0

        lax.fori_loop(0, NY // RC, cut, 0)
        lane = lax.rem(iota((D, LANES), 1), SLOTS)
        out = jnp.zeros((D, LANES), F32)
        for j in range(SLOTS):
            hot = a_mat[j * D : (j + 1) * D, :]
            got_rows = dot(hot, p_hi[...], (1, 0)) + dot(hot, p_lo[...], (1, 0))
            here = zcols[:, j : j + 1] == iota((D, NZ), 1)
            col = jnp.sum(jnp.where(here, got_rows, 0.0), axis=1, keepdims=True)
            out = jnp.where(lane == j, col, out)
        return out

    def unpack(arrived):
        rows = dot(arrived[:, 0, 0:SLOTS], owner_hot[...], (0, 0), True)
        return jnp.sum(rows * rank_hot[pl.ds(0, SLOTS), :], axis=0, keepdims=True)

    def against(v):
        acc = jnp.zeros((H, 6, block), F32)
        for b in range(IF // block):
            acc = acc + vres[:, :, b * block : (b + 1) * block] * v[None, :, b * block : (b + 1) * block]
        return jnp.sum(jnp.sum(acc, axis=1), axis=1, keepdims=True)

    def as_row(col):
        return jnp.sum(jnp.where(iota((H, LANES), 0) == iota((H, LANES), 1), col, 0.0), axis=0, keepdims=True)

    def as_col(row):
        return jnp.sum(jnp.where(iota((H, LANES), 0) == iota((H, LANES), 1), row, 0.0), axis=1, keepdims=True)

    sweep(0, pa, pb, True)
    moments(f1_x, wall_f1, g_send, H)
    tree_one(g_send, g_one, 0)
    sweep(1, pb, pa, True)
    for j in range(SLOTS):
        a_mat[j * D : (j + 1) * D, :] = mask(row_of[:, j : j + 1] == iota((D, R), 1)).astype(BF16)
    tree_two(g_one, g_mid, g_two, 0)
    sweep(2, pa, pb, True)
    g_all = tree_end(g_two, 0)
    gram = g_all[0:H, :]
    _, solid1 = wall_update(f1_x, g_all[H : H + 8, :])
    flux = SOURCE_GAIN * jnp.sum(nrm * solid1, axis=0, keepdims=True)
    m_solid[:, 0, :] = dot(owner_hot[...], rank_hot[...] * flux, (1, 1), True)
    each(m_solid, a_solid, SOLID)
    known = jnp.concatenate([solid1 - x[0:3], -x[3:6]], axis=0)
    h_known = against(known)
    square = iota((H, LANES), 0) == iota((H, LANES), 1)
    gram = jnp.where(iota((H, LANES), 1) < H, gram, 0.0)
    on_diag = jnp.where(square, gram, 0.0)
    trace = jnp.sum(jnp.sum(on_diag, axis=1, keepdims=True), axis=0, keepdims=True)
    ridge = RIDGE * trace / H + TINY
    beside = mask(iota((H, LANES), 1) == iota((H, LANES), 0) + H)
    inverse = eliminate(gram + jnp.where(square, ridge, 0.0) + beside, H)
    inverse = jnp.where(iota((H, LANES), 1) < H, pltpu.roll(inverse, LANES - H, 1), 0.0)
    all_arrived(a_weights, WEIGHTS)
    sweep(3, pb, pa, True)

    seen = sample()
    folded = [
        jnp.sum(a_weights[:, q, :] * seen, axis=0, keepdims=True) for q in range(H // per_row)
    ]
    folded = jnp.concatenate([jnp.broadcast_to(f, (per_row, LANES)) for f in folded], axis=0)
    mine = iota((H, LANES), 1) // SLOTS == lax.rem(iota((H, LANES), 0), per_row)
    h_col = h_known - jnp.sum(jnp.where(mine, folded, 0.0), axis=1, keepdims=True)
    m_first[...] = as_row(h_col)
    same(m_first, a_first, FIRST)
    m_back[:, 0, :] = seen
    each(m_back, a_back, BACK)
    all_arrived(a_solid, SOLID)
    all_arrived(a_first, FIRST)
    h_row = jnp.sum(a_first[...], axis=0)
    coeffs = -jnp.sum(inverse * h_row, axis=1, keepdims=True)
    extra = jnp.zeros((D, LANES), F32)
    for q in range(H // per_row):
        pick = iota((H, LANES), 0) == q * per_row + iota((H, LANES), 1) // SLOTS
        c_row = jnp.sum(jnp.where(pick, coeffs, 0.0), axis=0, keepdims=True)
        extra = extra + a_weights[:, H // per_row + q, :] * c_row
    step = LANES // 2
    while step >= SLOTS:
        extra = extra + pltpu.roll(extra, step, 1)
        step //= 2
    scatter(a_solid[:, 0, :] + extra)

    sweep(4, pa, pb, True)
    all_arrived(a_back, BACK)
    out1 = jnp.concatenate([solid1, -unpack(a_back) * nrm], axis=0)
    res1 = out1 - x
    x2 = out1
    for a in range(H):
        x2 = x2 + coeffs[a : a + 1, :] * vout[a]
    force(x2, f2_x)
    wall_f2 = planes(f2_x, 2, W1, 3)
    for copy in wall_f2:
        copy.start()
    sweep(5, pb, pa, True)
    moments(f2_x, wall_f2, q_send, 0)
    tree_one(q_send, q_one, 2)
    shifted = pltpu.roll(pltpu.roll(gram, 1, 0), 1, 1)
    inside = (iota((H, LANES), 0) > 0) & (iota((H, LANES), 1) > 0) & (iota((H, LANES), 1) < H)
    shifted = jnp.where(inside, shifted, 0.0)
    trace = jnp.sum(
        jnp.sum(jnp.where(square, shifted, 0.0), axis=1, keepdims=True), axis=0, keepdims=True
    )
    sweep(6, pa, pb, True)
    tree_two(q_one, q_mid, q_two, 2)
    sweep(7, pb, pa, False)
    save = pltpu.make_async_copy(pa.at[:, pl.ds(8, NY), :], p_out, out_sem)
    save.start()
    m_back2[:, 0, :] = sample()
    each(m_back2, a_back2, BACK2)
    new, solid2 = wall_update(f2_x, tree_end(q_two, 2))
    for w in range(W1):
        for c in range(3):
            wall_out[c, :, w, :] = new[w][c]
    all_arrived(a_back2, BACK2)
    out2 = jnp.concatenate([solid2, -unpack(a_back2) * nrm], axis=0)
    change = out2 - x2 - res1
    change_out = out2 - out1
    cross = against(change)
    own = jnp.sum(jnp.sum(change * change, axis=1, keepdims=True), axis=0, keepdims=True)
    old = jnp.sum(jnp.sum(change * res1, axis=1, keepdims=True), axis=0, keepdims=True)
    lane = iota((1, LANES), 1)
    m_last[...] = jnp.where(lane == H, own, jnp.where(lane == H + 1, old, as_row(cross)))
    same(m_last, a_last, LAST)
    all_arrived(a_last, LAST)
    last = jnp.sum(a_last[...], axis=0)
    own, old = last[:, H : H + 1], last[:, H + 1 : H + 2]
    cross = jnp.where((lane > 0) & (lane < H), pltpu.roll(last, 1, 1), jnp.where(lane == 0, own, 0.0))
    h_row = pltpu.roll(jnp.where(lane < H, h_row, 0.0), 1, 1)
    h_row = jnp.where(lane == 0, own + old, h_row + cross)
    cross_col = as_col(cross)
    left_row = iota((H, LANES), 0) == 0
    gram = jnp.where(left_row, cross, jnp.where(iota((H, LANES), 1) == 0, cross_col, shifted))
    ridge = RIDGE * (trace + own) / H + TINY
    gram = gram + jnp.where(square, ridge, 0.0)
    gram = jnp.where(iota((H, LANES), 1) == H, as_col(h_row), gram)
    coeffs = -eliminate(gram, H)[:, H : H + 1]
    state = out2 + coeffs[0:1, :] * change_out
    for a in range(H - 1):
        state = state + coeffs[a + 1 : a + 2, :] * vout[a]
    state_out[...] = state

    for arrived, r in (
        (a_cells, CELLS),
        (a_weights, WEIGHTS),
        (a_solid, SOLID),
        (a_first, FIRST),
        (a_back, BACK),
        (a_back2, BACK2),
        (a_last, LAST),
    ):
        all_sent(arrived, r)
    for ch in range(NCH):
        for copy in halo(pb, SWEEPS * COUPLE - 1, ch):
            copy.wait_send()
    save.wait()


def local(cfg, *args):
    (D, SP, LO, CX, NY, NZ, L3, W1, S2, IF, H, NCH, RC) = cfg
    (p, coef, rhs, ws, stiff, load, normals, owner, cell, x, vres, vout) = args
    R, K = CX * NY, SLOTS * D
    EX = SWEEPS * COUPLE
    wide = LANES
    G = H + 8

    def vmem(*shape, dtype=F32):
        return pltpu.VMEM(shape, dtype)

    dma = pltpu.SemaphoreType.DMA
    scratch = [
        vmem(CX, NY + 16, NZ), vmem(CX, NY + 16, NZ), vmem(CX, NY, NZ), vmem(R, NZ), vmem(R, NZ),
        vmem(EX, NY, NZ), vmem(EX, NY, NZ),
        vmem(R, K, dtype=BF16), vmem(K, R, dtype=BF16), vmem(K, NZ, dtype=BF16), vmem(K, NZ, dtype=BF16),
        vmem(R, NZ, dtype=BF16), vmem(R, NZ, dtype=BF16),
        vmem(3, L3, W1, S2), vmem(L3, W1, S2), vmem(3, L3, W1, S2),
        vmem(3, IF), vmem(1, IF, dtype=jnp.int32), vmem(1, IF, dtype=jnp.int32), vmem(6, IF),
        vmem(H, 6, IF), vmem(H, 6, IF),
        vmem(D, IF), vmem(LANES, IF),
        vmem(D, 1, wide), vmem(D, 1, wide), vmem(D, 8, wide), vmem(D, 8, wide),
        vmem(D, 1, wide), vmem(D, 1, wide), vmem(D, 1, wide), vmem(D, 1, wide), vmem(D, 1, wide), vmem(D, 1, wide),
        vmem(1, wide), vmem(D, 1, wide), vmem(1, wide), vmem(D, 1, wide),
        vmem(W1 + 2, 3, L3, S2), vmem(W1 + 2, L3, S2), vmem(W1 + 4, 3, L3, S2), vmem(W1 + 4, 3, L3, S2),
        vmem(W1, 3, L3, S2), vmem(W1, 3, L3, S2),
        vmem(G, wide), vmem(LO, G, wide), vmem(G, wide), vmem(D // LO, G, wide),
        vmem(8, wide), vmem(LO, 8, wide), vmem(8, wide), vmem(D // LO, 8, wide),
        vmem(LANES, IF), vmem(D, SLOTS, dtype=jnp.int32),
        dma((12,)), dma((ROUNDS,)), dma((ROUNDS,)), dma((EX, 2, NCH)), dma((EX, 2, NCH)),
        dma((4, 2)), dma((4, 2)), dma((4,)), dma((4,)), dma(()),
    ]
    anywhere = pl.BlockSpec(memory_space=pl.ANY)
    inside = pl.BlockSpec(memory_space=pltpu.VMEM)
    state, pressure, wall = pl.pallas_call(
        functools.partial(kernel, cfg),
        out_shape=(
            jax.ShapeDtypeStruct((6, IF), F32),
            jax.ShapeDtypeStruct((CX, NY, NZ), F32),
            jax.ShapeDtypeStruct((3, L3, W1, S2), F32),
        ),
        in_specs=[anywhere] * 12,
        out_specs=(inside, anywhere, inside),
        scratch_shapes=scratch,
        compiler_params=pltpu.CompilerParams(
            collective_id=0, has_side_effects=True, vmem_limit_bytes=60 * 2**20
        ),
    )(
        p, coef, rhs.reshape(R, NZ), ws, stiff, load, normals,
        owner.reshape(1, IF), cell.reshape(1, IF), x, vres, vout,
    )
    return state, pressure, wall


def solution(mesh):
    sp = mesh.shape["space"]
    devices = mesh.shape["solver"] * sp

    def run(*args):
        CX, NY, NZ = args[0].shape
        _, L3, W1, S2 = args[3].shape
        IF, H = args[8].shape[0], args[10].shape[0]
        lo = 8 if devices > 8 else 4
        cfg = (devices, sp, lo, CX, NY, NZ, L3, W1, S2, IF, H, 4, min(32, NY // 4))
        return local(cfg, *args)

    in_specs = (
        P(BOTH, None, None),
        P(BOTH, None, None),
        P(BOTH, None, None),
        P(None, None, BOTH, None),
        P(None, BOTH, None),
        P(None, None, BOTH, None),
        P(None, BOTH),
        P(BOTH, None),
        P(BOTH),
        P(None, BOTH),
        P(None, None, BOTH),
        P(None, None, BOTH),
    )
    out_specs = (P(None, BOTH), P(BOTH, None, None), P(None, None, BOTH, None))
    return jax.shard_map(run, mesh=mesh, in_specs=in_specs, out_specs=out_specs, check_vma=False)
```

```python
import functools

import jax
import jax.numpy as jnp
from jax import lax
from jax.experimental import pallas as pl
from jax.experimental.pallas import tpu as pltpu
from jax.sharding import PartitionSpec as P

SWEEPS = 4
COUPLE = 2
OMEGA = 0.8
SOURCE_GAIN = 4.0
RIDGE = 0.1
TINY = 1e-06
SLOTS = 16
LANES = 128
MESH = pl.DeviceIdType.MESH
F32 = jnp.float32
BF16 = jnp.bfloat16
BOTH = ("solver", "space")
CELLS, WEIGHTS, SOLID, FIRST, BACK, MOVED, BACK2, LAST = range(8)
ROUNDS = 8


def iota(shape, dim):
    return lax.broadcasted_iota(jnp.int32, shape, dim)


def dot(a, b, contract, exact=False):
    return lax.dot_general(
        a,
        b,
        (((contract[0],), (contract[1],)), ((), ())),
        precision=lax.Precision.HIGHEST if exact else None,
        preferred_element_type=F32,
    )


def mask(flag):
    return jnp.where(flag, 1.0, 0.0).astype(F32)


def eliminate(m, size):
    row = iota(m.shape, 0)
    for k in range(size):
        pivot_row = m[k : k + 1, :] / m[k : k + 1, k : k + 1]
        m = jnp.where(row == k, pivot_row, m - m[:, k : k + 1] * pivot_row)
    return m


def kernel(cfg, *refs):
    (D, SP, LO, CX, NY, NZ, L3, W1, S2, IF, H, NCH, RC) = cfg
    HI = D // LO
    R, K = CX * NY, SLOTS * D
    (
        p_hbm, coef_hbm, rhs_hbm, ws_hbm, stiff_hbm, load_hbm, normal_hbm, owner_hbm, cell_hbm, x_hbm, v_hbm, w_hbm,
        points_out, small_out, p_out, wall_out,
        pa, pb, weight, rhs, total, halo_l, halo_r, at, a_mat, f_hi, f_lo, p_hi, p_lo,
        ws_v, stiff_v, load_v, normal, owner, cell, x0, vres, vout,
        owner_hot, rank_hot,
        m_cells, a_cells, m_weights, a_weights, m_solid, a_solid, m_back, a_back, m_back2, a_back2, m_moved, a_moved,
        m_first, a_first, m_last, a_last,
        ws_x, stiff_x, f1_x, f2_x, kf, base,
        g_send, g_one, g_mid, g_two, q_send, q_one, q_mid, q_two,
        u_rows, zcols,
        load_sem, all_send, all_recv, halo_send, halo_recv, wall_send, wall_recv, tree_send, tree_recv, out_sem,
    ) = refs
    me = lax.axis_index("solver") * SP + lax.axis_index("space")
    left, right = lax.rem(me + D - 1, D), lax.rem(me + 1, D)
    keep_l = jnp.where(me > 0, 1.0, 0.0).astype(F32)
    keep_r = jnp.where(me < D - 1, 1.0, 0.0).astype(F32)

    def at_device(d):
        return (d // SP, lax.rem(d, SP))

    def remote(src, dst, send, recv, d):
        return pltpu.make_async_remote_copy(
            src_ref=src,
            dst_ref=dst,
            send_sem=send,
            recv_sem=recv,
            device_id=at_device(d),
            device_id_type=MESH,
        )

    def spot(xx):
        return CX - 2 if xx == 0 else xx - 1 if xx < CX - 1 else xx

    loads = [
        pltpu.make_async_copy(src, dst, load_sem.at[i])
        for i, (src, dst) in enumerate(
            (
                (owner_hbm, owner),
                (cell_hbm, cell),
                (normal_hbm, normal),
                (x_hbm, x0),
                (p_hbm, pa.at[:, pl.ds(8, NY), :]),
                (ws_hbm, ws_v),
                (stiff_hbm, stiff_v),
                (load_hbm, load_v),
                (v_hbm, vres),
                (w_hbm, vout),
                (coef_hbm, weight),
            )
            + tuple(
                (rhs_hbm.at[pl.ds(xx * NY, NY), :], rhs.at[pl.ds(spot(xx) * NY, NY), :])
                for xx in range(CX)
            )
        )
    ]
    for copy in loads:
        copy.start()
    barrier = pltpu.get_barrier_semaphore()

    NS = D // SP
    my_s, my_p = me // SP, lax.rem(me, SP)

    def peers(act):
        for ds in sorted(range(NS), key=lambda q: -min(q, NS - q)):
            there = lax.rem(my_s + ds, NS)

            def one(k, _):
                act(there, lax.rem(my_p + SP // 2 + k, SP))
                return 0

            if ds:
                lax.fori_loop(0, SP, one, 0, unroll=4)
            else:
                lax.fori_loop(0, SP // 2, one, 0, unroll=4 if SP >= 8 else 1)
                lax.fori_loop(SP // 2 + 1, SP, one, 0, unroll=3 if SP >= 8 else 1)

    def start_remote(src, dst, r, there, low):
        pltpu.make_async_remote_copy(
            src_ref=src,
            dst_ref=dst,
            send_sem=all_send.at[r],
            recv_sem=all_recv.at[r],
            device_id=(there, low),
            device_id_type=MESH,
        ).start()

    def greet(there, low):
        pl.semaphore_signal(barrier, inc=1, device_id=(there, low), device_id_type=MESH)

    peers(greet)

    def each(msg, arrived, r):
        peers(lambda there, low: start_remote(msg.at[there * SP + low], arrived.at[me], r, there, low))
        arrived[me] = msg[me]

    def same(row, arrived, r):
        peers(lambda there, low: start_remote(row, arrived.at[me], r, there, low))
        arrived[me] = row[...]

    def all_arrived(arrived, r):
        part = arrived.at[pl.ds(0, D - 1)]
        remote(part, part, all_send.at[r], all_recv.at[r], right).wait_recv()

    def all_sent(arrived, r):
        part = arrived.at[pl.ds(0, D - 1)]
        remote(part, part, all_send.at[r], all_recv.at[r], right).wait_send()

    lo, hi = lax.rem(me, LO), me // LO

    def tree_one(send, one, r):
        for k in range(1, LO):
            d = hi * LO + lax.rem(lo + k, LO)
            remote(send, one.at[lo], tree_send.at[r], tree_recv.at[r], d).start()
        one[lo] = send[...]

    def tree_two(one, mid, two, r):
        part = one.at[pl.ds(0, LO - 1)]
        remote(part, part, tree_send.at[r], tree_recv.at[r], right).wait()
        mid[...] = jnp.sum(one[...], axis=0)
        for k in range(1, HI):
            d = lax.rem(hi + k, HI) * LO + lo
            remote(mid, two.at[hi], tree_send.at[r + 1], tree_recv.at[r + 1], d).start()
        two[hi] = mid[...]

    def tree_end(two, r):
        part = two.at[pl.ds(0, HI - 1)]
        remote(part, part, tree_send.at[r + 1], tree_recv.at[r + 1], right).wait()
        return jnp.sum(two[...], axis=0)

    for copy in loads[:4]:
        copy.wait()
    block = min(IF, LANES)
    before = mask(iota((block, block), 0) < iota((block, block), 1)).astype(BF16)
    ones = jnp.ones((block, block), BF16)
    carry = jnp.zeros((D, block), F32)
    for b in range(IF // block):
        cols = pl.ds(b * block, block)
        hot = mask(owner[:, cols] == iota((D, block), 0))
        owner_hot[:, cols] = hot
        hot16 = hot.astype(BF16)
        rank = jnp.sum(hot * (carry + dot(hot16, before, (1, 0))), axis=0, keepdims=True)
        carry = carry + dot(hot16, ones, (1, 0))
        slot = lax.rem(iota((LANES, block), 0), SLOTS).astype(F32)
        rank_hot[:, cols] = mask(slot == rank)
    x = x0[...]
    nrm = normal[...]
    flux = SOURCE_GAIN * jnp.sum(nrm * x[0:3], axis=0, keepdims=True)
    group = iota((LANES, IF), 0) // SLOTS
    named = (cell[...] + 1).astype(F32)
    squared = jnp.sum(nrm * nrm, axis=0, keepdims=True)
    along = jnp.sum(nrm * x[3:6], axis=0, keepdims=True)
    packed = jnp.where(group == 2, squared, jnp.where(group == 3, along, 0.0))
    packed = jnp.where(group == 0, flux, jnp.where(group == 1, named, packed))
    packed = rank_hot[...] * packed
    m_cells[:, 0, :] = dot(owner_hot[...], packed, (1, 1), True)

    pl.semaphore_wait(barrier, D - 1)
    each(m_cells, a_cells, CELLS)

    def halo(buf, e, ch):
        rows = pl.ds(pl.multiple_of(ch * (NY // NCH), 8), NY // NCH)
        inner = pl.ds(pl.multiple_of(ch * (NY // NCH) + 8, 8), NY // NCH)
        to_left = remote(
            buf.at[0, inner, :], halo_r.at[e, rows, :], halo_send.at[e, 0, ch], halo_recv.at[e, 0, ch], left
        )
        to_right = remote(
            buf.at[CX - 1, inner, :], halo_l.at[e, rows, :], halo_send.at[e, 1, ch], halo_recv.at[e, 1, ch], right
        )
        return to_left, to_right

    loads[4].wait()
    for ch in range(NCH):
        for copy in halo(pa, 0, ch):
            copy.start()

    for copy in loads[5:8]:
        copy.wait()
    for w in range(W1):
        for c in range(3):
            ws_x[1 + w, c] = ws_v[c, :, w, :]
        stiff_x[1 + w] = stiff_v[:, w, :]

    def planes(buf, width, count, r):
        return (
            remote(buf.at[pl.ds(width, width)], buf.at[pl.ds(width + count, width)], wall_send.at[r, 0], wall_recv.at[r, 0], left),
            remote(buf.at[pl.ds(count, width)], buf.at[pl.ds(0, width)], wall_send.at[r, 1], wall_recv.at[r, 1], right),
        )

    wall_static = planes(ws_x, 1, W1, 0) + planes(stiff_x, 1, W1, 1)
    for copy in wall_static:
        copy.start()

    pad = jnp.zeros((CX, 8, NZ), F32)
    for buf in (pa, pb):
        buf[:, pl.ds(0, 8), :] = pad
        buf[:, pl.ds(NY + 8, 8), :] = pad

    loads[8].wait()
    loads[9].wait()
    per_row = LANES // SLOTS

    def weights(ref, at_row, factor, first):
        u = sum(ref[at_row + c] * (factor * nrm[c : c + 1]) for c in range(3))
        for q in range(H // per_row):
            for i in range(per_row):
                a = q * per_row + i
                u_rows[i * SLOTS : (i + 1) * SLOTS, :] = rank_hot[0:SLOTS, :] * u[a : a + 1, :]
            m_weights[:, first + q, :] = dot(owner_hot[...], u_rows[...], (1, 1), True)

    weights(vres, 3, 1.0, 0)
    weights(vout, 0, SOURCE_GAIN, H // per_row)

    def layers(f):
        row = iota(f.shape, 1)
        up = jnp.where(row == 0, 0.0, pltpu.roll(f, 1, 1))
        down = jnp.where(row == L3 - 1, 0.0, pltpu.roll(f, L3 - 1, 1))
        return up + down + pltpu.roll(f, 1, 2) + pltpu.roll(f, S2 - 1, 2)

    def tangent(low, f, high, stiff):
        return (6.0 + stiff)[None] * f - (low + high + layers(f))

    for copy in wall_static:
        copy.wait()

    def force(x_now, dest):
        for w in range(W1):
            part = pl.ds(w * S2, S2)
            for c in range(3):
                b = base[w, c]
                t = x_now[3 + c : 4 + c, w * S2 : (w + 1) * S2]
                row = iota((L3, S2), 0)
                dest[2 + w, c] = b + jnp.where(row == 0, t, 0.0)

    for w in range(W1):
        low = ws_x[w] * (keep_l if w == 0 else 1.0)
        high = ws_x[w + 2] * (keep_r if w == W1 - 1 else 1.0)
        k_w = tangent(low, ws_x[w + 1], high, stiff_x[w + 1])
        for c in range(3):
            base[w, c] = load_v[c, :, w, :] - k_w[c]
    force(x, f1_x)
    wall_f1 = planes(f1_x, 2, W1, 2)
    for copy in wall_f1:
        copy.start()

    gram = jnp.zeros((H, H), F32)
    for c in range(6):
        v_c = vres[c]
        gram = gram + dot(v_c, v_c, (1, 1), True)
    g_send[0:H, 0:H] = gram
    for copy in loads[10:]:
        copy.wait()

    def invert(i, _):
        rows = pl.ds(pl.multiple_of(i * RC, 8), RC)
        for xx in range(CX):
            weight[xx, rows, :] = OMEGA / (6.0 + weight[xx, rows, :])
        return 0

    lax.fori_loop(0, NY // RC, invert, 0)

    all_arrived(a_cells, CELLS)
    y_bits, z_bits = NY.bit_length() - 1, NZ.bit_length() - 1

    def placed(cells):
        xx = cells >> (y_bits + z_bits)
        xx = jnp.where(xx == 0, CX - 2, jnp.where((xx > 0) & (xx < CX - 1), xx - 1, xx))
        return xx * NY + jnp.bitwise_and(cells >> z_bits, NY - 1)

    got = a_cells[:, 0, :]
    found = got[:, SLOTS : 2 * SLOTS].astype(jnp.int32) - 1
    row_of = placed(found)
    zcols[:, 0:SLOTS] = jnp.bitwise_and(found, NZ - 1)
    flipped = got.T[SLOTS : 2 * SLOTS, :].astype(jnp.int32) - 1
    row_flat = placed(flipped)

    def mark(xx, _):
        for j in range(SLOTS):
            hit = iota((NY, D), 0) + xx * NY == row_flat[j : j + 1, :]
            at[pl.ds(pl.multiple_of(xx * NY, 8), NY), j * D : (j + 1) * D] = mask(hit).astype(BF16)
        return 0

    lax.fori_loop(0, CX, mark, 0)

    def spread(flux_now):
        for j in range(SLOTS):
            f_j = flux_now[:, j : j + 1]
            top = f_j.astype(BF16).astype(F32)
            here = zcols[:, j : j + 1] == iota((D, NZ), 1)
            f_hi[j * D : (j + 1) * D, :] = jnp.where(here, top, 0.0).astype(BF16)
            f_lo[j * D : (j + 1) * D, :] = jnp.where(here, f_j - top, 0.0).astype(BF16)

    inner_rows, edge_rows = (0, (CX - 2) * NY), ((CX - 2) * NY, 2 * NY)

    def place(which):
        rows = pl.ds(*which)
        hot = at[rows, :]
        found_here = dot(hot, f_hi[...], (1, 0)) + dot(hot, f_lo[...], (1, 0))
        total[rows, :] = rhs[rows, :] + found_here

    spread(got)
    place(edge_rows)

    def update(src, dst, xx, y0, up, down):
        ext = src[xx, pl.ds(y0, RC + 16), :]
        c = ext[8 : 8 + RC]
        beside = pltpu.roll(ext, 1, 0)[8 : 8 + RC] + pltpu.roll(ext, RC + 15, 0)[8 : 8 + RC]
        lane = iota((RC, NZ), 1)
        beside = beside + jnp.where(lane == 0, 0.0, pltpu.roll(c, 1, 1))
        beside = beside + jnp.where(lane == NZ - 1, 0.0, pltpu.roll(c, NZ - 1, 1))
        rows = pl.ds(pl.multiple_of(spot(xx) * NY + y0, 8), RC)
        new = (1.0 - OMEGA) * c + weight[xx, pl.ds(y0, RC), :] * (total[rows, :] + up + down + beside)
        dst[xx, pl.ds(pl.multiple_of(y0 + 8, 8), RC), :] = new

    chunk = NY // NCH

    def edges(e, src, dst, send):
        if e >= 1:
            for ch in range(NCH):
                for copy in halo(dst, e - 1, ch):
                    copy.wait_send()

        def edge(ch, _):
            to_left, to_right = halo(src, e, ch)
            to_left.wait_recv()
            to_right.wait_recv()

            def part(i, _):
                y0 = pl.multiple_of(ch * chunk + i * RC, 8)
                up = halo_l[e, pl.ds(y0, RC), :] * keep_l
                down = src[1, pl.ds(pl.multiple_of(y0 + 8, 8), RC), :]
                update(src, dst, 0, y0, up, down)
                up = src[CX - 2, pl.ds(pl.multiple_of(y0 + 8, 8), RC), :]
                down = halo_r[e, pl.ds(y0, RC), :] * keep_r
                update(src, dst, CX - 1, y0, up, down)
                return 0

            lax.fori_loop(0, chunk // RC, part, 0)
            if send:
                for copy in halo(dst, e + 1, ch):
                    copy.start()
            return 0

        lax.fori_loop(0, NCH, edge, 0)

    def inside(src, dst):
        def inner(i, _):
            y0 = pl.multiple_of(i * RC, 8)
            for xx in range(1, CX - 1):
                up = src[xx - 1, pl.ds(pl.multiple_of(y0 + 8, 8), RC), :]
                down = src[xx + 1, pl.ds(pl.multiple_of(y0 + 8, 8), RC), :]
                update(src, dst, xx, y0, up, down)
            return 0

        lax.fori_loop(0, NY // RC, inner, 0)

    def moments(f_x, copies, dest, first):
        for copy in copies:
            copy.wait()
        ext = []
        for i in range(W1 + 4):
            f = f_x[i]
            ext.append(f * keep_l if i < 2 else f * keep_r if i >= W1 + 2 else f)
        image = []
        for i in range(W1 + 2):
            image.append(tangent(ext[i], ext[i + 1], ext[i + 2], stiff_x[i]))
        image[0] = image[0] * keep_l
        image[-1] = image[-1] * keep_r
        sums = [jnp.zeros((L3, S2), F32) for _ in range(4)]
        for w in range(W1):
            f, k1 = ext[w + 2], image[w + 1]
            k2 = tangent(image[w], k1, image[w + 2], stiff_x[w + 1])
            kf[w] = k1
            for n, (one, two) in enumerate(((f, f), (f, k1), (k1, k1), (k1, k2))):
                sums[n] = sums[n] + jnp.sum(one * two, axis=0)
        for n in range(4):
            s = jnp.sum(sums[n], axis=0, keepdims=True)
            width = min(S2, LANES)
            s = sum(s[:, i * width : (i + 1) * width] for i in range(S2 // width))
            dest[first + n : first + n + 1, 0:width] = s

    def wall_update(f_x, rows):
        width = min(S2, LANES)
        m0, m1, m2, m3 = (jnp.sum(rows[n : n + 1, 0:width], axis=1, keepdims=True) for n in range(4))
        alpha0 = m0 / m1
        left_over = m0 - 2.0 * alpha0 * m1 + alpha0 * alpha0 * m2
        grow = 1.0 + left_over / m0
        alpha1 = left_over / (grow * grow * m1 - 2.0 * grow * alpha0 * m2 + alpha0 * alpha0 * m3)
        on_f, on_k = alpha0 + alpha1 * grow, alpha1 * alpha0
        new = []
        for w in range(W1):
            new.append(ws_x[w + 1] + on_f[None] * f_x[w + 2] - on_k[None] * kf[w])
        rows_out = [
            jnp.concatenate([new[w][c, 0:1, :] for w in range(W1)], axis=1) for c in range(3)
        ]
        return new, jnp.concatenate(rows_out, axis=0)

    def sample(which, planes_of):
        def cut(i, _):
            for xx in planes_of:
                v = pa[xx, pl.ds(pl.multiple_of(i * RC + 8, 8), RC), :]
                top = v.astype(BF16)
                rows = pl.ds(pl.multiple_of(spot(xx) * NY + i * RC, 8), RC)
                p_hi[rows, :] = top
                p_lo[rows, :] = (v - top.astype(F32)).astype(BF16)
            return 0

        lax.fori_loop(0, NY // RC, cut, 0)
        lane = lax.rem(iota((D, LANES), 1), SLOTS)
        out = jnp.zeros((D, LANES), F32)
        first, count = which
        rows = pl.ds(first, count)
        for j in range(0, SLOTS, 2):
            hot = a_mat[j * D : (j + 2) * D, first : first + count]
            got_rows = dot(hot, p_hi[rows, :], (1, 0)) + dot(hot, p_lo[rows, :], (1, 0))
            for i in range(2):
                here = zcols[:, j + i : j + i + 1] == iota((D, NZ), 1)
                part = got_rows[i * D : (i + 1) * D]
                col = jnp.sum(jnp.where(here, part, 0.0), axis=1, keepdims=True)
                out = jnp.where(lane == j + i, col, out)
        return out

    mid = tuple(range(1, CX - 1))
    ends = (0, CX - 1)

    def unpack(arrived):
        rows = dot(arrived[:, 0, 0:SLOTS], owner_hot[...], (0, 0), True)
        return jnp.sum(rows * rank_hot[pl.ds(0, SLOTS), :], axis=0, keepdims=True)

    def against(v):
        acc = sum(vres[c] * v[c : c + 1] for c in range(6))
        return jnp.sum(acc, axis=1, keepdims=True)

    def combine(coef, first):
        rows = [jnp.sum(coef * vout[c], axis=0, keepdims=True) for c in range(6)]
        return first + jnp.concatenate(rows, axis=0)

    def as_row(col):
        return jnp.sum(jnp.where(iota((H, LANES), 0) == iota((H, LANES), 1), col, 0.0), axis=0, keepdims=True)

    edges(0, pa, pb, True)
    place(inner_rows)
    inside(pa, pb)
    moments(f1_x, wall_f1, g_send, H)
    tree_one(g_send, g_one, 0)
    edges(1, pb, pa, True)
    inside(pb, pa)
    each(m_weights, a_weights, WEIGHTS)
    tree_two(g_one, g_mid, g_two, 0)
    edges(2, pa, pb, True)
    inside(pa, pb)
    for j in range(SLOTS):
        a_mat[j * D : (j + 1) * D, :] = mask(row_of[:, j : j + 1] == iota((D, R), 1)).astype(BF16)
    g_all = tree_end(g_two, 0)
    gram = g_all[0:H, :]
    _, solid1 = wall_update(f1_x, g_all[H : H + 8, :])
    flux = SOURCE_GAIN * jnp.sum(nrm * solid1, axis=0, keepdims=True)
    m_solid[:, 0, :] = dot(owner_hot[...], rank_hot[...] * flux, (1, 1), True)
    known = jnp.concatenate([solid1 - x[0:3], -x[3:6]], axis=0)
    h_known = against(known)
    inside(pb, pa)
    seen1 = sample(inner_rows, mid)
    edges(3, pb, pa, True)
    each(m_solid, a_solid, SOLID)
    all_arrived(a_weights, WEIGHTS)

    seen1 = seen1 + sample(edge_rows, ends)
    mine = iota((H, LANES), 1) // SLOTS == lax.rem(iota((H, LANES), 0), per_row)

    def owned(values):
        rows = [
            jnp.sum(a_weights[:, q, :] * values, axis=0, keepdims=True) for q in range(H // per_row)
        ]
        rows = jnp.concatenate([jnp.broadcast_to(f, (per_row, LANES)) for f in rows], axis=0)
        return jnp.sum(jnp.where(mine, rows, 0.0), axis=1, keepdims=True)

    m_first[...] = as_row(h_known - owned(seen1))
    same(m_first, a_first, FIRST)
    m_back[:, 0, :] = seen1
    each(m_back, a_back, BACK)
    square = iota((H, LANES), 0) == iota((H, LANES), 1)
    gram = jnp.where(iota((H, LANES), 1) < H, gram, 0.0)
    on_diag = jnp.where(square, gram, 0.0)
    trace = jnp.sum(jnp.sum(on_diag, axis=1, keepdims=True), axis=0, keepdims=True)
    ridge = RIDGE * trace / H + TINY
    beside = mask(iota((H, LANES), 1) == iota((H, LANES), 0) + H)
    inverse = eliminate(gram + jnp.where(square, ridge, 0.0) + beside, H)
    inverse = jnp.where(iota((H, LANES), 1) < H, pltpu.roll(inverse, LANES - H, 1), 0.0)
    all_arrived(a_solid, SOLID)
    all_arrived(a_first, FIRST)
    h_row = jnp.sum(a_first[...], axis=0)
    coeffs = -jnp.sum(inverse * h_row, axis=1, keepdims=True)
    extra = jnp.zeros((D, LANES), F32)
    for q in range(H // per_row):
        pick = iota((H, LANES), 0) == q * per_row + iota((H, LANES), 1) // SLOTS
        c_row = jnp.sum(jnp.where(pick, coeffs, 0.0), axis=0, keepdims=True)
        extra = extra + a_weights[:, H // per_row + q, :] * c_row
    step = LANES // 2
    while step >= SLOTS:
        extra = extra + pltpu.roll(extra, step, 1)
        step //= 2
    spread(a_solid[:, 0, :] + extra)
    place(edge_rows)

    edges(4, pa, pb, True)
    all_arrived(a_back, BACK)
    out1 = jnp.concatenate([solid1, -unpack(a_back) * nrm], axis=0)
    res1 = out1 - x
    x2 = combine(coeffs, out1)
    force(x2, f2_x)
    wall_f2 = planes(f2_x, 2, W1, 3)
    for copy in wall_f2:
        copy.start()
    place(inner_rows)
    inside(pa, pb)
    edges(5, pb, pa, True)
    inside(pb, pa)
    moments(f2_x, wall_f2, q_send, 0)
    tree_one(q_send, q_one, 2)
    moved = x2[3:6] - x[3:6]
    step_along = jnp.sum(nrm * moved, axis=0, keepdims=True)
    m_moved[:, 0, :] = dot(owner_hot[...], rank_hot[...] * step_along, (1, 1), True)
    edges(6, pa, pb, True)
    tree_two(q_one, q_mid, q_two, 2)
    inside(pa, pb)
    each(m_moved, a_moved, MOVED)
    shifted = pltpu.roll(pltpu.roll(gram, 1, 0), 1, 1)
    low = (iota((H, LANES), 0) > 0) & (iota((H, LANES), 1) > 0) & (iota((H, LANES), 1) < H)
    small_out[0:H, :] = jnp.where(low, shifted, 0.0)
    inside(pb, pa)
    seen2 = sample(inner_rows, mid)
    new, solid2 = wall_update(f2_x, tree_end(q_two, 2))
    for w in range(W1):
        for c in range(3):
            wall_out[c, :, w, :] = new[w][c]
    known = jnp.concatenate([solid2 - x2[0:3] - res1[0:3], -moved], axis=0)
    cross_known = against(known)
    own_known = jnp.sum(jnp.sum(known * known, axis=1, keepdims=True), axis=0, keepdims=True)
    old_known = jnp.sum(jnp.sum(known * res1, axis=1, keepdims=True), axis=0, keepdims=True)
    edges(7, pb, pa, False)
    save = pltpu.make_async_copy(pa.at[:, pl.ds(8, NY), :], p_out, out_sem)
    save.start()
    all_arrived(a_moved, MOVED)
    seen2 = seen2 + sample(edge_rows, ends)
    gained = seen2 - seen1
    cells_msg = a_cells[:, 0, :]
    n_n = pltpu.roll(cells_msg, LANES - 2 * SLOTS, 1)
    n_t = pltpu.roll(cells_msg, LANES - 3 * SLOTS, 1)
    single = iota((D, LANES), 1) < SLOTS
    own = jnp.where(single, gained * (gained * n_n + 2.0 * a_moved[:, 0, :]), 0.0)
    old = jnp.where(single, gained * (seen1 * n_n + n_t), 0.0)
    own = own_known + jnp.sum(jnp.sum(own, axis=0, keepdims=True), axis=1, keepdims=True)
    old = old_known + jnp.sum(jnp.sum(old, axis=0, keepdims=True), axis=1, keepdims=True)
    lane = iota((1, LANES), 1)
    cross = as_row(cross_known - owned(gained))
    m_last[...] = jnp.where(lane == H, own, jnp.where(lane == H + 1, old, cross))
    same(m_last, a_last, LAST)
    m_back2[:, 0, :] = seen2
    each(m_back2, a_back2, BACK2)
    small_out[H + 1 : H + 2, :] = h_row
    small_out[H + 2 : H + 3, :] = jnp.broadcast_to(
        trace - gram[H - 1 : H, H - 1 : H], (1, LANES)
    )
    all_arrived(a_last, LAST)
    small_out[H : H + 1, :] = jnp.sum(a_last[...], axis=0)
    all_arrived(a_back2, BACK2)
    out2 = jnp.concatenate([solid2, -unpack(a_back2) * nrm], axis=0)
    points_out[0] = out2
    points_out[1] = out2 - out1

    for arrived, r in (
        (a_cells, CELLS),
        (a_weights, WEIGHTS),
        (a_solid, SOLID),
        (a_first, FIRST),
        (a_back, BACK),
        (a_moved, MOVED),
        (a_back2, BACK2),
        (a_last, LAST),
    ):
        all_sent(arrived, r)
    for ch in range(NCH):
        for copy in halo(pb, SWEEPS * COUPLE - 1, ch):
            copy.wait_send()
    save.wait()


def finish(H, p_in, wall_in, points, small, w_hbm, state_out, p_out, wall_out, vout, sem):
    parts = p_in.shape[0]
    fetch = pltpu.make_async_copy(w_hbm, vout, sem.at[0])
    fetch.start()
    moves = [pltpu.make_async_copy(wall_in, wall_out, sem.at[1])]
    for i in range(parts):
        moves.append(pltpu.make_async_copy(p_in.at[i], p_out.at[i], sem.at[2 + i]))
    for copy in moves:
        copy.start()
    lane, row = iota((1, LANES), 1), iota((H, LANES), 0)
    lanes = iota((H, LANES), 1)
    square = row == lanes

    def as_col(values):
        return jnp.sum(jnp.where(square, values, 0.0), axis=1, keepdims=True)

    last, h_row = small[H : H + 1, :], small[H + 1 : H + 2, :]
    own, old = last[:, H : H + 1], last[:, H + 1 : H + 2]
    cross = jnp.where((lane > 0) & (lane < H), pltpu.roll(last, 1, 1), jnp.where(lane == 0, own, 0.0))
    h_row = pltpu.roll(jnp.where(lane < H, h_row, 0.0), 1, 1)
    h_row = jnp.where(lane == 0, own + old, h_row + cross)
    gram = jnp.where(row == 0, cross, jnp.where(lanes == 0, as_col(cross), small[0:H, :]))
    ridge = RIDGE * (small[H + 2 : H + 3, 0:1] + own) / H + TINY
    gram = gram + jnp.where(square, ridge, 0.0)
    gram = jnp.where(lanes == H, as_col(h_row), gram)
    coeffs = -eliminate(gram, H)[:, H : H + 1]
    rest = jnp.where(iota((H, 1), 0) < H - 1, pltpu.roll(coeffs * jnp.ones((H, LANES), F32), H - 1, 0)[:, 0:1], 0.0)
    fetch.wait()
    rows = [jnp.sum(rest * vout[c], axis=0, keepdims=True) for c in range(6)]
    state_out[...] = points[0] + coeffs[0:1, :] * points[1] + jnp.concatenate(rows, axis=0)
    for copy in moves:
        copy.wait()


def local(cfg, *args):
    (D, SP, LO, CX, NY, NZ, L3, W1, S2, IF, H, NCH, RC) = cfg
    (p, coef, rhs, ws, stiff, load, normals, owner, cell, x, vres, vout) = args
    vres, vout = vres.transpose(1, 0, 2), vout.transpose(1, 0, 2)
    R, K = CX * NY, SLOTS * D
    EX = SWEEPS * COUPLE
    wide = LANES
    G = H + 8

    def vmem(*shape, dtype=F32):
        return pltpu.VMEM(shape, dtype)

    dma = pltpu.SemaphoreType.DMA
    scratch = [
        vmem(CX, NY + 16, NZ), vmem(CX, NY + 16, NZ), vmem(CX, NY, NZ), vmem(R, NZ), vmem(R, NZ),
        vmem(EX, NY, NZ), vmem(EX, NY, NZ),
        vmem(R, K, dtype=BF16), vmem(K, R, dtype=BF16), vmem(K, NZ, dtype=BF16), vmem(K, NZ, dtype=BF16),
        vmem(R, NZ, dtype=BF16), vmem(R, NZ, dtype=BF16),
        vmem(3, L3, W1, S2), vmem(L3, W1, S2), vmem(3, L3, W1, S2),
        vmem(3, IF), vmem(1, IF, dtype=jnp.int32), vmem(1, IF, dtype=jnp.int32), vmem(6, IF),
        vmem(6, H, IF), vmem(6, H, IF),
        vmem(D, IF), vmem(LANES, IF),
        vmem(D, 1, wide), vmem(D, 1, wide), vmem(D, 8, wide), vmem(D, 8, wide),
        vmem(D, 1, wide), vmem(D, 1, wide), vmem(D, 1, wide), vmem(D, 1, wide), vmem(D, 1, wide), vmem(D, 1, wide),
        vmem(D, 1, wide), vmem(D, 1, wide),
        vmem(1, wide), vmem(D, 1, wide), vmem(1, wide), vmem(D, 1, wide),
        vmem(W1 + 2, 3, L3, S2), vmem(W1 + 2, L3, S2), vmem(W1 + 4, 3, L3, S2), vmem(W1 + 4, 3, L3, S2),
        vmem(W1, 3, L3, S2), vmem(W1, 3, L3, S2),
        vmem(G, wide), vmem(LO, G, wide), vmem(G, wide), vmem(D // LO, G, wide),
        vmem(8, wide), vmem(LO, 8, wide), vmem(8, wide), vmem(D // LO, 8, wide),
        vmem(LANES, IF), vmem(D, SLOTS, dtype=jnp.int32),
        dma((11 + CX,)), dma((ROUNDS,)), dma((ROUNDS,)), dma((EX, 2, NCH)), dma((EX, 2, NCH)),
        dma((4, 2)), dma((4, 2)), dma((4,)), dma((4,)), dma(()),
    ]
    anywhere = pl.BlockSpec(memory_space=pl.ANY)
    inside = pl.BlockSpec(memory_space=pltpu.VMEM)
    points, small, pressure, wall = pl.pallas_call(
        functools.partial(kernel, cfg),
        out_shape=(
            jax.ShapeDtypeStruct((2, 6, IF), F32),
            jax.ShapeDtypeStruct((H + 8, LANES), F32),
            jax.ShapeDtypeStruct((CX, NY, NZ), F32),
            jax.ShapeDtypeStruct((3, L3, W1, S2), F32),
        ),
        in_specs=[anywhere] * 12,
        out_specs=(inside, inside, anywhere, inside),
        scratch_shapes=scratch,
        compiler_params=pltpu.CompilerParams(
            collective_id=0, has_side_effects=True, vmem_limit_bytes=60 * 2**20
        ),
    )(
        p, coef, rhs.reshape(R, NZ), ws, stiff, load, normals,
        owner.reshape(1, IF), cell.reshape(1, IF), x, vres, vout,
    )
    return pl.pallas_call(
        functools.partial(finish, H),
        out_shape=(
            jax.ShapeDtypeStruct((6, IF), F32),
            jax.ShapeDtypeStruct((CX, NY, NZ), F32),
            jax.ShapeDtypeStruct((3, L3, W1, S2), F32),
        ),
        in_specs=[anywhere, anywhere, inside, inside, anywhere],
        out_specs=(inside, anywhere, anywhere),
        scratch_shapes=[vmem(6, H, IF), dma((2 + CX,))],
    )(pressure, wall, points, small, vout)


def solution(mesh):
    sp = mesh.shape["space"]
    devices = mesh.shape["solver"] * sp

    def run(*args):
        CX, NY, NZ = args[0].shape
        _, L3, W1, S2 = args[3].shape
        IF, H = args[8].shape[0], args[10].shape[0]
        lo = 8 if devices > 8 else 4
        cfg = (devices, sp, lo, CX, NY, NZ, L3, W1, S2, IF, H, 4, min(32, NY // 4))
        return local(cfg, *args)

    in_specs = (
        P(BOTH, None, None),
        P(BOTH, None, None),
        P(BOTH, None, None),
        P(None, None, BOTH, None),
        P(None, BOTH, None),
        P(None, None, BOTH, None),
        P(None, BOTH),
        P(BOTH, None),
        P(BOTH),
        P(None, BOTH),
        P(None, None, BOTH),
        P(None, None, BOTH),
    )
    out_specs = (P(None, BOTH), P(BOTH, None, None), P(None, None, BOTH, None))
    return jax.shard_map(run, mesh=mesh, in_specs=in_specs, out_specs=out_specs, check_vma=False)
```

```python
import functools

import jax
import jax.numpy as jnp
from jax import lax
from jax.experimental import pallas as pl
from jax.experimental.pallas import tpu as pltpu
from jax.sharding import PartitionSpec as P

SWEEPS = 4
COUPLE = 2
OMEGA = 0.8
SOURCE_GAIN = 4.0
RIDGE = 0.1
TINY = 1e-06
SLOTS = 16
LANES = 128
MESH = pl.DeviceIdType.MESH
F32 = jnp.float32
BF16 = jnp.bfloat16
BOTH = ("solver", "space")
CELLS, WEIGHTS, SOLID, FIRST, BACK, MOVED, BACK2, LAST = range(8)
ROUNDS = 8


def iota(shape, dim):
    return lax.broadcasted_iota(jnp.int32, shape, dim)


def dot(a, b, contract, exact=False):
    return lax.dot_general(
        a,
        b,
        (((contract[0],), (contract[1],)), ((), ())),
        precision=lax.Precision.HIGHEST if exact else None,
        preferred_element_type=F32,
    )


def mask(flag):
    return jnp.where(flag, 1.0, 0.0).astype(F32)


def eliminate(m, size, first=0):
    row = iota(m.shape, 0)
    for k in range(first, size):
        pivot_row = m[k : k + 1, :] / m[k : k + 1, k : k + 1]
        m = jnp.where(row == k, pivot_row, m - m[:, k : k + 1] * pivot_row)
    return m


def kernel(cfg, *refs):
    (D, SP, LO, CX, NY, NZ, L3, W1, S2, IF, H, NCH, RC) = cfg
    HI = D // LO
    R, K = CX * NY, SLOTS * D
    (
        p_hbm, coef_hbm, rhs_hbm, ws_hbm, stiff_hbm, load_hbm, normal_hbm, owner_hbm, cell_hbm, x_hbm, v_hbm, w_hbm,
        points_out, small_out, p_out, wall_out,
        pa, pb, weight, rhs, total, halo_l, halo_r, at, a_mat, f_hi, f_lo, p_hi, p_lo,
        ws_v, stiff_v, load_v, normal, owner, cell, x0, vres, vout,
        owner_hot, rank_hot,
        m_cells, a_cells, m_weights, a_weights, m_solid, a_solid, m_back, a_back, m_back2, a_back2, m_moved, a_moved,
        m_first, a_first, m_last, a_last,
        ws_x, stiff_x, f1_x, f2_x, kf, base,
        g_send, g_one, g_mid, g_two, q_send, q_one, q_mid, q_two,
        u_rows, zcols,
        load_sem, all_send, all_recv, halo_send, halo_recv, wall_send, wall_recv, tree_send, tree_recv, out_sem,
    ) = refs
    me = lax.axis_index("solver") * SP + lax.axis_index("space")
    left, right = lax.rem(me + D - 1, D), lax.rem(me + 1, D)
    keep_l = jnp.where(me > 0, 1.0, 0.0).astype(F32)
    keep_r = jnp.where(me < D - 1, 1.0, 0.0).astype(F32)

    def at_device(d):
        return (d // SP, lax.rem(d, SP))

    def remote(src, dst, send, recv, d):
        return pltpu.make_async_remote_copy(
            src_ref=src,
            dst_ref=dst,
            send_sem=send,
            recv_sem=recv,
            device_id=at_device(d),
            device_id_type=MESH,
        )

    def spot(xx):
        return CX - 2 if xx == 0 else xx - 1 if xx < CX - 1 else xx

    loads = [
        pltpu.make_async_copy(src, dst, load_sem.at[i])
        for i, (src, dst) in enumerate(
            (
                (owner_hbm, owner),
                (cell_hbm, cell),
                (normal_hbm, normal),
                (x_hbm, x0),
                (p_hbm, pa.at[:, pl.ds(8, NY), :]),
                (ws_hbm, ws_v),
                (stiff_hbm, stiff_v),
                (load_hbm, load_v),
                (v_hbm, vres),
                (w_hbm, vout),
                (coef_hbm, weight),
            )
            + tuple(
                (rhs_hbm.at[pl.ds(xx * NY, NY), :], rhs.at[pl.ds(spot(xx) * NY, NY), :])
                for xx in range(CX)
            )
        )
    ]
    for copy in loads:
        copy.start()
    barrier = pltpu.get_barrier_semaphore()

    NS = D // SP
    my_s, my_p = me // SP, lax.rem(me, SP)

    def peers(act):
        for ds in sorted(range(NS), key=lambda q: -min(q, NS - q)):
            there = lax.rem(my_s + ds, NS)

            def one(k, _):
                act(there, lax.rem(my_p + SP // 2 + k, SP))
                return 0

            if ds:
                lax.fori_loop(0, SP, one, 0, unroll=4)
            else:
                lax.fori_loop(0, SP // 2, one, 0, unroll=4 if SP >= 8 else 1)
                lax.fori_loop(SP // 2 + 1, SP, one, 0, unroll=3 if SP >= 8 else 1)

    def start_remote(src, dst, r, there, low):
        pltpu.make_async_remote_copy(
            src_ref=src,
            dst_ref=dst,
            send_sem=all_send.at[r],
            recv_sem=all_recv.at[r],
            device_id=(there, low),
            device_id_type=MESH,
        ).start()

    def greet(there, low):
        pl.semaphore_signal(barrier, inc=1, device_id=(there, low), device_id_type=MESH)

    peers(greet)

    def each(msg, arrived, r):
        peers(lambda there, low: start_remote(msg.at[there * SP + low], arrived.at[me], r, there, low))
        arrived[me] = msg[me]

    def same(row, arrived, r):
        peers(lambda there, low: start_remote(row, arrived.at[me], r, there, low))
        arrived[me] = row[...]

    def all_arrived(arrived, r):
        part = arrived.at[pl.ds(0, D - 1)]
        remote(part, part, all_send.at[r], all_recv.at[r], right).wait_recv()

    def all_sent(arrived, r):
        part = arrived.at[pl.ds(0, D - 1)]
        remote(part, part, all_send.at[r], all_recv.at[r], right).wait_send()

    lo, hi = lax.rem(me, LO), me // LO

    def tree_one(send, one, r):
        for k in range(1, LO):
            d = hi * LO + lax.rem(lo + k, LO)
            remote(send, one.at[lo], tree_send.at[r], tree_recv.at[r], d).start()
        one[lo] = send[...]

    def tree_two(one, mid, two, r):
        part = one.at[pl.ds(0, LO - 1)]
        remote(part, part, tree_send.at[r], tree_recv.at[r], right).wait()
        mid[...] = jnp.sum(one[...], axis=0)
        for k in range(1, HI):
            d = lax.rem(hi + k, HI) * LO + lo
            remote(mid, two.at[hi], tree_send.at[r + 1], tree_recv.at[r + 1], d).start()
        two[hi] = mid[...]

    def tree_end(two, r):
        part = two.at[pl.ds(0, HI - 1)]
        remote(part, part, tree_send.at[r + 1], tree_recv.at[r + 1], right).wait()
        return jnp.sum(two[...], axis=0)

    for copy in loads[:4]:
        copy.wait()
    block = min(IF, LANES)
    before = mask(iota((block, block), 0) < iota((block, block), 1)).astype(BF16)
    ones = jnp.ones((block, block), BF16)
    carry = jnp.zeros((D, block), F32)
    for b in range(IF // block):
        cols = pl.ds(b * block, block)
        hot = mask(owner[:, cols] == iota((D, block), 0))
        owner_hot[:, cols] = hot
        hot16 = hot.astype(BF16)
        rank = jnp.sum(hot * (carry + dot(hot16, before, (1, 0))), axis=0, keepdims=True)
        carry = carry + dot(hot16, ones, (1, 0))
        slot = lax.rem(iota((LANES, block), 0), SLOTS).astype(F32)
        rank_hot[:, cols] = mask(slot == rank)
    x = x0[...]
    nrm = normal[...]
    flux = SOURCE_GAIN * jnp.sum(nrm * x[0:3], axis=0, keepdims=True)
    group = iota((LANES, IF), 0) // SLOTS
    named = (cell[...] + 1).astype(F32)
    squared = jnp.sum(nrm * nrm, axis=0, keepdims=True)
    along = jnp.sum(nrm * x[3:6], axis=0, keepdims=True)
    packed = jnp.where(group == 2, squared, jnp.where(group == 3, along, 0.0))
    packed = jnp.where(group == 0, flux, jnp.where(group == 1, named, packed))
    packed = rank_hot[...] * packed
    m_cells[:, 0, :] = dot(owner_hot[...], packed, (1, 1), True)

    pl.semaphore_wait(barrier, D - 1)
    each(m_cells, a_cells, CELLS)

    def halo(buf, e, ch):
        rows = pl.ds(pl.multiple_of(ch * (NY // NCH), 8), NY // NCH)
        inner = pl.ds(pl.multiple_of(ch * (NY // NCH) + 8, 8), NY // NCH)
        to_left = remote(
            buf.at[0, inner, :], halo_r.at[e, rows, :], halo_send.at[e, 0, ch], halo_recv.at[e, 0, ch], left
        )
        to_right = remote(
            buf.at[CX - 1, inner, :], halo_l.at[e, rows, :], halo_send.at[e, 1, ch], halo_recv.at[e, 1, ch], right
        )
        return to_left, to_right

    loads[4].wait()
    for ch in range(NCH):
        for copy in halo(pa, 0, ch):
            copy.start()

    for copy in loads[5:8]:
        copy.wait()
    for w in range(W1):
        for c in range(3):
            ws_x[1 + w, c] = ws_v[c, :, w, :]
        stiff_x[1 + w] = stiff_v[:, w, :]

    def planes(buf, width, count, r):
        return (
            remote(buf.at[pl.ds(width, width)], buf.at[pl.ds(width + count, width)], wall_send.at[r, 0], wall_recv.at[r, 0], left),
            remote(buf.at[pl.ds(count, width)], buf.at[pl.ds(0, width)], wall_send.at[r, 1], wall_recv.at[r, 1], right),
        )

    wall_static = planes(ws_x, 1, W1, 0) + planes(stiff_x, 1, W1, 1)
    for copy in wall_static:
        copy.start()

    pad = jnp.zeros((CX, 8, NZ), F32)
    for buf in (pa, pb):
        buf[:, pl.ds(0, 8), :] = pad
        buf[:, pl.ds(NY + 8, 8), :] = pad

    loads[8].wait()
    loads[9].wait()
    per_row = LANES // SLOTS

    def weights(ref, at_row, factor, first):
        u = sum(ref[at_row + c] * (factor * nrm[c : c + 1]) for c in range(3))
        for q in range(H // per_row):
            for i in range(per_row):
                a = q * per_row + i
                u_rows[i * SLOTS : (i + 1) * SLOTS, :] = rank_hot[0:SLOTS, :] * u[a : a + 1, :]
            m_weights[:, first + q, :] = dot(owner_hot[...], u_rows[...], (1, 1), True)

    weights(vres, 3, 1.0, 0)
    weights(vout, 0, SOURCE_GAIN, H // per_row)

    def layers(f):
        row = iota(f.shape, 1)
        up = jnp.where(row == 0, 0.0, pltpu.roll(f, 1, 1))
        down = jnp.where(row == L3 - 1, 0.0, pltpu.roll(f, L3 - 1, 1))
        return up + down + pltpu.roll(f, 1, 2) + pltpu.roll(f, S2 - 1, 2)

    def tangent(low, f, high, stiff):
        return (6.0 + stiff)[None] * f - (low + high + layers(f))

    for copy in wall_static:
        copy.wait()

    def force(x_now, dest):
        for w in range(W1):
            part = pl.ds(w * S2, S2)
            for c in range(3):
                b = base[w, c]
                t = x_now[3 + c : 4 + c, w * S2 : (w + 1) * S2]
                row = iota((L3, S2), 0)
                dest[2 + w, c] = b + jnp.where(row == 0, t, 0.0)

    for w in range(W1):
        low = ws_x[w] * (keep_l if w == 0 else 1.0)
        high = ws_x[w + 2] * (keep_r if w == W1 - 1 else 1.0)
        k_w = tangent(low, ws_x[w + 1], high, stiff_x[w + 1])
        for c in range(3):
            base[w, c] = load_v[c, :, w, :] - k_w[c]
    force(x, f1_x)
    wall_f1 = planes(f1_x, 2, W1, 2)
    for copy in wall_f1:
        copy.start()

    gram = jnp.zeros((H, H), F32)
    for c in range(6):
        v_c = vres[c]
        gram = gram + dot(v_c, v_c, (1, 1), True)
    g_send[0:H, 0:H] = gram
    for copy in loads[10:]:
        copy.wait()

    def invert(i, _):
        rows = pl.ds(pl.multiple_of(i * RC, 8), RC)
        for xx in range(CX):
            weight[xx, rows, :] = OMEGA / (6.0 + weight[xx, rows, :])
        return 0

    lax.fori_loop(0, NY // RC, invert, 0)

    all_arrived(a_cells, CELLS)
    y_bits, z_bits = NY.bit_length() - 1, NZ.bit_length() - 1

    def placed(cells):
        xx = cells >> (y_bits + z_bits)
        xx = jnp.where(xx == 0, CX - 2, jnp.where((xx > 0) & (xx < CX - 1), xx - 1, xx))
        return xx * NY + jnp.bitwise_and(cells >> z_bits, NY - 1)

    got = a_cells[:, 0, :]
    found = got[:, SLOTS : 2 * SLOTS].astype(jnp.int32) - 1
    row_of = placed(found)
    zcols[:, 0:SLOTS] = jnp.bitwise_and(found, NZ - 1)
    flipped = got.T[SLOTS : 2 * SLOTS, :].astype(jnp.int32) - 1
    row_flat = placed(flipped)

    def mark(xx, _):
        for j in range(SLOTS):
            hit = iota((NY, D), 0) + xx * NY == row_flat[j : j + 1, :]
            at[pl.ds(pl.multiple_of(xx * NY, 8), NY), j * D : (j + 1) * D] = mask(hit).astype(BF16)
        return 0

    lax.fori_loop(0, CX, mark, 0)

    def spread(flux_now):
        for j in range(SLOTS):
            f_j = flux_now[:, j : j + 1]
            top = f_j.astype(BF16).astype(F32)
            here = zcols[:, j : j + 1] == iota((D, NZ), 1)
            f_hi[j * D : (j + 1) * D, :] = jnp.where(here, top, 0.0).astype(BF16)
            f_lo[j * D : (j + 1) * D, :] = jnp.where(here, f_j - top, 0.0).astype(BF16)

    inner_rows, edge_rows = (0, (CX - 2) * NY), ((CX - 2) * NY, 2 * NY)

    def place(which):
        rows = pl.ds(*which)
        hot = at[rows, :]
        found_here = dot(hot, f_hi[...], (1, 0)) + dot(hot, f_lo[...], (1, 0))
        total[rows, :] = rhs[rows, :] + found_here

    spread(got)
    place(edge_rows)

    def update(src, dst, xx, y0, up, down):
        ext = src[xx, pl.ds(y0, RC + 16), :]
        c = ext[8 : 8 + RC]
        beside = pltpu.roll(ext, 1, 0)[8 : 8 + RC] + pltpu.roll(ext, RC + 15, 0)[8 : 8 + RC]
        lane = iota((RC, NZ), 1)
        beside = beside + jnp.where(lane == 0, 0.0, pltpu.roll(c, 1, 1))
        beside = beside + jnp.where(lane == NZ - 1, 0.0, pltpu.roll(c, NZ - 1, 1))
        rows = pl.ds(pl.multiple_of(spot(xx) * NY + y0, 8), RC)
        new = (1.0 - OMEGA) * c + weight[xx, pl.ds(y0, RC), :] * (total[rows, :] + up + down + beside)
        dst[xx, pl.ds(pl.multiple_of(y0 + 8, 8), RC), :] = new

    chunk = NY // NCH

    def edges(e, src, dst, send):
        if e >= 1:
            for ch in range(NCH):
                for copy in halo(dst, e - 1, ch):
                    copy.wait_send()

        def edge(ch, _):
            to_left, to_right = halo(src, e, ch)
            to_left.wait_recv()
            to_right.wait_recv()

            def part(i, _):
                y0 = pl.multiple_of(ch * chunk + i * RC, 8)
                up = halo_l[e, pl.ds(y0, RC), :] * keep_l
                down = src[1, pl.ds(pl.multiple_of(y0 + 8, 8), RC), :]
                update(src, dst, 0, y0, up, down)
                up = src[CX - 2, pl.ds(pl.multiple_of(y0 + 8, 8), RC), :]
                down = halo_r[e, pl.ds(y0, RC), :] * keep_r
                update(src, dst, CX - 1, y0, up, down)
                return 0

            lax.fori_loop(0, chunk // RC, part, 0)
            if send:
                for copy in halo(dst, e + 1, ch):
                    copy.start()
            return 0

        lax.fori_loop(0, NCH, edge, 0)

    def inside(src, dst):
        def inner(i, _):
            y0 = pl.multiple_of(i * RC, 8)
            for xx in range(1, CX - 1):
                up = src[xx - 1, pl.ds(pl.multiple_of(y0 + 8, 8), RC), :]
                down = src[xx + 1, pl.ds(pl.multiple_of(y0 + 8, 8), RC), :]
                update(src, dst, xx, y0, up, down)
            return 0

        lax.fori_loop(0, NY // RC, inner, 0)

    def moments(f_x, copies, dest, first):
        for copy in copies:
            copy.wait()
        ext = []
        for i in range(W1 + 4):
            f = f_x[i]
            ext.append(f * keep_l if i < 2 else f * keep_r if i >= W1 + 2 else f)
        image = []
        for i in range(W1 + 2):
            image.append(tangent(ext[i], ext[i + 1], ext[i + 2], stiff_x[i]))
        image[0] = image[0] * keep_l
        image[-1] = image[-1] * keep_r
        sums = [jnp.zeros((L3, S2), F32) for _ in range(4)]
        for w in range(W1):
            f, k1 = ext[w + 2], image[w + 1]
            k2 = tangent(image[w], k1, image[w + 2], stiff_x[w + 1])
            kf[w] = k1
            for n, (one, two) in enumerate(((f, f), (f, k1), (k1, k1), (k1, k2))):
                sums[n] = sums[n] + jnp.sum(one * two, axis=0)
        for n in range(4):
            s = jnp.sum(sums[n], axis=0, keepdims=True)
            width = min(S2, LANES)
            s = sum(s[:, i * width : (i + 1) * width] for i in range(S2 // width))
            dest[first + n : first + n + 1, 0:width] = s

    def wall_update(f_x, rows):
        width = min(S2, LANES)
        m0, m1, m2, m3 = (jnp.sum(rows[n : n + 1, 0:width], axis=1, keepdims=True) for n in range(4))
        alpha0 = m0 / m1
        left_over = m0 - 2.0 * alpha0 * m1 + alpha0 * alpha0 * m2
        grow = 1.0 + left_over / m0
        alpha1 = left_over / (grow * grow * m1 - 2.0 * grow * alpha0 * m2 + alpha0 * alpha0 * m3)
        on_f, on_k = alpha0 + alpha1 * grow, alpha1 * alpha0
        new = []
        for w in range(W1):
            new.append(ws_x[w + 1] + on_f[None] * f_x[w + 2] - on_k[None] * kf[w])
        rows_out = [
            jnp.concatenate([new[w][c, 0:1, :] for w in range(W1)], axis=1) for c in range(3)
        ]
        return new, jnp.concatenate(rows_out, axis=0)

    def sample(which, planes_of):
        def cut(i, _):
            for xx in planes_of:
                v = pa[xx, pl.ds(pl.multiple_of(i * RC + 8, 8), RC), :]
                top = v.astype(BF16)
                rows = pl.ds(pl.multiple_of(spot(xx) * NY + i * RC, 8), RC)
                p_hi[rows, :] = top
                p_lo[rows, :] = (v - top.astype(F32)).astype(BF16)
            return 0

        lax.fori_loop(0, NY // RC, cut, 0)
        lane = lax.rem(iota((D, LANES), 1), SLOTS)
        out = jnp.zeros((D, LANES), F32)
        first, count = which
        rows = pl.ds(first, count)
        for j in range(0, SLOTS, 2):
            hot = a_mat[j * D : (j + 2) * D, first : first + count]
            got_rows = dot(hot, p_hi[rows, :], (1, 0)) + dot(hot, p_lo[rows, :], (1, 0))
            for i in range(2):
                here = zcols[:, j + i : j + i + 1] == iota((D, NZ), 1)
                part = got_rows[i * D : (i + 1) * D]
                col = jnp.sum(jnp.where(here, part, 0.0), axis=1, keepdims=True)
                out = jnp.where(lane == j + i, col, out)
        return out

    mid = tuple(range(1, CX - 1))
    ends = (0, CX - 1)

    def unpack(arrived):
        rows = dot(arrived[:, 0, 0:SLOTS], owner_hot[...], (0, 0), True)
        return jnp.sum(rows * rank_hot[pl.ds(0, SLOTS), :], axis=0, keepdims=True)

    def against(v):
        acc = sum(vres[c] * v[c : c + 1] for c in range(6))
        return jnp.sum(acc, axis=1, keepdims=True)

    def combine(coef, first):
        rows = [jnp.sum(coef * vout[c], axis=0, keepdims=True) for c in range(6)]
        return first + jnp.concatenate(rows, axis=0)

    def as_row(col):
        return jnp.sum(jnp.where(iota((H, LANES), 0) == iota((H, LANES), 1), col, 0.0), axis=0, keepdims=True)

    edges(0, pa, pb, True)
    place(inner_rows)
    inside(pa, pb)
    moments(f1_x, wall_f1, g_send, H)
    tree_one(g_send, g_one, 0)
    edges(1, pb, pa, True)
    inside(pb, pa)
    each(m_weights, a_weights, WEIGHTS)
    tree_two(g_one, g_mid, g_two, 0)
    edges(2, pa, pb, True)
    inside(pa, pb)
    for j in range(SLOTS):
        a_mat[j * D : (j + 1) * D, :] = mask(row_of[:, j : j + 1] == iota((D, R), 1)).astype(BF16)
    g_all = tree_end(g_two, 0)
    gram = g_all[0:H, :]
    _, solid1 = wall_update(f1_x, g_all[H : H + 8, :])
    flux = SOURCE_GAIN * jnp.sum(nrm * solid1, axis=0, keepdims=True)
    m_solid[:, 0, :] = dot(owner_hot[...], rank_hot[...] * flux, (1, 1), True)
    known = jnp.concatenate([solid1 - x[0:3], -x[3:6]], axis=0)
    h_known = against(known)
    inside(pb, pa)
    seen1 = sample(inner_rows, mid)
    edges(3, pb, pa, True)
    each(m_solid, a_solid, SOLID)
    all_arrived(a_weights, WEIGHTS)

    seen1 = seen1 + sample(edge_rows, ends)
    mine = iota((H, LANES), 1) // SLOTS == lax.rem(iota((H, LANES), 0), per_row)

    def owned(values):
        rows = [
            jnp.sum(a_weights[:, q, :] * values, axis=0, keepdims=True) for q in range(H // per_row)
        ]
        rows = jnp.concatenate([jnp.broadcast_to(f, (per_row, LANES)) for f in rows], axis=0)
        return jnp.sum(jnp.where(mine, rows, 0.0), axis=1, keepdims=True)

    m_first[...] = as_row(h_known - owned(seen1))
    same(m_first, a_first, FIRST)
    m_back[:, 0, :] = seen1
    each(m_back, a_back, BACK)
    square = iota((H, LANES), 0) == iota((H, LANES), 1)
    gram = jnp.where(iota((H, LANES), 1) < H, gram, 0.0)
    on_diag = jnp.where(square, gram, 0.0)
    trace = jnp.sum(jnp.sum(on_diag, axis=1, keepdims=True), axis=0, keepdims=True)
    ridge = RIDGE * trace / H + TINY
    beside = mask(iota((H, LANES), 1) == iota((H, LANES), 0) + H)
    inverse = eliminate(gram + jnp.where(square, ridge, 0.0) + beside, H)
    inverse = jnp.where(iota((H, LANES), 1) < H, pltpu.roll(inverse, LANES - H, 1), 0.0)
    all_arrived(a_solid, SOLID)
    all_arrived(a_first, FIRST)
    h_row = jnp.sum(a_first[...], axis=0)
    coeffs = -jnp.sum(inverse * h_row, axis=1, keepdims=True)
    extra = jnp.zeros((D, LANES), F32)
    for q in range(H // per_row):
        pick = iota((H, LANES), 0) == q * per_row + iota((H, LANES), 1) // SLOTS
        c_row = jnp.sum(jnp.where(pick, coeffs, 0.0), axis=0, keepdims=True)
        extra = extra + a_weights[:, H // per_row + q, :] * c_row
    step = LANES // 2
    while step >= SLOTS:
        extra = extra + pltpu.roll(extra, step, 1)
        step //= 2
    spread(a_solid[:, 0, :] + extra)
    place(edge_rows)

    edges(4, pa, pb, True)
    all_arrived(a_back, BACK)
    out1 = jnp.concatenate([solid1, -unpack(a_back) * nrm], axis=0)
    res1 = out1 - x
    x2 = combine(coeffs, out1)
    force(x2, f2_x)
    wall_f2 = planes(f2_x, 2, W1, 3)
    for copy in wall_f2:
        copy.start()
    place(inner_rows)
    inside(pa, pb)
    edges(5, pb, pa, True)
    inside(pb, pa)
    moments(f2_x, wall_f2, q_send, 0)
    tree_one(q_send, q_one, 2)
    moved = x2[3:6] - x[3:6]
    step_along = jnp.sum(nrm * moved, axis=0, keepdims=True)
    m_moved[:, 0, :] = dot(owner_hot[...], rank_hot[...] * step_along, (1, 1), True)
    edges(6, pa, pb, True)
    tree_two(q_one, q_mid, q_two, 2)
    inside(pa, pb)
    each(m_moved, a_moved, MOVED)
    shifted = pltpu.roll(pltpu.roll(gram, 1, 0), 1, 1)
    low = (iota((H, LANES), 0) > 0) & (iota((H, LANES), 1) > 0) & (iota((H, LANES), 1) < H)
    small_out[0:H, :] = jnp.where(low, shifted, 0.0)
    inside(pb, pa)
    seen2 = sample(inner_rows, mid)
    new, solid2 = wall_update(f2_x, tree_end(q_two, 2))
    for w in range(W1):
        for c in range(3):
            wall_out[c, :, w, :] = new[w][c]
    known = jnp.concatenate([solid2 - x2[0:3] - res1[0:3], -moved], axis=0)
    cross_known = against(known)
    own_known = jnp.sum(jnp.sum(known * known, axis=1, keepdims=True), axis=0, keepdims=True)
    old_known = jnp.sum(jnp.sum(known * res1, axis=1, keepdims=True), axis=0, keepdims=True)
    edges(7, pb, pa, False)
    save = pltpu.make_async_copy(pa.at[:, pl.ds(8, NY), :], p_out, out_sem)
    save.start()
    all_arrived(a_moved, MOVED)
    seen2 = seen2 + sample(edge_rows, ends)
    gained = seen2 - seen1
    cells_msg = a_cells[:, 0, :]
    n_n = pltpu.roll(cells_msg, LANES - 2 * SLOTS, 1)
    n_t = pltpu.roll(cells_msg, LANES - 3 * SLOTS, 1)
    single = iota((D, LANES), 1) < SLOTS
    own = jnp.where(single, gained * (gained * n_n + 2.0 * a_moved[:, 0, :]), 0.0)
    old = jnp.where(single, gained * (seen1 * n_n + n_t), 0.0)
    own = own_known + jnp.sum(jnp.sum(own, axis=0, keepdims=True), axis=1, keepdims=True)
    old = old_known + jnp.sum(jnp.sum(old, axis=0, keepdims=True), axis=1, keepdims=True)
    lane = iota((1, LANES), 1)
    cross = as_row(cross_known - owned(gained))
    m_last[...] = jnp.where(lane == H, own, jnp.where(lane == H + 1, old, cross))
    same(m_last, a_last, LAST)
    m_back2[:, 0, :] = seen2
    each(m_back2, a_back2, BACK2)
    small_out[H + 1 : H + 2, :] = h_row
    small_out[H + 2 : H + 3, :] = jnp.broadcast_to(
        trace - gram[H - 1 : H, H - 1 : H], (1, LANES)
    )
    all_arrived(a_last, LAST)
    small_out[H : H + 1, :] = jnp.sum(a_last[...], axis=0)
    all_arrived(a_back2, BACK2)
    out2 = jnp.concatenate([solid2, -unpack(a_back2) * nrm], axis=0)
    points_out[0] = out2
    points_out[1] = out2 - out1

    for arrived, r in (
        (a_cells, CELLS),
        (a_weights, WEIGHTS),
        (a_solid, SOLID),
        (a_first, FIRST),
        (a_back, BACK),
        (a_moved, MOVED),
        (a_back2, BACK2),
        (a_last, LAST),
    ):
        all_sent(arrived, r)
    for ch in range(NCH):
        for copy in halo(pb, SWEEPS * COUPLE - 1, ch):
            copy.wait_send()
    save.wait()


def finish(H, p_in, wall_in, points, small, w_hbm, state_out, p_out, wall_out, vout, p_v, wall_v, sem):
    parts = p_in.shape[0]
    pairs = [(wall_in, wall_v, wall_out)]
    pairs += [(p_in.at[i], p_v.at[i], p_out.at[i]) for i in range(parts)]
    come = [pltpu.make_async_copy(a, b, sem.at[0, i]) for i, (a, b, _) in enumerate(pairs)]
    leave = [pltpu.make_async_copy(b, c, sem.at[1, i]) for i, (_, b, c) in enumerate(pairs)]
    fetch = pltpu.make_async_copy(w_hbm, vout, sem.at[0, parts + 1])
    for copy in come:
        copy.start()
    fetch.start()
    lane, row = iota((1, LANES), 1), iota((H, LANES), 0)
    lanes = iota((H, LANES), 1)
    square = row == lanes

    def as_col(values):
        return jnp.sum(jnp.where(square, values, 0.0), axis=1, keepdims=True)

    last, h_row = small[H : H + 1, :], small[H + 1 : H + 2, :]
    own, old = last[:, H : H + 1], last[:, H + 1 : H + 2]
    cross = jnp.where((lane > 0) & (lane < H), pltpu.roll(last, 1, 1), jnp.where(lane == 0, own, 0.0))
    h_row = pltpu.roll(jnp.where(lane < H, h_row, 0.0), 1, 1)
    h_row = jnp.where(lane == 0, own + old, h_row + cross)
    gram = jnp.where(row == 0, cross, jnp.where(lanes == 0, as_col(cross), small[0:H, :]))
    ridge = RIDGE * (small[H + 2 : H + 3, 0:1] + own) / H + TINY
    gram = gram + jnp.where(square, ridge, 0.0)
    gram = jnp.where(lanes == H, as_col(h_row), gram)
    gram = eliminate(gram, H // 4)
    for a, b in zip(come, leave, strict=True):
        a.wait()
        b.start()
    coeffs = -eliminate(gram, H, H // 4)[:, H : H + 1]
    rest = jnp.where(iota((H, 1), 0) < H - 1, pltpu.roll(coeffs * jnp.ones((H, LANES), F32), H - 1, 0)[:, 0:1], 0.0)
    fetch.wait()
    rows = [jnp.sum(rest * vout[c], axis=0, keepdims=True) for c in range(6)]
    state_out[...] = points[0] + coeffs[0:1, :] * points[1] + jnp.concatenate(rows, axis=0)
    for copy in leave:
        copy.wait()


def local(cfg, *args):
    (D, SP, LO, CX, NY, NZ, L3, W1, S2, IF, H, NCH, RC) = cfg
    (p, coef, rhs, ws, stiff, load, normals, owner, cell, x, vres, vout) = args
    vres, vout = vres.transpose(1, 0, 2), vout.transpose(1, 0, 2)
    R, K = CX * NY, SLOTS * D
    EX = SWEEPS * COUPLE
    wide = LANES
    G = H + 8

    def vmem(*shape, dtype=F32):
        return pltpu.VMEM(shape, dtype)

    dma = pltpu.SemaphoreType.DMA
    scratch = [
        vmem(CX, NY + 16, NZ), vmem(CX, NY + 16, NZ), vmem(CX, NY, NZ), vmem(R, NZ), vmem(R, NZ),
        vmem(EX, NY, NZ), vmem(EX, NY, NZ),
        vmem(R, K, dtype=BF16), vmem(K, R, dtype=BF16), vmem(K, NZ, dtype=BF16), vmem(K, NZ, dtype=BF16),
        vmem(R, NZ, dtype=BF16), vmem(R, NZ, dtype=BF16),
        vmem(3, L3, W1, S2), vmem(L3, W1, S2), vmem(3, L3, W1, S2),
        vmem(3, IF), vmem(1, IF, dtype=jnp.int32), vmem(1, IF, dtype=jnp.int32), vmem(6, IF),
        vmem(6, H, IF), vmem(6, H, IF),
        vmem(D, IF), vmem(LANES, IF),
        vmem(D, 1, wide), vmem(D, 1, wide), vmem(D, 8, wide), vmem(D, 8, wide),
        vmem(D, 1, wide), vmem(D, 1, wide), vmem(D, 1, wide), vmem(D, 1, wide), vmem(D, 1, wide), vmem(D, 1, wide),
        vmem(D, 1, wide), vmem(D, 1, wide),
        vmem(1, wide), vmem(D, 1, wide), vmem(1, wide), vmem(D, 1, wide),
        vmem(W1 + 2, 3, L3, S2), vmem(W1 + 2, L3, S2), vmem(W1 + 4, 3, L3, S2), vmem(W1 + 4, 3, L3, S2),
        vmem(W1, 3, L3, S2), vmem(W1, 3, L3, S2),
        vmem(G, wide), vmem(LO, G, wide), vmem(G, wide), vmem(D // LO, G, wide),
        vmem(8, wide), vmem(LO, 8, wide), vmem(8, wide), vmem(D // LO, 8, wide),
        vmem(LANES, IF), vmem(D, SLOTS, dtype=jnp.int32),
        dma((11 + CX,)), dma((ROUNDS,)), dma((ROUNDS,)), dma((EX, 2, NCH)), dma((EX, 2, NCH)),
        dma((4, 2)), dma((4, 2)), dma((4,)), dma((4,)), dma(()),
    ]
    anywhere = pl.BlockSpec(memory_space=pl.ANY)
    inside = pl.BlockSpec(memory_space=pltpu.VMEM)
    points, small, pressure, wall = pl.pallas_call(
        functools.partial(kernel, cfg),
        out_shape=(
            jax.ShapeDtypeStruct((2, 6, IF), F32),
            jax.ShapeDtypeStruct((H + 8, LANES), F32),
            jax.ShapeDtypeStruct((CX, NY, NZ), F32),
            jax.ShapeDtypeStruct((3, L3, W1, S2), F32),
        ),
        in_specs=[anywhere] * 12,
        out_specs=(inside, inside, anywhere, inside),
        scratch_shapes=scratch,
        compiler_params=pltpu.CompilerParams(
            collective_id=0, has_side_effects=True, vmem_limit_bytes=60 * 2**20
        ),
    )(
        p, coef, rhs.reshape(R, NZ), ws, stiff, load, normals,
        owner.reshape(1, IF), cell.reshape(1, IF), x, vres, vout,
    )
    return pl.pallas_call(
        functools.partial(finish, H),
        out_shape=(
            jax.ShapeDtypeStruct((6, IF), F32),
            jax.ShapeDtypeStruct((CX, NY, NZ), F32),
            jax.ShapeDtypeStruct((3, L3, W1, S2), F32),
        ),
        in_specs=[anywhere, anywhere, inside, inside, anywhere],
        out_specs=(inside, anywhere, anywhere),
        scratch_shapes=[vmem(6, H, IF), vmem(CX, NY, NZ), vmem(3, L3, W1, S2), dma((2, CX + 2))],
    )(pressure, wall, points, small, vout)


def solution(mesh):
    sp = mesh.shape["space"]
    devices = mesh.shape["solver"] * sp

    def run(*args):
        CX, NY, NZ = args[0].shape
        _, L3, W1, S2 = args[3].shape
        IF, H = args[8].shape[0], args[10].shape[0]
        lo = 8 if devices > 8 else 4
        cfg = (devices, sp, lo, CX, NY, NZ, L3, W1, S2, IF, H, 4, min(32, NY // 4))
        return local(cfg, *args)

    in_specs = (
        P(BOTH, None, None),
        P(BOTH, None, None),
        P(BOTH, None, None),
        P(None, None, BOTH, None),
        P(None, BOTH, None),
        P(None, None, BOTH, None),
        P(None, BOTH),
        P(BOTH, None),
        P(BOTH),
        P(None, BOTH),
        P(None, None, BOTH),
        P(None, None, BOTH),
    )
    out_specs = (P(None, BOTH), P(BOTH, None, None), P(None, None, BOTH, None))
    return jax.shard_map(run, mesh=mesh, in_specs=in_specs, out_specs=out_specs, check_vma=False)
```

```python
import functools

import jax
import jax.numpy as jnp
from jax import lax
from jax.experimental import pallas as pl
from jax.experimental.pallas import tpu as pltpu
from jax.sharding import PartitionSpec as P

SWEEPS = 4
COUPLE = 2
OMEGA = 0.8
SOURCE_GAIN = 4.0
RIDGE = 0.1
TINY = 1e-06
SLOTS = 16
LANES = 128
MESH = pl.DeviceIdType.MESH
F32 = jnp.float32
BF16 = jnp.bfloat16
BOTH = ("solver", "space")
CELLS, WEIGHTS, SOLID, FIRST, BACK, MOVED, BACK2, LAST = range(8)
ROUNDS = 8


def iota(shape, dim):
    return lax.broadcasted_iota(jnp.int32, shape, dim)


def dot(a, b, contract, exact=False):
    return lax.dot_general(
        a,
        b,
        (((contract[0],), (contract[1],)), ((), ())),
        precision=lax.Precision.HIGHEST if exact else None,
        preferred_element_type=F32,
    )


def mask(flag):
    return jnp.where(flag, 1.0, 0.0).astype(F32)


def eliminate(m, size):
    row = iota(m.shape, 0)
    for k in range(size):
        pivot_row = m[k : k + 1, :] / m[k : k + 1, k : k + 1]
        m = jnp.where(row == k, pivot_row, m - m[:, k : k + 1] * pivot_row)
    return m


def kernel(cfg, *refs):
    (D, SP, LO, CX, NY, NZ, L3, W1, S2, IF, H, NCH, RC) = cfg
    HI = D // LO
    R, K = CX * NY, SLOTS * D
    (
        p_hbm, coef_hbm, rhs_hbm, ws_hbm, stiff_hbm, load_hbm, normal_hbm, owner_hbm, cell_hbm, x_hbm, v_hbm, w_hbm,
        state_out, p_out, wall_out,
        pa, pb, weight, rhs, total, halo_l, halo_r, at, a_mat, f_hi, f_lo, p_hi, p_lo,
        ws_v, stiff_v, load_v, normal, owner, cell, x0, vres, vout,
        owner_hot, rank_hot,
        m_cells, a_cells, m_weights, a_weights, m_solid, a_solid, m_back, a_back, m_back2, a_back2, m_moved, a_moved,
        m_first, a_first, m_last, a_last,
        ws_x, stiff_x, f1_x, f2_x, kf, base,
        g_send, g_one, g_mid, g_two, q_send, q_one, q_mid, q_two,
        u_rows, zcols,
        load_sem, all_send, all_recv, halo_send, halo_recv, wall_send, wall_recv, tree_send, tree_recv, out_sem,
    ) = refs
    me = lax.axis_index("solver") * SP + lax.axis_index("space")
    left, right = lax.rem(me + D - 1, D), lax.rem(me + 1, D)
    keep_l = jnp.where(me > 0, 1.0, 0.0).astype(F32)
    keep_r = jnp.where(me < D - 1, 1.0, 0.0).astype(F32)

    def at_device(d):
        return (d // SP, lax.rem(d, SP))

    def remote(src, dst, send, recv, d):
        return pltpu.make_async_remote_copy(
            src_ref=src,
            dst_ref=dst,
            send_sem=send,
            recv_sem=recv,
            device_id=at_device(d),
            device_id_type=MESH,
        )

    def spot(xx):
        return CX - 2 if xx == 0 else xx - 1 if xx < CX - 1 else xx

    loads = [
        pltpu.make_async_copy(src, dst, load_sem.at[i])
        for i, (src, dst) in enumerate(
            (
                (owner_hbm, owner),
                (cell_hbm, cell),
                (normal_hbm, normal),
                (x_hbm, x0),
                (p_hbm, pa.at[:, pl.ds(8, NY), :]),
                (ws_hbm, ws_v),
                (stiff_hbm, stiff_v),
                (load_hbm, load_v),
                (v_hbm, vres),
                (w_hbm, vout),
                (coef_hbm, weight),
            )
            + tuple(
                (rhs_hbm.at[pl.ds(xx * NY, NY), :], rhs.at[pl.ds(spot(xx) * NY, NY), :])
                for xx in range(CX)
            )
        )
    ]
    for copy in loads:
        copy.start()
    barrier = pltpu.get_barrier_semaphore()

    NS = D // SP
    my_s, my_p = me // SP, lax.rem(me, SP)

    def peers(act):
        for ds in sorted(range(NS), key=lambda q: -min(q, NS - q)):
            there = lax.rem(my_s + ds, NS)

            def one(k, _):
                act(there, lax.rem(my_p + SP // 2 + k, SP))
                return 0

            if ds:
                lax.fori_loop(0, SP, one, 0, unroll=4)
            else:
                lax.fori_loop(0, SP // 2, one, 0, unroll=4 if SP >= 8 else 1)
                lax.fori_loop(SP // 2 + 1, SP, one, 0, unroll=3 if SP >= 8 else 1)

    def start_remote(src, dst, r, there, low):
        pltpu.make_async_remote_copy(
            src_ref=src,
            dst_ref=dst,
            send_sem=all_send.at[r],
            recv_sem=all_recv.at[r],
            device_id=(there, low),
            device_id_type=MESH,
        ).start()

    def greet(there, low):
        pl.semaphore_signal(barrier, inc=1, device_id=(there, low), device_id_type=MESH)

    peers(greet)

    def each(msg, arrived, r):
        peers(lambda there, low: start_remote(msg.at[there * SP + low], arrived.at[me], r, there, low))
        arrived[me] = msg[me]

    def same(row, arrived, r):
        peers(lambda there, low: start_remote(row, arrived.at[me], r, there, low))
        arrived[me] = row[...]

    def all_arrived(arrived, r):
        part = arrived.at[pl.ds(0, D - 1)]
        remote(part, part, all_send.at[r], all_recv.at[r], right).wait_recv()

    def all_sent(arrived, r):
        part = arrived.at[pl.ds(0, D - 1)]
        remote(part, part, all_send.at[r], all_recv.at[r], right).wait_send()

    lo, hi = lax.rem(me, LO), me // LO

    def tree_one(send, one, r):
        for k in range(1, LO):
            d = hi * LO + lax.rem(lo + k, LO)
            remote(send, one.at[lo], tree_send.at[r], tree_recv.at[r], d).start()
        one[lo] = send[...]

    def tree_two(one, mid, two, r):
        part = one.at[pl.ds(0, LO - 1)]
        remote(part, part, tree_send.at[r], tree_recv.at[r], right).wait()
        mid[...] = jnp.sum(one[...], axis=0)
        for k in range(1, HI):
            d = lax.rem(hi + k, HI) * LO + lo
            remote(mid, two.at[hi], tree_send.at[r + 1], tree_recv.at[r + 1], d).start()
        two[hi] = mid[...]

    def tree_end(two, r):
        part = two.at[pl.ds(0, HI - 1)]
        remote(part, part, tree_send.at[r + 1], tree_recv.at[r + 1], right).wait()
        return jnp.sum(two[...], axis=0)

    for copy in loads[:4]:
        copy.wait()
    block = min(IF, LANES)
    before = mask(iota((block, block), 0) < iota((block, block), 1)).astype(BF16)
    ones = jnp.ones((block, block), BF16)
    carry = jnp.zeros((D, block), F32)
    for b in range(IF // block):
        cols = pl.ds(b * block, block)
        hot = mask(owner[:, cols] == iota((D, block), 0))
        owner_hot[:, cols] = hot
        hot16 = hot.astype(BF16)
        rank = jnp.sum(hot * (carry + dot(hot16, before, (1, 0))), axis=0, keepdims=True)
        carry = carry + dot(hot16, ones, (1, 0))
        slot = lax.rem(iota((LANES, block), 0), SLOTS).astype(F32)
        rank_hot[:, cols] = mask(slot == rank)
    x = x0[...]
    nrm = normal[...]
    flux = SOURCE_GAIN * jnp.sum(nrm * x[0:3], axis=0, keepdims=True)
    group = iota((LANES, IF), 0) // SLOTS
    named = (cell[...] + 1).astype(F32)
    squared = jnp.sum(nrm * nrm, axis=0, keepdims=True)
    along = jnp.sum(nrm * x[3:6], axis=0, keepdims=True)
    packed = jnp.where(group == 2, squared, jnp.where(group == 3, along, 0.0))
    packed = jnp.where(group == 0, flux, jnp.where(group == 1, named, packed))
    packed = rank_hot[...] * packed
    m_cells[:, 0, :] = dot(owner_hot[...], packed, (1, 1), True)

    pl.semaphore_wait(barrier, D - 1)
    each(m_cells, a_cells, CELLS)

    def halo(buf, e, ch):
        rows = pl.ds(ch * (NY // NCH), NY // NCH)
        inner = pl.ds(ch * (NY // NCH) + 8, NY // NCH)
        to_left = remote(
            buf.at[0, inner, :], halo_r.at[e, rows, :], halo_send.at[e, 0, ch], halo_recv.at[e, 0, ch], left
        )
        to_right = remote(
            buf.at[CX - 1, inner, :], halo_l.at[e, rows, :], halo_send.at[e, 1, ch], halo_recv.at[e, 1, ch], right
        )
        return to_left, to_right

    loads[4].wait()
    for ch in range(NCH):
        for copy in halo(pa, 0, ch):
            copy.start()

    for copy in loads[5:8]:
        copy.wait()
    for w in range(W1):
        for c in range(3):
            ws_x[1 + w, c] = ws_v[c, :, w, :]
        stiff_x[1 + w] = stiff_v[:, w, :]

    def planes(buf, width, count, r):
        return (
            remote(buf.at[pl.ds(width, width)], buf.at[pl.ds(width + count, width)], wall_send.at[r, 0], wall_recv.at[r, 0], left),
            remote(buf.at[pl.ds(count, width)], buf.at[pl.ds(0, width)], wall_send.at[r, 1], wall_recv.at[r, 1], right),
        )

    wall_static = planes(ws_x, 1, W1, 0) + planes(stiff_x, 1, W1, 1)
    for copy in wall_static:
        copy.start()

    pad = jnp.zeros((CX, 8, NZ), F32)
    for buf in (pa, pb):
        buf[:, pl.ds(0, 8), :] = pad
        buf[:, pl.ds(NY + 8, 8), :] = pad

    loads[8].wait()
    loads[9].wait()
    per_row = LANES // SLOTS

    def weights(ref, at_row, factor, first):
        u = sum(ref[at_row + c] * (factor * nrm[c : c + 1]) for c in range(3))
        for q in range(H // per_row):
            for i in range(per_row):
                a = q * per_row + i
                u_rows[i * SLOTS : (i + 1) * SLOTS, :] = rank_hot[0:SLOTS, :] * u[a : a + 1, :]
            m_weights[:, first + q, :] = dot(owner_hot[...], u_rows[...], (1, 1), True)

    weights(vres, 3, 1.0, 0)
    weights(vout, 0, SOURCE_GAIN, H // per_row)

    each(m_weights, a_weights, WEIGHTS)

    def layers(f):
        row = iota(f.shape, 1)
        up = jnp.where(row == 0, 0.0, pltpu.roll(f, 1, 1))
        down = jnp.where(row == L3 - 1, 0.0, pltpu.roll(f, L3 - 1, 1))
        return up + down + pltpu.roll(f, 1, 2) + pltpu.roll(f, S2 - 1, 2)

    def tangent(low, f, high, stiff):
        return (6.0 + stiff)[None] * f - (low + high + layers(f))

    for copy in wall_static:
        copy.wait()

    def force(x_now, dest):
        for w in range(W1):
            part = pl.ds(w * S2, S2)
            for c in range(3):
                b = base[w, c]
                t = x_now[3 + c : 4 + c, w * S2 : (w + 1) * S2]
                row = iota((L3, S2), 0)
                dest[2 + w, c] = b + jnp.where(row == 0, t, 0.0)

    for w in range(W1):
        low = ws_x[w] * (keep_l if w == 0 else 1.0)
        high = ws_x[w + 2] * (keep_r if w == W1 - 1 else 1.0)
        k_w = tangent(low, ws_x[w + 1], high, stiff_x[w + 1])
        for c in range(3):
            base[w, c] = load_v[c, :, w, :] - k_w[c]
    force(x, f1_x)
    wall_f1 = planes(f1_x, 2, W1, 2)
    for copy in wall_f1:
        copy.start()

    gram = jnp.zeros((H, H), F32)
    for c in range(6):
        v_c = vres[c]
        gram = gram + dot(v_c, v_c, (1, 1), True)
    g_send[0:8, :] = jnp.concatenate([gram[8 * q : 8 * q + 8, :] for q in range(H // 8)], axis=1)
    for copy in loads[10:]:
        copy.wait()

    def invert(i, _):
        rows = pl.ds(pl.multiple_of(i * RC, 8), RC)
        for xx in range(CX):
            weight[xx, rows, :] = OMEGA / (6.0 + weight[xx, rows, :])
        return 0

    lax.fori_loop(0, NY // RC, invert, 0)

    all_arrived(a_cells, CELLS)
    y_bits, z_bits = NY.bit_length() - 1, NZ.bit_length() - 1

    def placed(cells):
        xx = cells >> (y_bits + z_bits)
        xx = jnp.where(xx == 0, CX - 2, jnp.where((xx > 0) & (xx < CX - 1), xx - 1, xx))
        return xx * NY + jnp.bitwise_and(cells >> z_bits, NY - 1)

    got = a_cells[:, 0, :]
    found = got[:, SLOTS : 2 * SLOTS].astype(jnp.int32) - 1
    row_of = placed(found)
    zcols[:, 0:SLOTS] = jnp.bitwise_and(found, NZ - 1)
    flipped = got.T[SLOTS : 2 * SLOTS, :].astype(jnp.int32) - 1
    row_flat = placed(flipped)

    def mark(first, last):
        def one(i, _):
            y0 = pl.multiple_of(i * RC, 8)
            for j in range(SLOTS):
                hit = iota((RC, D), 0) == row_flat[j : j + 1, :] - y0
                at[pl.ds(y0, RC), j * D : (j + 1) * D] = mask(hit).astype(BF16)
            return 0

        lax.fori_loop(first // RC, last // RC, one, 0)

    mark((CX - 2) * NY, R)

    def spread(flux_now):
        for j in range(SLOTS):
            f_j = flux_now[:, j : j + 1]
            top = f_j.astype(BF16).astype(F32)
            here = zcols[:, j : j + 1] == iota((D, NZ), 1)
            f_hi[j * D : (j + 1) * D, :] = jnp.where(here, top, 0.0).astype(BF16)
            f_lo[j * D : (j + 1) * D, :] = jnp.where(here, f_j - top, 0.0).astype(BF16)

    inner_rows, edge_rows = (0, (CX - 2) * NY), ((CX - 2) * NY, 2 * NY)

    def place(which):
        rows = pl.ds(*which)
        hot = at[rows, :]
        found_here = dot(hot, f_hi[...], (1, 0)) + dot(hot, f_lo[...], (1, 0))
        total[rows, :] = rhs[rows, :] + found_here

    spread(got)
    place(edge_rows)

    def update(src, dst, xx, y0, up, down):
        ext = src[xx, pl.ds(y0, RC + 16), :]
        c = ext[8 : 8 + RC]
        beside = pltpu.roll(ext, 1, 0)[8 : 8 + RC] + pltpu.roll(ext, RC + 15, 0)[8 : 8 + RC]
        lane = iota((RC, NZ), 1)
        beside = beside + jnp.where(lane == 0, 0.0, pltpu.roll(c, 1, 1))
        beside = beside + jnp.where(lane == NZ - 1, 0.0, pltpu.roll(c, NZ - 1, 1))
        rows = pl.ds(pl.multiple_of(spot(xx) * NY + y0, 8), RC)
        new = (1.0 - OMEGA) * c + weight[xx, pl.ds(y0, RC), :] * (total[rows, :] + up + down + beside)
        dst[xx, pl.ds(pl.multiple_of(y0 + 8, 8), RC), :] = new

    chunk = NY // NCH

    def edges(e, src, dst, send, beside=()):
        for ch in range(NCH):
            for work in beside[ch] if beside else ():
                work()
            if e >= 1:
                for copy in halo(dst, e - 1, ch):
                    copy.wait_send()
            to_left, to_right = halo(src, e, ch)
            to_left.wait_recv()
            to_right.wait_recv()

            def part(i, _, ch=ch):
                y0 = pl.multiple_of(ch * chunk + i * RC, 8)
                up = halo_l[e, pl.ds(y0, RC), :] * keep_l
                down = src[1, pl.ds(pl.multiple_of(y0 + 8, 8), RC), :]
                update(src, dst, 0, y0, up, down)
                up = src[CX - 2, pl.ds(pl.multiple_of(y0 + 8, 8), RC), :]
                down = halo_r[e, pl.ds(y0, RC), :] * keep_r
                update(src, dst, CX - 1, y0, up, down)
                return 0

            lax.fori_loop(0, chunk // RC, part, 0)
            if send:
                for copy in halo(dst, e + 1, ch):
                    copy.start()

    def inside(src, dst):
        def inner(i, _):
            y0 = pl.multiple_of(i * RC, 8)
            for xx in range(1, CX - 1):
                up = src[xx - 1, pl.ds(pl.multiple_of(y0 + 8, 8), RC), :]
                down = src[xx + 1, pl.ds(pl.multiple_of(y0 + 8, 8), RC), :]
                update(src, dst, xx, y0, up, down)
            return 0

        lax.fori_loop(0, NY // RC, inner, 0)

    def moments(f_x, copies, dest, first):
        for copy in copies:
            copy.wait()
        ext = []
        for i in range(W1 + 4):
            f = f_x[i]
            ext.append(f * keep_l if i < 2 else f * keep_r if i >= W1 + 2 else f)
        image = []
        for i in range(W1 + 2):
            image.append(tangent(ext[i], ext[i + 1], ext[i + 2], stiff_x[i]))
        image[0] = image[0] * keep_l
        image[-1] = image[-1] * keep_r
        sums = [jnp.zeros((L3, S2), F32) for _ in range(4)]
        for w in range(W1):
            f, k1 = ext[w + 2], image[w + 1]
            k2 = tangent(image[w], k1, image[w + 2], stiff_x[w + 1])
            kf[w] = k1
            for n, (one, two) in enumerate(((f, f), (f, k1), (k1, k1), (k1, k2))):
                sums[n] = sums[n] + jnp.sum(one * two, axis=0)
        for n in range(4):
            s = jnp.sum(sums[n], axis=0, keepdims=True)
            width = min(S2, LANES)
            s = sum(s[:, i * width : (i + 1) * width] for i in range(S2 // width))
            dest[first + n : first + n + 1, 0:width] = s

    def wall_update(f_x, rows):
        width = min(S2, LANES)
        m0, m1, m2, m3 = (jnp.sum(rows[n : n + 1, 0:width], axis=1, keepdims=True) for n in range(4))
        alpha0 = m0 / m1
        left_over = m0 - 2.0 * alpha0 * m1 + alpha0 * alpha0 * m2
        grow = 1.0 + left_over / m0
        alpha1 = left_over / (grow * grow * m1 - 2.0 * grow * alpha0 * m2 + alpha0 * alpha0 * m3)
        on_f, on_k = alpha0 + alpha1 * grow, alpha1 * alpha0
        new = []
        for w in range(W1):
            new.append(ws_x[w + 1] + on_f[None] * f_x[w + 2] - on_k[None] * kf[w])
        rows_out = [
            jnp.concatenate([new[w][c, 0:1, :] for w in range(W1)], axis=1) for c in range(3)
        ]
        return new, jnp.concatenate(rows_out, axis=0)

    def cut_planes(planes_of):
        def cut(i, _):
            for xx in planes_of:
                v = pa[xx, pl.ds(pl.multiple_of(i * RC + 8, 8), RC), :]
                top = v.astype(BF16)
                rows = pl.ds(pl.multiple_of(spot(xx) * NY + i * RC, 8), RC)
                p_hi[rows, :] = top
                p_lo[rows, :] = (v - top.astype(F32)).astype(BF16)
            return 0

        lax.fori_loop(0, NY // RC, cut, 0)

    def sample(which, slots, out):
        lane = lax.rem(iota((D, LANES), 1), SLOTS)
        first, count = which
        rows = pl.ds(first, count)
        for j in range(*slots, 2):
            hot = a_mat[j * D : (j + 2) * D, first : first + count]
            got_rows = dot(hot, p_hi[rows, :], (1, 0)) + dot(hot, p_lo[rows, :], (1, 0))
            for i in range(2):
                here = zcols[:, j + i : j + i + 1] == iota((D, NZ), 1)
                part = got_rows[i * D : (i + 1) * D]
                col = jnp.sum(jnp.where(here, part, 0.0), axis=1, keepdims=True)
                out = jnp.where(lane == j + i, col, out)
        return out

    mid = tuple(range(1, CX - 1))
    ends = (0, CX - 1)

    def unpack(arrived):
        rows = dot(arrived[:, 0, 0:SLOTS], owner_hot[...], (0, 0), True)
        return jnp.sum(rows * rank_hot[pl.ds(0, SLOTS), :], axis=0, keepdims=True)

    def against(v):
        acc = sum(vres[c] * v[c : c + 1] for c in range(6))
        return jnp.sum(acc, axis=1, keepdims=True)

    def combine(coef, first):
        rows = [jnp.sum(coef * vout[c], axis=0, keepdims=True) for c in range(6)]
        return first + jnp.concatenate(rows, axis=0)

    def as_row(col):
        return jnp.sum(jnp.where(iota((H, LANES), 0) == iota((H, LANES), 1), col, 0.0), axis=0, keepdims=True)

    def as_col(row):
        return jnp.sum(jnp.where(iota((H, LANES), 0) == iota((H, LANES), 1), row, 0.0), axis=1, keepdims=True)

    box = {}
    none = jnp.zeros((D, LANES), F32)
    half = SLOTS // 2

    def wall_first():
        moments(f1_x, wall_f1, g_send, 8)
        tree_one(g_send, g_one, 0)

    def hot_rows(first, last):
        def work():
            for j in range(first, last):
                a_mat[j * D : (j + 1) * D, :] = mask(row_of[:, j : j + 1] == iota((D, R), 1)).astype(BF16)

        return work

    def solid_first():
        g_all = tree_end(g_two, 0)
        box["gram"] = jnp.concatenate(
            [
                g_all[0:8, :] if q == 0 else pltpu.roll(g_all[0:8, :], LANES - H * q, 1)
                for q in range(H // 8)
            ],
            axis=0,
        )
        _, solid = wall_update(f1_x, g_all[8:16, :])
        box["solid"] = solid
        flux = SOURCE_GAIN * jnp.sum(nrm * solid, axis=0, keepdims=True)
        m_solid[:, 0, :] = dot(owner_hot[...], rank_hot[...] * flux, (1, 1), True)

    def solid_sent():
        each(m_solid, a_solid, SOLID)
        known = jnp.concatenate([box["solid"] - x[0:3], -x[3:6]], axis=0)
        box["h_known"] = against(known)

    def sampled(name, first, last, cut):
        def work():
            if cut:
                cut_planes(mid)
            box[name] = sample(inner_rows, (first, last), box.get(name, none))

        return work

    edges(0, pa, pb, True)
    edges(
        1,
        pb,
        pa,
        True,
        (
            (wall_first, lambda: mark(0, (CX - 2) * NY), lambda: place(inner_rows), lambda: inside(pa, pb)),
            (hot_rows(0, half),),
            (hot_rows(half, SLOTS),),
            (lambda: tree_two(g_one, g_mid, g_two, 0),),
        ),
    )
    edges(2, pa, pb, True, ((lambda: inside(pb, pa),), (), (solid_first,), (solid_sent,)))
    edges(
        3,
        pb,
        pa,
        True,
        (
            (lambda: inside(pa, pb),),
            (lambda: inside(pb, pa),),
            (sampled("seen1", 0, half, True),),
            (sampled("seen1", half, SLOTS, False), lambda: all_arrived(a_weights, WEIGHTS)),
        ),
    )
    gram, solid1, h_known = box["gram"], box["solid"], box["h_known"]
    cut_planes(ends)
    seen1 = sample(edge_rows, (0, SLOTS), none) + box["seen1"]
    mine = iota((H, LANES), 1) // SLOTS == lax.rem(iota((H, LANES), 0), per_row)

    def owned(values):
        rows = [
            jnp.sum(a_weights[:, q, :] * values, axis=0, keepdims=True) for q in range(H // per_row)
        ]
        rows = jnp.concatenate([jnp.broadcast_to(f, (per_row, LANES)) for f in rows], axis=0)
        return jnp.sum(jnp.where(mine, rows, 0.0), axis=1, keepdims=True)

    m_first[...] = as_row(h_known - owned(seen1))
    same(m_first, a_first, FIRST)
    m_back[:, 0, :] = seen1
    each(m_back, a_back, BACK)
    square = iota((H, LANES), 0) == iota((H, LANES), 1)
    gram = jnp.where(iota((H, LANES), 1) < H, gram, 0.0)
    on_diag = jnp.where(square, gram, 0.0)
    trace = jnp.sum(jnp.sum(on_diag, axis=1, keepdims=True), axis=0, keepdims=True)
    ridge = RIDGE * trace / H + TINY
    beside = mask(iota((H, LANES), 1) == iota((H, LANES), 0) + H)
    inverse = eliminate(gram + jnp.where(square, ridge, 0.0) + beside, H)
    inverse = jnp.where(iota((H, LANES), 1) < H, pltpu.roll(inverse, LANES - H, 1), 0.0)
    all_arrived(a_solid, SOLID)
    all_arrived(a_first, FIRST)
    h_row = jnp.sum(a_first[...], axis=0)
    coeffs = -jnp.sum(inverse * h_row, axis=1, keepdims=True)
    extra = jnp.zeros((D, LANES), F32)
    for q in range(H // per_row):
        pick = iota((H, LANES), 0) == q * per_row + iota((H, LANES), 1) // SLOTS
        c_row = jnp.sum(jnp.where(pick, coeffs, 0.0), axis=0, keepdims=True)
        extra = extra + a_weights[:, H // per_row + q, :] * c_row
    step = LANES // 2
    while step >= SLOTS:
        extra = extra + pltpu.roll(extra, step, 1)
        step //= 2
    spread(a_solid[:, 0, :] + extra)
    place(edge_rows)

    def back_first():
        all_arrived(a_back, BACK)
        out1 = jnp.concatenate([solid1, -unpack(a_back) * nrm], axis=0)
        x2 = combine(coeffs, out1)
        force(x2, f2_x)
        for copy in planes(f2_x, 2, W1, 3):
            copy.start()
        box.update(out1=out1, x2=x2, res1=out1 - x)

    def moved_along():
        moved = box["x2"][3:6] - x[3:6]
        step_along = jnp.sum(nrm * moved, axis=0, keepdims=True)
        m_moved[:, 0, :] = dot(owner_hot[...], rank_hot[...] * step_along, (1, 1), True)
        box["moved"] = moved

    def wall_second():
        moments(f2_x, planes(f2_x, 2, W1, 3), q_send, 0)
        tree_one(q_send, q_one, 2)

    def shift():
        shifted = pltpu.roll(pltpu.roll(gram, 1, 0), 1, 1)
        low = (iota((H, LANES), 0) > 0) & (iota((H, LANES), 1) > 0) & (iota((H, LANES), 1) < H)
        box["shifted"] = jnp.where(low, shifted, 0.0)
        box["trace"] = trace - gram[H - 1 : H, H - 1 : H]

    def solid_second():
        new, solid2 = wall_update(f2_x, tree_end(q_two, 2))
        for w in range(W1):
            for c in range(3):
                wall_out[c, :, w, :] = new[w][c]
        res1 = box["res1"]
        known = jnp.concatenate([solid2 - box["x2"][0:3] - res1[0:3], -box["moved"]], axis=0)
        box["solid2"] = solid2
        box["cross"] = against(known)
        box["own"] = jnp.sum(jnp.sum(known * known, axis=1, keepdims=True), axis=0, keepdims=True)
        box["old"] = jnp.sum(jnp.sum(known * res1, axis=1, keepdims=True), axis=0, keepdims=True)

    edges(4, pa, pb, True)
    edges(
        5,
        pb,
        pa,
        True,
        (
            (back_first, lambda: place(inner_rows), lambda: inside(pa, pb)),
            (moved_along,),
            (wall_second,),
            (lambda: each(m_moved, a_moved, MOVED),),
        ),
    )
    edges(
        6,
        pa,
        pb,
        True,
        ((lambda: inside(pb, pa),), (shift,), (lambda: tree_two(q_one, q_mid, q_two, 2),), ()),
    )
    edges(
        7,
        pb,
        pa,
        False,
        (
            (lambda: inside(pa, pb),),
            (lambda: inside(pb, pa),),
            (sampled("seen2", 0, half, True),),
            (sampled("seen2", half, SLOTS, False), solid_second),
        ),
    )
    out1, shifted, trace, solid2 = box["out1"], box["shifted"], box["trace"], box["solid2"]
    cross_known, own_known, old_known = box["cross"], box["own"], box["old"]
    save = pltpu.make_async_copy(pa.at[:, pl.ds(8, NY), :], p_out, out_sem)
    save.start()
    all_arrived(a_moved, MOVED)
    cut_planes(ends)
    seen2 = sample(edge_rows, (0, SLOTS), none) + box["seen2"]
    gained = seen2 - seen1
    cells_msg = a_cells[:, 0, :]
    n_n = pltpu.roll(cells_msg, LANES - 2 * SLOTS, 1)
    n_t = pltpu.roll(cells_msg, LANES - 3 * SLOTS, 1)
    single = iota((D, LANES), 1) < SLOTS
    own = jnp.where(single, gained * (gained * n_n + 2.0 * a_moved[:, 0, :]), 0.0)
    old = jnp.where(single, gained * (seen1 * n_n + n_t), 0.0)
    own = own_known + jnp.sum(jnp.sum(own, axis=0, keepdims=True), axis=1, keepdims=True)
    old = old_known + jnp.sum(jnp.sum(old, axis=0, keepdims=True), axis=1, keepdims=True)
    lane = iota((1, LANES), 1)
    cross = as_row(cross_known - owned(gained))
    m_last[...] = jnp.where(lane == H, own, jnp.where(lane == H + 1, old, cross))
    same(m_last, a_last, LAST)
    m_back2[:, 0, :] = seen2
    each(m_back2, a_back2, BACK2)
    all_arrived(a_last, LAST)
    last = jnp.sum(a_last[...], axis=0)
    own, old = last[:, H : H + 1], last[:, H + 1 : H + 2]
    cross = jnp.where((lane > 0) & (lane < H), pltpu.roll(last, 1, 1), jnp.where(lane == 0, own, 0.0))
    h_row = pltpu.roll(jnp.where(lane < H, h_row, 0.0), 1, 1)
    h_row = jnp.where(lane == 0, own + old, h_row + cross)
    lanes = iota((H, LANES), 1)
    first = iota((H, LANES), 0) == 0
    gram = jnp.where(first, cross, jnp.where(lanes == 0, as_col(cross), shifted))
    ridge = RIDGE * (trace + own) / H + TINY
    gram = gram + jnp.where(square, ridge, 0.0)
    gram = jnp.where(lanes == H, as_col(h_row), gram)
    coeffs = -eliminate(gram, H)[:, H : H + 1]
    rest = pltpu.roll(coeffs * jnp.ones((H, LANES), F32), H - 1, 0)[:, 0:1]
    rest = jnp.where(iota((H, 1), 0) < H - 1, rest, 0.0)
    state = combine(rest, jnp.zeros((6, IF), F32))
    all_arrived(a_back2, BACK2)
    out2 = jnp.concatenate([solid2, -unpack(a_back2) * nrm], axis=0)
    state_out[...] = out2 + coeffs[0:1, :] * (out2 - out1) + state

    for arrived, r in (
        (a_cells, CELLS),
        (a_weights, WEIGHTS),
        (a_solid, SOLID),
        (a_first, FIRST),
        (a_back, BACK),
        (a_moved, MOVED),
        (a_back2, BACK2),
        (a_last, LAST),
    ):
        all_sent(arrived, r)
    for ch in range(NCH):
        for copy in halo(pb, SWEEPS * COUPLE - 1, ch):
            copy.wait_send()
    save.wait()


def finish(*refs):
    sources, targets, stages, sem = refs[:3], refs[3:6], refs[6:9], refs[9]
    triples = []
    for source, stage, target in zip(sources, stages, targets, strict=True):
        if len(source.shape) == 3:
            triples += [(source.at[i], stage.at[i], target.at[i]) for i in range(source.shape[0])]
        else:
            triples.append((source, stage, target))
    come = [pltpu.make_async_copy(a, b, sem.at[0, i]) for i, (a, b, _) in enumerate(triples)]
    leave = [pltpu.make_async_copy(b, c, sem.at[1, i]) for i, (_, b, c) in enumerate(triples)]
    for copy in come:
        copy.start()
    for a, b in zip(come, leave, strict=True):
        a.wait()
        b.start()
    for copy in leave:
        copy.wait()


def local(cfg, *args):
    (D, SP, LO, CX, NY, NZ, L3, W1, S2, IF, H, NCH, RC) = cfg
    (p, coef, rhs, ws, stiff, load, normals, owner, cell, x, vres, vout) = args
    vres, vout = vres.transpose(1, 0, 2), vout.transpose(1, 0, 2)
    R, K = CX * NY, SLOTS * D
    EX = SWEEPS * COUPLE
    wide = LANES
    G = 16

    def vmem(*shape, dtype=F32):
        return pltpu.VMEM(shape, dtype)

    dma = pltpu.SemaphoreType.DMA
    scratch = [
        vmem(CX, NY + 16, NZ), vmem(CX, NY + 16, NZ), vmem(CX, NY, NZ), vmem(R, NZ), vmem(R, NZ),
        vmem(EX, NY, NZ), vmem(EX, NY, NZ),
        vmem(R, K, dtype=BF16), vmem(K, R, dtype=BF16), vmem(K, NZ, dtype=BF16), vmem(K, NZ, dtype=BF16),
        vmem(R, NZ, dtype=BF16), vmem(R, NZ, dtype=BF16),
        vmem(3, L3, W1, S2), vmem(L3, W1, S2), vmem(3, L3, W1, S2),
        vmem(3, IF), vmem(1, IF, dtype=jnp.int32), vmem(1, IF, dtype=jnp.int32), vmem(6, IF),
        vmem(6, H, IF), vmem(6, H, IF),
        vmem(D, IF), vmem(LANES, IF),
        vmem(D, 1, wide), vmem(D, 1, wide), vmem(D, 8, wide), vmem(D, 8, wide),
        vmem(D, 1, wide), vmem(D, 1, wide), vmem(D, 1, wide), vmem(D, 1, wide), vmem(D, 1, wide), vmem(D, 1, wide),
        vmem(D, 1, wide), vmem(D, 1, wide),
        vmem(1, wide), vmem(D, 1, wide), vmem(1, wide), vmem(D, 1, wide),
        vmem(W1 + 2, 3, L3, S2), vmem(W1 + 2, L3, S2), vmem(W1 + 4, 3, L3, S2), vmem(W1 + 4, 3, L3, S2),
        vmem(W1, 3, L3, S2), vmem(W1, 3, L3, S2),
        vmem(G, wide), vmem(LO, G, wide), vmem(G, wide), vmem(D // LO, G, wide),
        vmem(8, wide), vmem(LO, 8, wide), vmem(8, wide), vmem(D // LO, 8, wide),
        vmem(LANES, IF), vmem(D, SLOTS, dtype=jnp.int32),
        dma((11 + CX,)), dma((ROUNDS,)), dma((ROUNDS,)), dma((EX, 2, NCH)), dma((EX, 2, NCH)),
        dma((4, 2)), dma((4, 2)), dma((4,)), dma((4,)), dma(()),
    ]
    anywhere = pl.BlockSpec(memory_space=pl.ANY)
    inside = pl.BlockSpec(memory_space=pltpu.VMEM)
    shapes = (
        jax.ShapeDtypeStruct((6, IF), F32),
        jax.ShapeDtypeStruct((CX, NY, NZ), F32),
        jax.ShapeDtypeStruct((3, L3, W1, S2), F32),
    )
    results = pl.pallas_call(
        functools.partial(kernel, cfg),
        out_shape=shapes,
        in_specs=[anywhere] * 12,
        out_specs=(inside, anywhere, inside),
        scratch_shapes=scratch,
        compiler_params=pltpu.CompilerParams(
            collective_id=0, has_side_effects=True, vmem_limit_bytes=60 * 2**20
        ),
    )(
        p, coef, rhs.reshape(R, NZ), ws, stiff, load, normals,
        owner.reshape(1, IF), cell.reshape(1, IF), x, vres, vout,
    )
    return pl.pallas_call(
        finish,
        out_shape=shapes,
        in_specs=[anywhere] * 3,
        out_specs=(anywhere,) * 3,
        scratch_shapes=[vmem(6, IF), vmem(CX, NY, NZ), vmem(3, L3, W1, S2), dma((2, CX + 2))],
    )(*results)


def solution(mesh):
    sp = mesh.shape["space"]
    devices = mesh.shape["solver"] * sp

    def run(*args):
        CX, NY, NZ = args[0].shape
        _, L3, W1, S2 = args[3].shape
        IF, H = args[8].shape[0], args[10].shape[0]
        lo = 8 if devices > 8 else 4
        cfg = (devices, sp, lo, CX, NY, NZ, L3, W1, S2, IF, H, 4, min(32, NY // 4))
        return local(cfg, *args)

    in_specs = (
        P(BOTH, None, None),
        P(BOTH, None, None),
        P(BOTH, None, None),
        P(None, None, BOTH, None),
        P(None, BOTH, None),
        P(None, None, BOTH, None),
        P(None, BOTH),
        P(BOTH, None),
        P(BOTH),
        P(None, BOTH),
        P(None, None, BOTH),
        P(None, None, BOTH),
    )
    out_specs = (P(None, BOTH), P(BOTH, None, None), P(None, None, BOTH, None))
    return jax.shard_map(run, mesh=mesh, in_specs=in_specs, out_specs=out_specs, check_vma=False)
```

```python
import functools

import jax
import jax.numpy as jnp
from jax import lax
from jax.experimental import pallas as pl
from jax.experimental.pallas import tpu as pltpu
from jax.sharding import PartitionSpec as P

SWEEPS = 4
COUPLE = 2
OMEGA = 0.8
SOURCE_GAIN = 4.0
RIDGE = 0.1
TINY = 1e-06
SLOTS = 16
LANES = 128
MESH = pl.DeviceIdType.MESH
F32 = jnp.float32
BF16 = jnp.bfloat16
BOTH = ("solver", "space")
CELLS, WEIGHTS, SOLID, FIRST, BACK, MOVED, BACK2, LAST, WALL1, WALL2 = range(10)
ROUNDS = 10


def iota(shape, dim):
    return lax.broadcasted_iota(jnp.int32, shape, dim)


def dot(a, b, contract, exact=False):
    return lax.dot_general(
        a,
        b,
        (((contract[0],), (contract[1],)), ((), ())),
        precision=lax.Precision.HIGHEST if exact else None,
        preferred_element_type=F32,
    )


def mask(flag):
    return jnp.where(flag, 1.0, 0.0).astype(F32)


def eliminate(m, size):
    row = iota(m.shape, 0)
    for k in range(size):
        pivot_row = m[k : k + 1, :] / m[k : k + 1, k : k + 1]
        m = jnp.where(row == k, pivot_row, m - m[:, k : k + 1] * pivot_row)
    return m


def kernel(cfg, *refs):
    (D, SP, LO, CX, NY, NZ, L3, W1, S2, IF, H, NCH, RC) = cfg
    HI = D // LO
    R, K = CX * NY, SLOTS * D
    (
        p_hbm, coef_hbm, rhs_hbm, ws_hbm, stiff_hbm, load_hbm, normal_hbm, owner_hbm, cell_hbm, x_hbm, v_hbm, w_hbm,
        state_out, p_out, wall_out,
        pa, pb, weight, rhs, total, halo_l, halo_r, at, a_mat, f_hi, f_lo, p_hi, p_lo,
        ws_v, stiff_v, load_v, normal, owner, cell, x0, vres, vout,
        owner_hot, rank_hot,
        m_cells, a_cells, m_weights, a_weights, m_solid, a_solid, m_back, a_back, m_back2, a_back2, m_moved, a_moved,
        m_first, a_first, m_last, a_last,
        ws_x, stiff_x, f1_x, f2_x, kf, base,
        g_send, g_one, g_mid, g_two, m_wall1, a_wall1, m_wall2, a_wall2,
        u_rows, zcols,
        load_sem, all_send, all_recv, halo_send, halo_recv, wall_send, wall_recv, tree_send, tree_recv, out_sem,
    ) = refs
    me = lax.axis_index("solver") * SP + lax.axis_index("space")
    left, right = lax.rem(me + D - 1, D), lax.rem(me + 1, D)
    keep_l = jnp.where(me > 0, 1.0, 0.0).astype(F32)
    keep_r = jnp.where(me < D - 1, 1.0, 0.0).astype(F32)

    def at_device(d):
        return (d // SP, lax.rem(d, SP))

    def remote(src, dst, send, recv, d):
        return pltpu.make_async_remote_copy(
            src_ref=src,
            dst_ref=dst,
            send_sem=send,
            recv_sem=recv,
            device_id=at_device(d),
            device_id_type=MESH,
        )

    half_y = NY // 2
    edge_at = (CX - 2) * NY

    def offset(xx, part):
        if 0 < xx < CX - 1:
            return (xx - 1) * NY
        return edge_at + part * half_y + (half_y if xx else 0)

    loads = [
        pltpu.make_async_copy(src, dst, load_sem.at[i])
        for i, (src, dst) in enumerate(
            (
                (owner_hbm, owner),
                (cell_hbm, cell),
                (normal_hbm, normal),
                (x_hbm, x0),
                (p_hbm, pa.at[:, pl.ds(8, NY), :]),
                (ws_hbm, ws_v),
                (stiff_hbm, stiff_v),
                (load_hbm, load_v),
                (v_hbm, vres),
                (w_hbm, vout),
                (coef_hbm, weight),
            )
            + tuple(
                (
                    rhs_hbm.at[pl.ds(xx * NY + part * half_y, half_y), :],
                    rhs.at[pl.ds(offset(xx, part) + part * half_y, half_y), :],
                )
                for xx in range(CX)
                for part in range(2)
            )
        )
    ]
    for copy in loads:
        copy.start()
    barrier = pltpu.get_barrier_semaphore()

    NS = D // SP
    my_s, my_p = me // SP, lax.rem(me, SP)

    def peers(act):
        for ds in sorted(range(NS), key=lambda q: -min(q, NS - q)):
            there = lax.rem(my_s + ds, NS)

            def one(k, _):
                act(there, lax.rem(my_p + SP // 2 + k, SP))
                return 0

            if ds:
                lax.fori_loop(0, SP, one, 0, unroll=4)
            else:
                lax.fori_loop(0, SP // 2, one, 0, unroll=4 if SP >= 8 else 1)
                lax.fori_loop(SP // 2 + 1, SP, one, 0, unroll=3 if SP >= 8 else 1)

    def start_remote(src, dst, r, there, low):
        pltpu.make_async_remote_copy(
            src_ref=src,
            dst_ref=dst,
            send_sem=all_send.at[r],
            recv_sem=all_recv.at[r],
            device_id=(there, low),
            device_id_type=MESH,
        ).start()

    def greet(there, low):
        pl.semaphore_signal(barrier, inc=1, device_id=(there, low), device_id_type=MESH)

    peers(greet)

    def each(msg, arrived, r):
        peers(lambda there, low: start_remote(msg.at[there * SP + low], arrived.at[me], r, there, low))
        arrived[me] = msg[me]

    def same(row, arrived, r):
        peers(lambda there, low: start_remote(row, arrived.at[me], r, there, low))
        arrived[me] = row[...]

    def all_arrived(arrived, r):
        part = arrived.at[pl.ds(0, D - 1)]
        remote(part, part, all_send.at[r], all_recv.at[r], right).wait_recv()

    def all_sent(arrived, r):
        part = arrived.at[pl.ds(0, D - 1)]
        remote(part, part, all_send.at[r], all_recv.at[r], right).wait_send()

    lo, hi = lax.rem(me, LO), me // LO

    def tree_one(send, one, r):
        for k in range(1, LO):
            d = hi * LO + lax.rem(lo + k, LO)
            remote(send, one.at[lo], tree_send.at[r], tree_recv.at[r], d).start()
        one[lo] = send[...]

    def tree_two(one, mid, two, r):
        part = one.at[pl.ds(0, LO - 1)]
        remote(part, part, tree_send.at[r], tree_recv.at[r], right).wait()
        mid[...] = jnp.sum(one[...], axis=0)
        for k in range(1, HI):
            d = lax.rem(hi + k, HI) * LO + lo
            remote(mid, two.at[hi], tree_send.at[r + 1], tree_recv.at[r + 1], d).start()
        two[hi] = mid[...]

    def tree_end(two, r):
        part = two.at[pl.ds(0, HI - 1)]
        remote(part, part, tree_send.at[r + 1], tree_recv.at[r + 1], right).wait()
        return jnp.sum(two[...], axis=0)

    for copy in loads[:4]:
        copy.wait()
    block = min(IF, LANES)
    before = mask(iota((block, block), 0) < iota((block, block), 1)).astype(BF16)
    ones = jnp.ones((block, block), BF16)
    carry = jnp.zeros((D, block), F32)
    for b in range(IF // block):
        cols = pl.ds(b * block, block)
        hot = mask(owner[:, cols] == iota((D, block), 0))
        owner_hot[:, cols] = hot
        hot16 = hot.astype(BF16)
        rank = jnp.sum(hot * (carry + dot(hot16, before, (1, 0))), axis=0, keepdims=True)
        carry = carry + dot(hot16, ones, (1, 0))
        slot = lax.rem(iota((LANES, block), 0), SLOTS).astype(F32)
        rank_hot[:, cols] = mask(slot == rank)
    x = x0[...]
    nrm = normal[...]
    flux = SOURCE_GAIN * jnp.sum(nrm * x[0:3], axis=0, keepdims=True)
    group = iota((LANES, IF), 0) // SLOTS
    named = (cell[...] + 1).astype(F32)
    squared = jnp.sum(nrm * nrm, axis=0, keepdims=True)
    along = jnp.sum(nrm * x[3:6], axis=0, keepdims=True)
    packed = jnp.where(group == 2, squared, jnp.where(group == 3, along, 0.0))
    packed = jnp.where(group == 0, flux, jnp.where(group == 1, named, packed))
    packed = rank_hot[...] * packed
    m_cells[:, 0, :] = dot(owner_hot[...], packed, (1, 1), True)

    pl.semaphore_wait(barrier, D - 1)
    each(m_cells, a_cells, CELLS)

    def halo(buf, e, ch):
        rows = pl.ds(ch * (NY // NCH), NY // NCH)
        inner = pl.ds(ch * (NY // NCH) + 8, NY // NCH)
        to_left = remote(
            buf.at[0, inner, :], halo_r.at[e, rows, :], halo_send.at[e, 0, ch], halo_recv.at[e, 0, ch], left
        )
        to_right = remote(
            buf.at[CX - 1, inner, :], halo_l.at[e, rows, :], halo_send.at[e, 1, ch], halo_recv.at[e, 1, ch], right
        )
        return to_left, to_right

    loads[4].wait()
    for ch in range(NCH):
        for copy in halo(pa, 0, ch):
            copy.start()

    for copy in loads[5:8]:
        copy.wait()
    for w in range(W1):
        for c in range(3):
            ws_x[1 + w, c] = ws_v[c, :, w, :]
        stiff_x[1 + w] = stiff_v[:, w, :]

    def planes(buf, width, count, r):
        return (
            remote(buf.at[pl.ds(width, width)], buf.at[pl.ds(width + count, width)], wall_send.at[r, 0], wall_recv.at[r, 0], left),
            remote(buf.at[pl.ds(count, width)], buf.at[pl.ds(0, width)], wall_send.at[r, 1], wall_recv.at[r, 1], right),
        )

    wall_static = planes(ws_x, 1, W1, 0) + planes(stiff_x, 1, W1, 1)
    for copy in wall_static:
        copy.start()

    pad = jnp.zeros((CX, 8, NZ), F32)
    for buf in (pa, pb):
        buf[:, pl.ds(0, 8), :] = pad
        buf[:, pl.ds(NY + 8, 8), :] = pad

    loads[8].wait()
    loads[9].wait()
    per_row = LANES // SLOTS

    def weights(ref, at_row, factor, first):
        u = sum(ref[at_row + c] * (factor * nrm[c : c + 1]) for c in range(3))
        for q in range(H // per_row):
            for i in range(per_row):
                a = q * per_row + i
                u_rows[i * SLOTS : (i + 1) * SLOTS, :] = rank_hot[0:SLOTS, :] * u[a : a + 1, :]
            m_weights[:, first + q, :] = dot(owner_hot[...], u_rows[...], (1, 1), True)

    weights(vres, 3, 1.0, 0)
    weights(vout, 0, SOURCE_GAIN, H // per_row)

    each(m_weights, a_weights, WEIGHTS)

    def layers(f):
        row = iota(f.shape, 1)
        up = jnp.where(row == 0, 0.0, pltpu.roll(f, 1, 1))
        down = jnp.where(row == L3 - 1, 0.0, pltpu.roll(f, L3 - 1, 1))
        return up + down + pltpu.roll(f, 1, 2) + pltpu.roll(f, S2 - 1, 2)

    def tangent(low, f, high, stiff):
        return (6.0 + stiff)[None] * f - (low + high + layers(f))

    for copy in wall_static:
        copy.wait()

    def force(x_now, dest):
        for w in range(W1):
            part = pl.ds(w * S2, S2)
            for c in range(3):
                b = base[w, c]
                t = x_now[3 + c : 4 + c, w * S2 : (w + 1) * S2]
                row = iota((L3, S2), 0)
                dest[2 + w, c] = b + jnp.where(row == 0, t, 0.0)

    for w in range(W1):
        low = ws_x[w] * (keep_l if w == 0 else 1.0)
        high = ws_x[w + 2] * (keep_r if w == W1 - 1 else 1.0)
        k_w = tangent(low, ws_x[w + 1], high, stiff_x[w + 1])
        for c in range(3):
            base[w, c] = load_v[c, :, w, :] - k_w[c]
    force(x, f1_x)
    wall_f1 = planes(f1_x, 2, W1, 2)
    for copy in wall_f1:
        copy.start()

    gram = jnp.zeros((H, H), F32)
    for c in range(6):
        v_c = vres[c]
        gram = gram + dot(v_c, v_c, (1, 1), True)
    g_send[0:8, :] = jnp.concatenate([gram[8 * q : 8 * q + 8, :] for q in range(H // 8)], axis=1)
    tree_one(g_send, g_one, 0)
    for copy in loads[10:]:
        copy.wait()

    def invert(i, _):
        rows = pl.ds(pl.multiple_of(i * RC, 8), RC)
        for xx in range(CX):
            weight[xx, rows, :] = OMEGA / (6.0 + weight[xx, rows, :])
        return 0

    lax.fori_loop(0, NY // RC, invert, 0)

    all_arrived(a_cells, CELLS)
    y_bits, z_bits = NY.bit_length() - 1, NZ.bit_length() - 1

    def placed(cells):
        xx = cells >> (y_bits + z_bits)
        y = jnp.bitwise_and(cells >> z_bits, NY - 1)
        part = y >> (y_bits - 1)
        on_edge = edge_at + part * half_y + y + jnp.where(xx == 0, 0, half_y)
        inner = (xx > 0) & (xx < CX - 1)
        return jnp.where(inner, (xx - 1) * NY + y, jnp.where(xx < 0, -1, on_edge))

    got = a_cells[:, 0, :]
    found = got[:, SLOTS : 2 * SLOTS].astype(jnp.int32) - 1
    row_of = placed(found)
    zcols[:, 0:SLOTS] = jnp.bitwise_and(found, NZ - 1)
    flipped = got.T[SLOTS : 2 * SLOTS, :].astype(jnp.int32) - 1
    row_flat = placed(flipped)

    def mark(first, last):
        def one(i, _):
            y0 = pl.multiple_of(i * RC, 8)
            for j in range(SLOTS):
                hit = iota((RC, D), 0) == row_flat[j : j + 1, :] - y0
                at[pl.ds(y0, RC), j * D : (j + 1) * D] = mask(hit).astype(BF16)
            return 0

        lax.fori_loop(first // RC, last // RC, one, 0)

    mark(edge_at, edge_at + NY)

    def spread(flux_now):
        for j in range(SLOTS):
            f_j = flux_now[:, j : j + 1]
            top = f_j.astype(BF16).astype(F32)
            here = zcols[:, j : j + 1] == iota((D, NZ), 1)
            f_hi[j * D : (j + 1) * D, :] = jnp.where(here, top, 0.0).astype(BF16)
            f_lo[j * D : (j + 1) * D, :] = jnp.where(here, f_j - top, 0.0).astype(BF16)

    inner_rows, edge_rows = (0, edge_at), (edge_at, 2 * NY)
    edge_half = ((edge_at, NY), (edge_at + NY, NY))

    def place(which):
        rows = pl.ds(*which)
        hot = at[rows, :]
        found_here = dot(hot, f_hi[...], (1, 0)) + dot(hot, f_lo[...], (1, 0))
        total[rows, :] = rhs[rows, :] + found_here

    spread(got)

    def update(src, dst, xx, part, y0, up, down):
        ext = src[xx, pl.ds(y0, RC + 16), :]
        c = ext[8 : 8 + RC]
        beside = pltpu.roll(ext, 1, 0)[8 : 8 + RC] + pltpu.roll(ext, RC + 15, 0)[8 : 8 + RC]
        lane = iota((RC, NZ), 1)
        beside = beside + jnp.where(lane == 0, 0.0, pltpu.roll(c, 1, 1))
        beside = beside + jnp.where(lane == NZ - 1, 0.0, pltpu.roll(c, NZ - 1, 1))
        rows = pl.ds(pl.multiple_of(offset(xx, part) + y0, 8), RC)
        new = (1.0 - OMEGA) * c + weight[xx, pl.ds(y0, RC), :] * (total[rows, :] + up + down + beside)
        dst[xx, pl.ds(pl.multiple_of(y0 + 8, 8), RC), :] = new

    chunk = NY // NCH

    def edges(e, src, dst, send, beside=()):
        for ch in range(NCH):
            for work in beside[ch] if beside else ():
                work()
            if e >= 1:
                for copy in halo(dst, e - 1, ch):
                    copy.wait_send()
            to_left, to_right = halo(src, e, ch)
            to_left.wait_recv()
            to_right.wait_recv()

            def part(i, _, ch=ch):
                y0 = pl.multiple_of(ch * chunk + i * RC, 8)
                up = halo_l[e, pl.ds(y0, RC), :] * keep_l
                down = src[1, pl.ds(pl.multiple_of(y0 + 8, 8), RC), :]
                update(src, dst, 0, ch * chunk // half_y, y0, up, down)
                up = src[CX - 2, pl.ds(pl.multiple_of(y0 + 8, 8), RC), :]
                down = halo_r[e, pl.ds(y0, RC), :] * keep_r
                update(src, dst, CX - 1, ch * chunk // half_y, y0, up, down)
                return 0

            lax.fori_loop(0, chunk // RC, part, 0)
            if send:
                for copy in halo(dst, e + 1, ch):
                    copy.start()

    def inside(src, dst):
        def inner(i, _):
            y0 = pl.multiple_of(i * RC, 8)
            for xx in range(1, CX - 1):
                up = src[xx - 1, pl.ds(pl.multiple_of(y0 + 8, 8), RC), :]
                down = src[xx + 1, pl.ds(pl.multiple_of(y0 + 8, 8), RC), :]
                update(src, dst, xx, 0, y0, up, down)
            return 0

        lax.fori_loop(0, NY // RC, inner, 0)

    def moments(f_x, copies, dest):
        for copy in copies:
            copy.wait()
        ext = []
        for i in range(W1 + 4):
            f = f_x[i]
            ext.append(f * keep_l if i < 2 else f * keep_r if i >= W1 + 2 else f)
        image = []
        for i in range(W1 + 2):
            image.append(tangent(ext[i], ext[i + 1], ext[i + 2], stiff_x[i]))
        image[0] = image[0] * keep_l
        image[-1] = image[-1] * keep_r
        sums = [jnp.zeros((L3, S2), F32) for _ in range(4)]
        for w in range(W1):
            f, k1 = ext[w + 2], image[w + 1]
            k2 = tangent(image[w], k1, image[w + 2], stiff_x[w + 1])
            kf[w] = k1
            for n, (one, two) in enumerate(((f, f), (f, k1), (k1, k1), (k1, k2))):
                sums[n] = sums[n] + jnp.sum(one * two, axis=0)
        lane = iota((1, LANES), 1)
        row = jnp.zeros((1, LANES), F32)
        for n in range(4):
            one = jnp.sum(jnp.sum(sums[n], axis=0, keepdims=True), axis=1, keepdims=True)
            row = jnp.where(lane == n, one, row)
        dest[...] = row

    def wall_update(f_x, arrived, r):
        all_arrived(arrived, r)
        row = jnp.sum(arrived[...], axis=0)
        m0, m1, m2, m3 = (row[:, n : n + 1] for n in range(4))
        alpha0 = m0 / m1
        left_over = m0 - 2.0 * alpha0 * m1 + alpha0 * alpha0 * m2
        grow = 1.0 + left_over / m0
        alpha1 = left_over / (grow * grow * m1 - 2.0 * grow * alpha0 * m2 + alpha0 * alpha0 * m3)
        on_f, on_k = alpha0 + alpha1 * grow, alpha1 * alpha0
        new = []
        for w in range(W1):
            new.append(ws_x[w + 1] + on_f[None] * f_x[w + 2] - on_k[None] * kf[w])
        rows_out = [
            jnp.concatenate([new[w][c, 0:1, :] for w in range(W1)], axis=1) for c in range(3)
        ]
        return new, jnp.concatenate(rows_out, axis=0)

    def cut_planes(planes_of, part):
        def cut(i, _):
            for xx in planes_of:
                v = pa[xx, pl.ds(pl.multiple_of(i * RC + 8, 8), RC), :]
                top = v.astype(BF16)
                rows = pl.ds(pl.multiple_of(offset(xx, part) + i * RC, 8), RC)
                p_hi[rows, :] = top
                p_lo[rows, :] = (v - top.astype(F32)).astype(BF16)
            return 0

        lax.fori_loop(part * half_y // RC, (part + 1) * half_y // RC, cut, 0)

    def sample(which, slots, out):
        lane = lax.rem(iota((D, LANES), 1), SLOTS)
        first, count = which
        rows = pl.ds(first, count)
        for j in range(*slots, 2):
            hot = a_mat[j * D : (j + 2) * D, first : first + count]
            got_rows = dot(hot, p_hi[rows, :], (1, 0)) + dot(hot, p_lo[rows, :], (1, 0))
            for i in range(2):
                here = zcols[:, j + i : j + i + 1] == iota((D, NZ), 1)
                part = got_rows[i * D : (i + 1) * D]
                col = jnp.sum(jnp.where(here, part, 0.0), axis=1, keepdims=True)
                out = jnp.where(lane == j + i, col, out)
        return out

    mid = tuple(range(1, CX - 1))
    ends = (0, CX - 1)

    def unpack(arrived):
        rows = dot(arrived[:, 0, 0:SLOTS], owner_hot[...], (0, 0), True)
        return jnp.sum(rows * rank_hot[pl.ds(0, SLOTS), :], axis=0, keepdims=True)

    def against(v):
        acc = sum(vres[c] * v[c : c + 1] for c in range(6))
        return jnp.sum(acc, axis=1, keepdims=True)

    def combine(coef, first):
        rows = [jnp.sum(coef * vout[c], axis=0, keepdims=True) for c in range(6)]
        return first + jnp.concatenate(rows, axis=0)

    def as_row(col):
        return jnp.sum(jnp.where(iota((H, LANES), 0) == iota((H, LANES), 1), col, 0.0), axis=0, keepdims=True)

    def as_col(row):
        return jnp.sum(jnp.where(iota((H, LANES), 0) == iota((H, LANES), 1), row, 0.0), axis=1, keepdims=True)

    box = {}
    none = jnp.zeros((D, LANES), F32)
    half = SLOTS // 2

    def wall_first():
        moments(f1_x, wall_f1, m_wall1)
        same(m_wall1, a_wall1, WALL1)

    def hot_rows(first, last):
        def work():
            for j in range(first, last):
                a_mat[j * D : (j + 1) * D, :] = mask(row_of[:, j : j + 1] == iota((D, R), 1)).astype(BF16)

        return work

    def solid_first():
        _, solid = wall_update(f1_x, a_wall1, WALL1)
        box["solid"] = solid
        flux = SOURCE_GAIN * jnp.sum(nrm * solid, axis=0, keepdims=True)
        m_solid[:, 0, :] = dot(owner_hot[...], rank_hot[...] * flux, (1, 1), True)

    def solid_sent():
        each(m_solid, a_solid, SOLID)
        known = jnp.concatenate([box["solid"] - x[0:3], -x[3:6]], axis=0)
        box["h_known"] = against(known)

    def sampled_edge(name):
        def work():
            cut_planes(ends, 0)
            box[name] = box[name] + sample(edge_half[0], (0, SLOTS), none)

        return work

    def sampled(name, first, last, cut):
        def work():
            if cut:
                for part in range(2):
                    cut_planes(mid, part)
            box[name] = sample(inner_rows, (first, last), box.get(name, none))

        return work

    edge_work = (
        (lambda: place(edge_half[0]),),
        *((),) * (NCH // 2 - 1),
        (lambda: mark(edge_at + NY, R), lambda: place(edge_half[1]),),
        *((),) * (NCH // 2 - 1),
    )
    edges(0, pa, pb, True, edge_work)
    edges(
        1,
        pb,
        pa,
        True,
        (
            (lambda: mark(0, edge_at), lambda: place(inner_rows), lambda: inside(pa, pb)),
            (wall_first,),
            (hot_rows(0, half),),
            (hot_rows(half, SLOTS),),
        ),
    )
    edges(2, pa, pb, True, ((lambda: inside(pb, pa),), (lambda: tree_two(g_one, g_mid, g_two, 0),), (), (solid_first,)))
    edges(
        3,
        pb,
        pa,
        True,
        (
            (lambda: inside(pa, pb), solid_sent),
            (lambda: inside(pb, pa), sampled("seen1", 0, half, True)),
            (sampled("seen1", half, SLOTS, False), lambda: all_arrived(a_weights, WEIGHTS)),
            (sampled_edge("seen1"),),
        ),
    )
    solid1, h_known = box["solid"], box["h_known"]
    cut_planes(ends, 1)
    seen1 = sample(edge_half[1], (0, SLOTS), none) + box["seen1"]
    mine = iota((H, LANES), 1) // SLOTS == lax.rem(iota((H, LANES), 0), per_row)

    def owned(values):
        rows = [
            jnp.sum(a_weights[:, q, :] * values, axis=0, keepdims=True) for q in range(H // per_row)
        ]
        rows = jnp.concatenate([jnp.broadcast_to(f, (per_row, LANES)) for f in rows], axis=0)
        return jnp.sum(jnp.where(mine, rows, 0.0), axis=1, keepdims=True)

    m_first[...] = as_row(h_known - owned(seen1))
    same(m_first, a_first, FIRST)
    m_back[:, 0, :] = seen1
    each(m_back, a_back, BACK)
    square = iota((H, LANES), 0) == iota((H, LANES), 1)
    g_all = tree_end(g_two, 0)
    gram = [g_all if q == 0 else pltpu.roll(g_all, LANES - H * q, 1) for q in range(H // 8)]
    gram = jnp.concatenate(gram, axis=0)
    gram = jnp.where(iota((H, LANES), 1) < H, gram, 0.0)
    on_diag = jnp.where(square, gram, 0.0)
    trace = jnp.sum(jnp.sum(on_diag, axis=1, keepdims=True), axis=0, keepdims=True)
    ridge = RIDGE * trace / H + TINY
    beside = mask(iota((H, LANES), 1) == iota((H, LANES), 0) + H)
    inverse = eliminate(gram + jnp.where(square, ridge, 0.0) + beside, H)
    inverse = jnp.where(iota((H, LANES), 1) < H, pltpu.roll(inverse, LANES - H, 1), 0.0)
    all_arrived(a_solid, SOLID)
    all_arrived(a_first, FIRST)
    h_row = jnp.sum(a_first[...], axis=0)
    coeffs = -jnp.sum(inverse * h_row, axis=1, keepdims=True)
    extra = jnp.zeros((D, LANES), F32)
    for q in range(H // per_row):
        pick = iota((H, LANES), 0) == q * per_row + iota((H, LANES), 1) // SLOTS
        c_row = jnp.sum(jnp.where(pick, coeffs, 0.0), axis=0, keepdims=True)
        extra = extra + a_weights[:, H // per_row + q, :] * c_row
    step = LANES // 2
    while step >= SLOTS:
        extra = extra + pltpu.roll(extra, step, 1)
        step //= 2
    spread(a_solid[:, 0, :] + extra)

    def back_first():
        all_arrived(a_back, BACK)
        out1 = jnp.concatenate([solid1, -unpack(a_back) * nrm], axis=0)
        x2 = combine(coeffs, out1)
        force(x2, f2_x)
        for copy in planes(f2_x, 2, W1, 3):
            copy.start()
        box.update(out1=out1, x2=x2, res1=out1 - x)

    def moved_along():
        moved = box["x2"][3:6] - x[3:6]
        step_along = jnp.sum(nrm * moved, axis=0, keepdims=True)
        m_moved[:, 0, :] = dot(owner_hot[...], rank_hot[...] * step_along, (1, 1), True)
        box["moved"] = moved

    def wall_second():
        moments(f2_x, planes(f2_x, 2, W1, 3), m_wall2)
        same(m_wall2, a_wall2, WALL2)

    def shift():
        shifted = pltpu.roll(pltpu.roll(gram, 1, 0), 1, 1)
        low = (iota((H, LANES), 0) > 0) & (iota((H, LANES), 1) > 0) & (iota((H, LANES), 1) < H)
        box["shifted"] = jnp.where(low, shifted, 0.0)
        box["trace"] = trace - gram[H - 1 : H, H - 1 : H]

    def solid_second():
        new, solid2 = wall_update(f2_x, a_wall2, WALL2)
        for w in range(W1):
            for c in range(3):
                wall_out[c, :, w, :] = new[w][c]
        res1 = box["res1"]
        known = jnp.concatenate([solid2 - box["x2"][0:3] - res1[0:3], -box["moved"]], axis=0)
        box["solid2"] = solid2
        box["cross"] = against(known)
        box["own"] = jnp.sum(jnp.sum(known * known, axis=1, keepdims=True), axis=0, keepdims=True)
        box["old"] = jnp.sum(jnp.sum(known * res1, axis=1, keepdims=True), axis=0, keepdims=True)

    edge_work = (
        (lambda: place(edge_half[0]),),
        *((),) * (NCH // 2 - 1),
        (lambda: place(edge_half[1]),),
        *((),) * (NCH // 2 - 1),
    )
    edges(4, pa, pb, True, edge_work)
    edges(
        5,
        pb,
        pa,
        True,
        (
            (back_first, lambda: place(inner_rows), lambda: inside(pa, pb)),
            (moved_along,),
            (wall_second,),
            (),
        ),
    )
    edges(
        6,
        pa,
        pb,
        True,
        ((lambda: inside(pb, pa),), (lambda: each(m_moved, a_moved, MOVED),), (shift,), ()),
    )
    edges(
        7,
        pb,
        pa,
        False,
        (
            (lambda: inside(pa, pb),),
            (lambda: inside(pb, pa), sampled("seen2", 0, half, True)),
            (sampled("seen2", half, SLOTS, False), solid_second),
            (sampled_edge("seen2"),),
        ),
    )
    out1, shifted, trace, solid2 = box["out1"], box["shifted"], box["trace"], box["solid2"]
    cross_known, own_known, old_known = box["cross"], box["own"], box["old"]
    save = pltpu.make_async_copy(pa.at[:, pl.ds(8, NY), :], p_out, out_sem)
    save.start()
    all_arrived(a_moved, MOVED)
    cut_planes(ends, 1)
    seen2 = sample(edge_half[1], (0, SLOTS), none) + box["seen2"]
    gained = seen2 - seen1
    cells_msg = a_cells[:, 0, :]
    n_n = pltpu.roll(cells_msg, LANES - 2 * SLOTS, 1)
    n_t = pltpu.roll(cells_msg, LANES - 3 * SLOTS, 1)
    single = iota((D, LANES), 1) < SLOTS
    own = jnp.where(single, gained * (gained * n_n + 2.0 * a_moved[:, 0, :]), 0.0)
    old = jnp.where(single, gained * (seen1 * n_n + n_t), 0.0)
    own = own_known + jnp.sum(jnp.sum(own, axis=0, keepdims=True), axis=1, keepdims=True)
    old = old_known + jnp.sum(jnp.sum(old, axis=0, keepdims=True), axis=1, keepdims=True)
    lane = iota((1, LANES), 1)
    cross = as_row(cross_known - owned(gained))
    m_last[...] = jnp.where(lane == H, own, jnp.where(lane == H + 1, old, cross))
    same(m_last, a_last, LAST)
    m_back2[:, 0, :] = seen2
    each(m_back2, a_back2, BACK2)
    all_arrived(a_last, LAST)
    last = jnp.sum(a_last[...], axis=0)
    own, old = last[:, H : H + 1], last[:, H + 1 : H + 2]
    cross = jnp.where((lane > 0) & (lane < H), pltpu.roll(last, 1, 1), jnp.where(lane == 0, own, 0.0))
    h_row = pltpu.roll(jnp.where(lane < H, h_row, 0.0), 1, 1)
    h_row = jnp.where(lane == 0, own + old, h_row + cross)
    lanes = iota((H, LANES), 1)
    first = iota((H, LANES), 0) == 0
    gram = jnp.where(first, cross, jnp.where(lanes == 0, as_col(cross), shifted))
    ridge = RIDGE * (trace + own) / H + TINY
    gram = gram + jnp.where(square, ridge, 0.0)
    gram = jnp.where(lanes == H, as_col(h_row), gram)
    coeffs = -eliminate(gram, H)[:, H : H + 1]
    rest = pltpu.roll(coeffs * jnp.ones((H, LANES), F32), H - 1, 0)[:, 0:1]
    rest = jnp.where(iota((H, 1), 0) < H - 1, rest, 0.0)
    state = combine(rest, jnp.zeros((6, IF), F32))
    all_arrived(a_back2, BACK2)
    out2 = jnp.concatenate([solid2, -unpack(a_back2) * nrm], axis=0)
    state_out[...] = out2 + coeffs[0:1, :] * (out2 - out1) + state

    for arrived, r in (
        (a_cells, CELLS),
        (a_weights, WEIGHTS),
        (a_solid, SOLID),
        (a_first, FIRST),
        (a_back, BACK),
        (a_moved, MOVED),
        (a_wall1, WALL1),
        (a_wall2, WALL2),
        (a_back2, BACK2),
        (a_last, LAST),
    ):
        all_sent(arrived, r)
    for ch in range(NCH):
        for copy in halo(pb, SWEEPS * COUPLE - 1, ch):
            copy.wait_send()
    save.wait()


def finish(*refs):
    sources, targets, stages, sem = refs[:3], refs[3:6], refs[6:9], refs[9]
    triples = []
    for source, stage, target in zip(sources, stages, targets, strict=True):
        if len(source.shape) == 3:
            triples += [(source.at[i], stage.at[i], target.at[i]) for i in range(source.shape[0])]
        else:
            triples.append((source, stage, target))
    come = [pltpu.make_async_copy(a, b, sem.at[0, i]) for i, (a, b, _) in enumerate(triples)]
    leave = [pltpu.make_async_copy(b, c, sem.at[1, i]) for i, (_, b, c) in enumerate(triples)]
    for copy in come:
        copy.start()
    for a, b in zip(come, leave, strict=True):
        a.wait()
        b.start()
    for copy in leave:
        copy.wait()


def local(cfg, *args):
    (D, SP, LO, CX, NY, NZ, L3, W1, S2, IF, H, NCH, RC) = cfg
    (p, coef, rhs, ws, stiff, load, normals, owner, cell, x, vres, vout) = args
    vres, vout = vres.transpose(1, 0, 2), vout.transpose(1, 0, 2)
    R, K = CX * NY, SLOTS * D
    EX = SWEEPS * COUPLE
    wide = LANES
    G = 8

    def vmem(*shape, dtype=F32):
        return pltpu.VMEM(shape, dtype)

    dma = pltpu.SemaphoreType.DMA
    scratch = [
        vmem(CX, NY + 16, NZ), vmem(CX, NY + 16, NZ), vmem(CX, NY, NZ), vmem(R, NZ), vmem(R, NZ),
        vmem(EX, NY, NZ), vmem(EX, NY, NZ),
        vmem(R, K, dtype=BF16), vmem(K, R, dtype=BF16), vmem(K, NZ, dtype=BF16), vmem(K, NZ, dtype=BF16),
        vmem(R, NZ, dtype=BF16), vmem(R, NZ, dtype=BF16),
        vmem(3, L3, W1, S2), vmem(L3, W1, S2), vmem(3, L3, W1, S2),
        vmem(3, IF), vmem(1, IF, dtype=jnp.int32), vmem(1, IF, dtype=jnp.int32), vmem(6, IF),
        vmem(6, H, IF), vmem(6, H, IF),
        vmem(D, IF), vmem(LANES, IF),
        vmem(D, 1, wide), vmem(D, 1, wide), vmem(D, 8, wide), vmem(D, 8, wide),
        vmem(D, 1, wide), vmem(D, 1, wide), vmem(D, 1, wide), vmem(D, 1, wide), vmem(D, 1, wide), vmem(D, 1, wide),
        vmem(D, 1, wide), vmem(D, 1, wide),
        vmem(1, wide), vmem(D, 1, wide), vmem(1, wide), vmem(D, 1, wide),
        vmem(W1 + 2, 3, L3, S2), vmem(W1 + 2, L3, S2), vmem(W1 + 4, 3, L3, S2), vmem(W1 + 4, 3, L3, S2),
        vmem(W1, 3, L3, S2), vmem(W1, 3, L3, S2),
        vmem(G, wide), vmem(LO, G, wide), vmem(G, wide), vmem(D // LO, G, wide),
        vmem(1, wide), vmem(D, 1, wide), vmem(1, wide), vmem(D, 1, wide),
        vmem(LANES, IF), vmem(D, SLOTS, dtype=jnp.int32),
        dma((11 + 2 * CX,)), dma((ROUNDS,)), dma((ROUNDS,)), dma((EX, 2, NCH)), dma((EX, 2, NCH)),
        dma((4, 2)), dma((4, 2)), dma((4,)), dma((4,)), dma(()),
    ]
    anywhere = pl.BlockSpec(memory_space=pl.ANY)
    inside = pl.BlockSpec(memory_space=pltpu.VMEM)
    shapes = (
        jax.ShapeDtypeStruct((6, IF), F32),
        jax.ShapeDtypeStruct((CX, NY, NZ), F32),
        jax.ShapeDtypeStruct((3, L3, W1, S2), F32),
    )
    results = pl.pallas_call(
        functools.partial(kernel, cfg),
        out_shape=shapes,
        in_specs=[anywhere] * 12,
        out_specs=(inside, anywhere, inside),
        scratch_shapes=scratch,
        compiler_params=pltpu.CompilerParams(
            collective_id=0, has_side_effects=True, vmem_limit_bytes=60 * 2**20
        ),
    )(
        p, coef, rhs.reshape(R, NZ), ws, stiff, load, normals,
        owner.reshape(1, IF), cell.reshape(1, IF), x, vres, vout,
    )
    return pl.pallas_call(
        finish,
        out_shape=shapes,
        in_specs=[anywhere] * 3,
        out_specs=(anywhere,) * 3,
        scratch_shapes=[vmem(6, IF), vmem(CX, NY, NZ), vmem(3, L3, W1, S2), dma((2, CX + 2))],
    )(*results)


def solution(mesh):
    sp = mesh.shape["space"]
    devices = mesh.shape["solver"] * sp

    def run(*args):
        CX, NY, NZ = args[0].shape
        _, L3, W1, S2 = args[3].shape
        IF, H = args[8].shape[0], args[10].shape[0]
        lo = 8 if devices > 8 else 4
        cfg = (devices, sp, lo, CX, NY, NZ, L3, W1, S2, IF, H, 4, min(32, NY // 4))
        return local(cfg, *args)

    in_specs = (
        P(BOTH, None, None),
        P(BOTH, None, None),
        P(BOTH, None, None),
        P(None, None, BOTH, None),
        P(None, BOTH, None),
        P(None, None, BOTH, None),
        P(None, BOTH),
        P(BOTH, None),
        P(BOTH),
        P(None, BOTH),
        P(None, None, BOTH),
        P(None, None, BOTH),
    )
    out_specs = (P(None, BOTH), P(BOTH, None, None), P(None, None, BOTH, None))
    return jax.shard_map(run, mesh=mesh, in_specs=in_specs, out_specs=out_specs, check_vma=False)
```

```python
import functools

import jax
import jax.numpy as jnp
from jax import lax
from jax.experimental import pallas as pl
from jax.experimental.pallas import tpu as pltpu
from jax.sharding import PartitionSpec as P

SWEEPS = 4
COUPLE = 2
OMEGA = 0.8
SOURCE_GAIN = 4.0
RIDGE = 0.1
TINY = 1e-06
SLOTS = 16
LANES = 128
MESH = pl.DeviceIdType.MESH
F32 = jnp.float32
BF16 = jnp.bfloat16
BOTH = ("solver", "space")
CELLS, WEIGHTS, SOLID, FIRST, BACK, MOVED, BACK2, LAST, WALL1, WALL2 = range(10)
ROUNDS = 10


def iota(shape, dim):
    return lax.broadcasted_iota(jnp.int32, shape, dim)


def dot(a, b, contract, exact=False):
    return lax.dot_general(
        a,
        b,
        (((contract[0],), (contract[1],)), ((), ())),
        precision=lax.Precision.HIGHEST if exact else None,
        preferred_element_type=F32,
    )


def mask(flag):
    return jnp.where(flag, 1.0, 0.0).astype(F32)


def eliminate(m, size):
    row = iota(m.shape, 0)
    for k in range(size):
        pivot_row = m[k : k + 1, :] / m[k : k + 1, k : k + 1]
        m = jnp.where(row == k, pivot_row, m - m[:, k : k + 1] * pivot_row)
    return m


def kernel(cfg, *refs):
    (D, SP, LO, CX, NY, NZ, L3, W1, S2, IF, H, NCH, RC) = cfg
    HI = D // LO
    R, K = CX * NY, SLOTS * D
    (
        p_hbm, coef_hbm, rhs_hbm, ws_hbm, stiff_hbm, load_hbm, normal_hbm, owner_hbm, cell_hbm, x_hbm, v_hbm, w_hbm,
        state_out, p_out, wall_out,
        pa, pb, weight, rhs, total, halo_l, halo_r, at, a_mat, f_hi, f_lo, p_hi, p_lo,
        ws_v, stiff_v, load_v, normal, owner, cell, x0, vres, vout,
        owner_hot, rank_hot,
        m_cells, a_cells, m_weights, a_weights, m_solid, a_solid, m_back, a_back, m_back2, a_back2, m_moved, a_moved,
        m_first, a_first, m_last, a_last,
        ws_x, stiff_x, f1_x, f2_x, kf, base,
        g_send, g_one, g_mid, g_two, m_wall1, a_wall1, m_wall2, a_wall2,
        u_rows, zcols,
        load_sem, all_send, all_recv, halo_send, halo_recv, wall_send, wall_recv, tree_send, tree_recv, out_sem,
    ) = refs
    me = lax.axis_index("solver") * SP + lax.axis_index("space")
    left, right = lax.rem(me + D - 1, D), lax.rem(me + 1, D)
    keep_l = jnp.where(me > 0, 1.0, 0.0).astype(F32)
    keep_r = jnp.where(me < D - 1, 1.0, 0.0).astype(F32)

    def at_device(d):
        return (d // SP, lax.rem(d, SP))

    def remote(src, dst, send, recv, d):
        return pltpu.make_async_remote_copy(
            src_ref=src,
            dst_ref=dst,
            send_sem=send,
            recv_sem=recv,
            device_id=at_device(d),
            device_id_type=MESH,
        )

    half_y = NY // 2
    edge_at = (CX - 2) * NY

    def offset(xx, part):
        if 0 < xx < CX - 1:
            return (xx - 1) * NY
        return edge_at + part * half_y + (half_y if xx else 0)

    loads = [
        pltpu.make_async_copy(src, dst, load_sem.at[i])
        for i, (src, dst) in enumerate(
            (
                (owner_hbm, owner),
                (cell_hbm, cell),
                (normal_hbm, normal),
                (x_hbm, x0),
                (p_hbm, pa.at[:, pl.ds(8, NY), :]),
                (ws_hbm, ws_v),
                (stiff_hbm, stiff_v),
                (load_hbm, load_v),
                (v_hbm, vres),
                (w_hbm, vout),
                (coef_hbm, weight),
            )
            + tuple(
                (
                    rhs_hbm.at[pl.ds(xx * NY + part * half_y, half_y), :],
                    rhs.at[pl.ds(offset(xx, part) + part * half_y, half_y), :],
                )
                for xx in range(CX)
                for part in range(2)
            )
        )
    ]
    for copy in loads:
        copy.start()
    barrier = pltpu.get_barrier_semaphore()

    NS = D // SP
    my_s, my_p = me // SP, lax.rem(me, SP)

    def peers(act):
        for ds in sorted(range(NS), key=lambda q: -min(q, NS - q)):
            there = lax.rem(my_s + ds, NS)

            def one(k, _):
                act(there, lax.rem(my_p + SP // 2 + k, SP))
                return 0

            if ds:
                lax.fori_loop(0, SP, one, 0, unroll=4)
            else:
                lax.fori_loop(0, SP // 2, one, 0, unroll=4 if SP >= 8 else 1)
                lax.fori_loop(SP // 2 + 1, SP, one, 0, unroll=3 if SP >= 8 else 1)

    def start_remote(src, dst, r, there, low):
        pltpu.make_async_remote_copy(
            src_ref=src,
            dst_ref=dst,
            send_sem=all_send.at[r],
            recv_sem=all_recv.at[r],
            device_id=(there, low),
            device_id_type=MESH,
        ).start()

    def greet(there, low):
        pl.semaphore_signal(barrier, inc=1, device_id=(there, low), device_id_type=MESH)

    peers(greet)

    def each(msg, arrived, r):
        peers(lambda there, low: start_remote(msg.at[there * SP + low], arrived.at[me], r, there, low))
        arrived[me] = msg[me]

    def same(row, arrived, r):
        peers(lambda there, low: start_remote(row, arrived.at[me], r, there, low))
        arrived[me] = row[...]

    def all_arrived(arrived, r):
        part = arrived.at[pl.ds(0, D - 1)]
        remote(part, part, all_send.at[r], all_recv.at[r], right).wait_recv()

    def all_sent(arrived, r):
        part = arrived.at[pl.ds(0, D - 1)]
        remote(part, part, all_send.at[r], all_recv.at[r], right).wait_send()

    lo, hi = lax.rem(me, LO), me // LO

    def tree_one(send, one, r):
        for k in range(1, LO):
            d = hi * LO + lax.rem(lo + k, LO)
            remote(send, one.at[lo], tree_send.at[r], tree_recv.at[r], d).start()
        one[lo] = send[...]

    def tree_two(one, mid, two, r):
        part = one.at[pl.ds(0, LO - 1)]
        remote(part, part, tree_send.at[r], tree_recv.at[r], right).wait_recv()
        mid[...] = jnp.sum(one[...], axis=0)
        for k in range(1, HI):
            d = lax.rem(hi + k, HI) * LO + lo
            remote(mid, two.at[hi], tree_send.at[r + 1], tree_recv.at[r + 1], d).start()
        two[hi] = mid[...]

    def tree_end(two, r):
        part = two.at[pl.ds(0, HI - 1)]
        remote(part, part, tree_send.at[r + 1], tree_recv.at[r + 1], right).wait_recv()
        return jnp.sum(two[...], axis=0)

    for copy in loads[:4]:
        copy.wait()
    block = min(IF, LANES)
    before = mask(iota((block, block), 0) < iota((block, block), 1)).astype(BF16)
    ones = jnp.ones((block, block), BF16)
    carry = jnp.zeros((D, block), F32)
    for b in range(IF // block):
        cols = pl.ds(b * block, block)
        hot = mask(owner[:, cols] == iota((D, block), 0))
        owner_hot[:, cols] = hot
        hot16 = hot.astype(BF16)
        rank = jnp.sum(hot * (carry + dot(hot16, before, (1, 0))), axis=0, keepdims=True)
        carry = carry + dot(hot16, ones, (1, 0))
        slot = lax.rem(iota((LANES, block), 0), SLOTS).astype(F32)
        rank_hot[:, cols] = mask(slot == rank)
    x = x0[...]
    nrm = normal[...]
    flux = SOURCE_GAIN * jnp.sum(nrm * x[0:3], axis=0, keepdims=True)
    group = iota((LANES, IF), 0) // SLOTS
    named = (cell[...] + 1).astype(F32)
    squared = jnp.sum(nrm * nrm, axis=0, keepdims=True)
    along = jnp.sum(nrm * x[3:6], axis=0, keepdims=True)
    packed = jnp.where(group == 2, squared, jnp.where(group == 3, along, 0.0))
    packed = jnp.where(group == 0, flux, jnp.where(group == 1, named, packed))
    packed = rank_hot[...] * packed
    m_cells[:, 0, :] = dot(owner_hot[...], packed, (1, 1), True)

    pl.semaphore_wait(barrier, D - 1)
    each(m_cells, a_cells, CELLS)

    def halo(buf, e, ch):
        rows = pl.ds(ch * (NY // NCH), NY // NCH)
        inner = pl.ds(ch * (NY // NCH) + 8, NY // NCH)
        to_left = remote(
            buf.at[0, inner, :], halo_r.at[e, rows, :], halo_send.at[e, 0, ch], halo_recv.at[e, 0, ch], left
        )
        to_right = remote(
            buf.at[CX - 1, inner, :], halo_l.at[e, rows, :], halo_send.at[e, 1, ch], halo_recv.at[e, 1, ch], right
        )
        return to_left, to_right

    loads[4].wait()
    for ch in range(NCH):
        for copy in halo(pa, 0, ch):
            copy.start()

    for copy in loads[5:8]:
        copy.wait()
    for w in range(W1):
        for c in range(3):
            ws_x[1 + w, c] = ws_v[c, :, w, :]
        stiff_x[1 + w] = stiff_v[:, w, :]

    def planes(buf, width, count, r):
        return (
            remote(buf.at[pl.ds(width, width)], buf.at[pl.ds(width + count, width)], wall_send.at[r, 0], wall_recv.at[r, 0], left),
            remote(buf.at[pl.ds(count, width)], buf.at[pl.ds(0, width)], wall_send.at[r, 1], wall_recv.at[r, 1], right),
        )

    wall_static = planes(ws_x, 1, W1, 0) + planes(stiff_x, 1, W1, 1)
    for copy in wall_static:
        copy.start()

    pad = jnp.zeros((CX, 8, NZ), F32)
    for buf in (pa, pb):
        buf[:, pl.ds(0, 8), :] = pad
        buf[:, pl.ds(NY + 8, 8), :] = pad

    loads[8].wait()
    loads[9].wait()
    per_row = LANES // SLOTS

    def weights(ref, at_row, factor, first):
        u = sum(ref[at_row + c] * (factor * nrm[c : c + 1]) for c in range(3))
        for q in range(H // per_row):
            for i in range(per_row):
                a = q * per_row + i
                u_rows[i * SLOTS : (i + 1) * SLOTS, :] = rank_hot[0:SLOTS, :] * u[a : a + 1, :]
            m_weights[:, first + q, :] = dot(owner_hot[...], u_rows[...], (1, 1), True)

    weights(vres, 3, 1.0, 0)
    weights(vout, 0, SOURCE_GAIN, H // per_row)

    each(m_weights, a_weights, WEIGHTS)

    def layers(f):
        row = iota(f.shape, 1)
        up = jnp.where(row == 0, 0.0, pltpu.roll(f, 1, 1))
        down = jnp.where(row == L3 - 1, 0.0, pltpu.roll(f, L3 - 1, 1))
        return up + down + pltpu.roll(f, 1, 2) + pltpu.roll(f, S2 - 1, 2)

    def tangent(low, f, high, stiff):
        return (6.0 + stiff)[None] * f - (low + high + layers(f))

    for copy in wall_static:
        copy.wait()

    def force(x_now, dest):
        for w in range(W1):
            part = pl.ds(w * S2, S2)
            for c in range(3):
                b = base[w, c]
                t = x_now[3 + c : 4 + c, w * S2 : (w + 1) * S2]
                row = iota((L3, S2), 0)
                dest[2 + w, c] = b + jnp.where(row == 0, t, 0.0)

    for w in range(W1):
        low = ws_x[w] * (keep_l if w == 0 else 1.0)
        high = ws_x[w + 2] * (keep_r if w == W1 - 1 else 1.0)
        k_w = tangent(low, ws_x[w + 1], high, stiff_x[w + 1])
        for c in range(3):
            base[w, c] = load_v[c, :, w, :] - k_w[c]
    force(x, f1_x)
    wall_f1 = planes(f1_x, 2, W1, 2)
    for copy in wall_f1:
        copy.start()

    gram = jnp.zeros((H, H), F32)
    for c in range(6):
        v_c = vres[c]
        gram = gram + dot(v_c, v_c, (1, 1), True)
    g_send[0:8, :] = jnp.concatenate([gram[8 * q : 8 * q + 8, :] for q in range(H // 8)], axis=1)
    tree_one(g_send, g_one, 0)
    for copy in loads[10:]:
        copy.wait()

    def invert(i, _):
        rows = pl.ds(pl.multiple_of(i * RC, 8), RC)
        for xx in range(CX):
            weight[xx, rows, :] = OMEGA / (6.0 + weight[xx, rows, :])
        return 0

    lax.fori_loop(0, NY // RC, invert, 0)

    all_arrived(a_cells, CELLS)
    y_bits, z_bits = NY.bit_length() - 1, NZ.bit_length() - 1

    def placed(cells):
        xx = cells >> (y_bits + z_bits)
        y = jnp.bitwise_and(cells >> z_bits, NY - 1)
        part = y >> (y_bits - 1)
        on_edge = edge_at + part * half_y + y + jnp.where(xx == 0, 0, half_y)
        inner = (xx > 0) & (xx < CX - 1)
        return jnp.where(inner, (xx - 1) * NY + y, jnp.where(xx < 0, -1, on_edge))

    got = a_cells[:, 0, :]
    found = got[:, SLOTS : 2 * SLOTS].astype(jnp.int32) - 1
    row_of = placed(found)
    zcols[:, 0:SLOTS] = jnp.bitwise_and(found, NZ - 1)
    flipped = got.T[SLOTS : 2 * SLOTS, :].astype(jnp.int32) - 1
    row_flat = placed(flipped)

    def mark(first, last):
        def one(i, _):
            y0 = pl.multiple_of(i * RC, 8)
            for j in range(SLOTS):
                hit = iota((RC, D), 0) == row_flat[j : j + 1, :] - y0
                at[pl.ds(y0, RC), j * D : (j + 1) * D] = mask(hit).astype(BF16)
            return 0

        lax.fori_loop(first // RC, last // RC, one, 0)

    mark(edge_at, edge_at + NY)

    def spread(flux_now):
        for j in range(SLOTS):
            f_j = flux_now[:, j : j + 1]
            top = f_j.astype(BF16).astype(F32)
            here = zcols[:, j : j + 1] == iota((D, NZ), 1)
            f_hi[j * D : (j + 1) * D, :] = jnp.where(here, top, 0.0).astype(BF16)
            f_lo[j * D : (j + 1) * D, :] = jnp.where(here, f_j - top, 0.0).astype(BF16)

    inner_rows, edge_rows = (0, edge_at), (edge_at, 2 * NY)
    edge_half = ((edge_at, NY), (edge_at + NY, NY))

    def place(which):
        rows = pl.ds(*which)
        hot = at[rows, :]
        found_here = dot(hot, f_hi[...], (1, 0)) + dot(hot, f_lo[...], (1, 0))
        total[rows, :] = rhs[rows, :] + found_here

    spread(got)

    def update(src, dst, xx, part, y0, up, down):
        ext = src[xx, pl.ds(y0, RC + 16), :]
        c = ext[8 : 8 + RC]
        beside = pltpu.roll(ext, 1, 0)[8 : 8 + RC] + pltpu.roll(ext, RC + 15, 0)[8 : 8 + RC]
        lane = iota((RC, NZ), 1)
        beside = beside + jnp.where(lane == 0, 0.0, pltpu.roll(c, 1, 1))
        beside = beside + jnp.where(lane == NZ - 1, 0.0, pltpu.roll(c, NZ - 1, 1))
        rows = pl.ds(pl.multiple_of(offset(xx, part) + y0, 8), RC)
        new = (1.0 - OMEGA) * c + weight[xx, pl.ds(y0, RC), :] * (total[rows, :] + up + down + beside)
        dst[xx, pl.ds(pl.multiple_of(y0 + 8, 8), RC), :] = new

    chunk = NY // NCH

    def edges(e, src, dst, send, beside=()):
        for ch in range(NCH):
            for work in beside[ch] if beside else ():
                work()
            if e >= 1:
                for copy in halo(dst, e - 1, ch):
                    copy.wait_send()
            to_left, to_right = halo(src, e, ch)
            to_left.wait_recv()
            to_right.wait_recv()

            def part(i, _, ch=ch):
                y0 = pl.multiple_of(ch * chunk + i * RC, 8)
                up = halo_l[e, pl.ds(y0, RC), :] * keep_l
                down = src[1, pl.ds(pl.multiple_of(y0 + 8, 8), RC), :]
                update(src, dst, 0, ch * chunk // half_y, y0, up, down)
                up = src[CX - 2, pl.ds(pl.multiple_of(y0 + 8, 8), RC), :]
                down = halo_r[e, pl.ds(y0, RC), :] * keep_r
                update(src, dst, CX - 1, ch * chunk // half_y, y0, up, down)
                return 0

            lax.fori_loop(0, chunk // RC, part, 0)
            if send:
                for copy in halo(dst, e + 1, ch):
                    copy.start()

    def inside(src, dst):
        def inner(i, _):
            y0 = pl.multiple_of(i * RC, 8)
            for xx in range(1, CX - 1):
                up = src[xx - 1, pl.ds(pl.multiple_of(y0 + 8, 8), RC), :]
                down = src[xx + 1, pl.ds(pl.multiple_of(y0 + 8, 8), RC), :]
                update(src, dst, xx, 0, y0, up, down)
            return 0

        lax.fori_loop(0, NY // RC, inner, 0)

    def moments(f_x, copies, dest):
        for copy in copies:
            copy.wait()
        ext = []
        for i in range(W1 + 4):
            f = f_x[i]
            ext.append(f * keep_l if i < 2 else f * keep_r if i >= W1 + 2 else f)
        image = []
        for i in range(W1 + 2):
            image.append(tangent(ext[i], ext[i + 1], ext[i + 2], stiff_x[i]))
        image[0] = image[0] * keep_l
        image[-1] = image[-1] * keep_r
        sums = [jnp.zeros((L3, S2), F32) for _ in range(4)]
        for w in range(W1):
            f, k1 = ext[w + 2], image[w + 1]
            k2 = tangent(image[w], k1, image[w + 2], stiff_x[w + 1])
            kf[w] = k1
            for n, (one, two) in enumerate(((f, f), (f, k1), (k1, k1), (k1, k2))):
                sums[n] = sums[n] + jnp.sum(one * two, axis=0)
        lane = iota((1, LANES), 1)
        row = jnp.zeros((1, LANES), F32)
        for n in range(4):
            one = jnp.sum(jnp.sum(sums[n], axis=0, keepdims=True), axis=1, keepdims=True)
            row = jnp.where(lane == n, one, row)
        dest[...] = row

    def wall_update(f_x, arrived, r):
        all_arrived(arrived, r)
        row = jnp.sum(arrived[...], axis=0)
        m0, m1, m2, m3 = (row[:, n : n + 1] for n in range(4))
        alpha0 = m0 / m1
        left_over = m0 - 2.0 * alpha0 * m1 + alpha0 * alpha0 * m2
        grow = 1.0 + left_over / m0
        alpha1 = left_over / (grow * grow * m1 - 2.0 * grow * alpha0 * m2 + alpha0 * alpha0 * m3)
        on_f, on_k = alpha0 + alpha1 * grow, alpha1 * alpha0
        new = []
        for w in range(W1):
            new.append(ws_x[w + 1] + on_f[None] * f_x[w + 2] - on_k[None] * kf[w])
        rows_out = [
            jnp.concatenate([new[w][c, 0:1, :] for w in range(W1)], axis=1) for c in range(3)
        ]
        return new, jnp.concatenate(rows_out, axis=0)

    def cut_planes(planes_of, part):
        def cut(i, _):
            for xx in planes_of:
                v = pa[xx, pl.ds(pl.multiple_of(i * RC + 8, 8), RC), :]
                top = v.astype(BF16)
                rows = pl.ds(pl.multiple_of(offset(xx, part) + i * RC, 8), RC)
                p_hi[rows, :] = top
                p_lo[rows, :] = (v - top.astype(F32)).astype(BF16)
            return 0

        lax.fori_loop(part * half_y // RC, (part + 1) * half_y // RC, cut, 0)

    def sample(which, slots, out):
        lane = lax.rem(iota((D, LANES), 1), SLOTS)
        first, count = which
        rows = pl.ds(first, count)
        for j in range(*slots, 2):
            hot = a_mat[j * D : (j + 2) * D, first : first + count]
            got_rows = dot(hot, p_hi[rows, :], (1, 0)) + dot(hot, p_lo[rows, :], (1, 0))
            for i in range(2):
                here = zcols[:, j + i : j + i + 1] == iota((D, NZ), 1)
                part = got_rows[i * D : (i + 1) * D]
                col = jnp.sum(jnp.where(here, part, 0.0), axis=1, keepdims=True)
                out = jnp.where(lane == j + i, col, out)
        return out

    mid = tuple(range(1, CX - 1))
    ends = (0, CX - 1)

    def unpack(arrived):
        rows = dot(arrived[:, 0, 0:SLOTS], owner_hot[...], (0, 0), True)
        return jnp.sum(rows * rank_hot[pl.ds(0, SLOTS), :], axis=0, keepdims=True)

    def against(v):
        acc = sum(vres[c] * v[c : c + 1] for c in range(6))
        return jnp.sum(acc, axis=1, keepdims=True)

    def combine(coef, first):
        rows = [jnp.sum(coef * vout[c], axis=0, keepdims=True) for c in range(6)]
        return first + jnp.concatenate(rows, axis=0)

    def as_row(col):
        return jnp.sum(jnp.where(iota((H, LANES), 0) == iota((H, LANES), 1), col, 0.0), axis=0, keepdims=True)

    def as_col(row):
        return jnp.sum(jnp.where(iota((H, LANES), 0) == iota((H, LANES), 1), row, 0.0), axis=1, keepdims=True)

    box = {}
    none = jnp.zeros((D, LANES), F32)
    half = SLOTS // 2

    def wall_first():
        moments(f1_x, wall_f1, m_wall1)
        same(m_wall1, a_wall1, WALL1)

    def hot_rows(first, last):
        def work():
            for j in range(first, last):
                a_mat[j * D : (j + 1) * D, :] = mask(row_of[:, j : j + 1] == iota((D, R), 1)).astype(BF16)

        return work

    def solid_first():
        _, solid = wall_update(f1_x, a_wall1, WALL1)
        box["solid"] = solid
        flux = SOURCE_GAIN * jnp.sum(nrm * solid, axis=0, keepdims=True)
        m_solid[:, 0, :] = dot(owner_hot[...], rank_hot[...] * flux, (1, 1), True)

    def solid_sent():
        each(m_solid, a_solid, SOLID)
        known = jnp.concatenate([box["solid"] - x[0:3], -x[3:6]], axis=0)
        box["h_known"] = against(known)

    def sampled_edge(name):
        def work():
            cut_planes(ends, 0)
            box[name] = box[name] + sample(edge_half[0], (0, SLOTS), none)

        return work

    def sampled(name, first, last, cut):
        def work():
            if cut:
                for part in range(2):
                    cut_planes(mid, part)
            box[name] = sample(inner_rows, (first, last), box.get(name, none))

        return work

    edge_work = (
        (lambda: place(edge_half[0]),),
        *((),) * (NCH // 2 - 1),
        (lambda: mark(edge_at + NY, R), lambda: place(edge_half[1]),),
        *((),) * (NCH // 2 - 1),
    )
    edges(0, pa, pb, True, edge_work)
    edges(
        1,
        pb,
        pa,
        True,
        (
            (lambda: mark(0, edge_at), lambda: place(inner_rows), lambda: inside(pa, pb)),
            (wall_first,),
            (hot_rows(0, half),),
            (hot_rows(half, SLOTS),),
        ),
    )
    edges(2, pa, pb, True, ((lambda: inside(pb, pa),), (lambda: tree_two(g_one, g_mid, g_two, 0),), (), (solid_first,)))
    edges(
        3,
        pb,
        pa,
        True,
        (
            (lambda: inside(pa, pb), lambda: inside(pb, pa)),
            (solid_sent, sampled("seen1", 0, half, True)),
            (sampled("seen1", half, SLOTS, False), lambda: all_arrived(a_weights, WEIGHTS)),
            (sampled_edge("seen1"),),
        ),
    )
    solid1, h_known = box["solid"], box["h_known"]
    cut_planes(ends, 1)
    seen1 = sample(edge_half[1], (0, SLOTS), none) + box["seen1"]
    mine = iota((H, LANES), 1) // SLOTS == lax.rem(iota((H, LANES), 0), per_row)

    def owned(values):
        rows = [
            jnp.sum(a_weights[:, q, :] * values, axis=0, keepdims=True) for q in range(H // per_row)
        ]
        rows = jnp.concatenate([jnp.broadcast_to(f, (per_row, LANES)) for f in rows], axis=0)
        return jnp.sum(jnp.where(mine, rows, 0.0), axis=1, keepdims=True)

    m_first[...] = as_row(h_known - owned(seen1))
    same(m_first, a_first, FIRST)
    m_back[:, 0, :] = seen1
    each(m_back, a_back, BACK)
    square = iota((H, LANES), 0) == iota((H, LANES), 1)
    g_all = tree_end(g_two, 0)
    gram = [g_all if q == 0 else pltpu.roll(g_all, LANES - H * q, 1) for q in range(H // 8)]
    gram = jnp.concatenate(gram, axis=0)
    gram = jnp.where(iota((H, LANES), 1) < H, gram, 0.0)
    on_diag = jnp.where(square, gram, 0.0)
    trace = jnp.sum(jnp.sum(on_diag, axis=1, keepdims=True), axis=0, keepdims=True)
    ridge = RIDGE * trace / H + TINY
    beside = mask(iota((H, LANES), 1) == iota((H, LANES), 0) + H)
    inverse = eliminate(gram + jnp.where(square, ridge, 0.0) + beside, H)
    inverse = jnp.where(iota((H, LANES), 1) < H, pltpu.roll(inverse, LANES - H, 1), 0.0)
    all_arrived(a_solid, SOLID)
    all_arrived(a_first, FIRST)
    h_row = jnp.sum(a_first[...], axis=0)
    coeffs = -jnp.sum(inverse * h_row, axis=1, keepdims=True)
    extra = jnp.zeros((D, LANES), F32)
    for q in range(H // per_row):
        pick = iota((H, LANES), 0) == q * per_row + iota((H, LANES), 1) // SLOTS
        c_row = jnp.sum(jnp.where(pick, coeffs, 0.0), axis=0, keepdims=True)
        extra = extra + a_weights[:, H // per_row + q, :] * c_row
    step = LANES // 2
    while step >= SLOTS:
        extra = extra + pltpu.roll(extra, step, 1)
        step //= 2
    spread(a_solid[:, 0, :] + extra)

    def back_first():
        all_arrived(a_back, BACK)
        out1 = jnp.concatenate([solid1, -unpack(a_back) * nrm], axis=0)
        x2 = combine(coeffs, out1)
        force(x2, f2_x)
        for copy in planes(f2_x, 2, W1, 3):
            copy.start()
        box.update(out1=out1, x2=x2, res1=out1 - x)

    def moved_along():
        moved = box["x2"][3:6] - x[3:6]
        step_along = jnp.sum(nrm * moved, axis=0, keepdims=True)
        m_moved[:, 0, :] = dot(owner_hot[...], rank_hot[...] * step_along, (1, 1), True)
        box["moved"] = moved

    def wall_second():
        moments(f2_x, planes(f2_x, 2, W1, 3), m_wall2)
        same(m_wall2, a_wall2, WALL2)

    def shift():
        shifted = pltpu.roll(pltpu.roll(gram, 1, 0), 1, 1)
        low = (iota((H, LANES), 0) > 0) & (iota((H, LANES), 1) > 0) & (iota((H, LANES), 1) < H)
        box["shifted"] = jnp.where(low, shifted, 0.0)
        box["trace"] = trace - gram[H - 1 : H, H - 1 : H]

    def solid_second():
        new, solid2 = wall_update(f2_x, a_wall2, WALL2)
        for w in range(W1):
            for c in range(3):
                wall_out[c, :, w, :] = new[w][c]
        res1 = box["res1"]
        known = jnp.concatenate([solid2 - box["x2"][0:3] - res1[0:3], -box["moved"]], axis=0)
        box["solid2"] = solid2
        box["cross"] = against(known)
        box["own"] = jnp.sum(jnp.sum(known * known, axis=1, keepdims=True), axis=0, keepdims=True)
        box["old"] = jnp.sum(jnp.sum(known * res1, axis=1, keepdims=True), axis=0, keepdims=True)

    edge_work = (
        (lambda: place(edge_half[0]),),
        *((),) * (NCH // 2 - 1),
        (lambda: place(edge_half[1]),),
        *((),) * (NCH // 2 - 1),
    )
    edges(4, pa, pb, True, edge_work)
    edges(
        5,
        pb,
        pa,
        True,
        (
            (back_first, lambda: place(inner_rows), lambda: inside(pa, pb)),
            (moved_along,),
            (wall_second,),
            (),
        ),
    )
    edges(
        6,
        pa,
        pb,
        True,
        ((lambda: inside(pb, pa),), (lambda: each(m_moved, a_moved, MOVED),), (shift,), ()),
    )
    edges(
        7,
        pb,
        pa,
        False,
        (
            (lambda: inside(pa, pb),),
            (lambda: inside(pb, pa), sampled("seen2", 0, half, True)),
            (sampled("seen2", half, SLOTS, False), solid_second),
            (sampled_edge("seen2"),),
        ),
    )
    out1, shifted, trace, solid2 = box["out1"], box["shifted"], box["trace"], box["solid2"]
    cross_known, own_known, old_known = box["cross"], box["own"], box["old"]
    save = pltpu.make_async_copy(pa.at[:, pl.ds(8, NY), :], p_out, out_sem)
    save.start()
    all_arrived(a_moved, MOVED)
    cut_planes(ends, 1)
    seen2 = sample(edge_half[1], (0, SLOTS), none) + box["seen2"]
    gained = seen2 - seen1
    cells_msg = a_cells[:, 0, :]
    n_n = pltpu.roll(cells_msg, LANES - 2 * SLOTS, 1)
    n_t = pltpu.roll(cells_msg, LANES - 3 * SLOTS, 1)
    single = iota((D, LANES), 1) < SLOTS
    own = jnp.where(single, gained * (gained * n_n + 2.0 * a_moved[:, 0, :]), 0.0)
    old = jnp.where(single, gained * (seen1 * n_n + n_t), 0.0)
    own = own_known + jnp.sum(jnp.sum(own, axis=0, keepdims=True), axis=1, keepdims=True)
    old = old_known + jnp.sum(jnp.sum(old, axis=0, keepdims=True), axis=1, keepdims=True)
    lane = iota((1, LANES), 1)
    cross = as_row(cross_known - owned(gained))
    m_last[...] = jnp.where(lane == H, own, jnp.where(lane == H + 1, old, cross))
    same(m_last, a_last, LAST)
    m_back2[:, 0, :] = seen2
    each(m_back2, a_back2, BACK2)
    all_arrived(a_last, LAST)
    last = jnp.sum(a_last[...], axis=0)
    own, old = last[:, H : H + 1], last[:, H + 1 : H + 2]
    cross = jnp.where((lane > 0) & (lane < H), pltpu.roll(last, 1, 1), jnp.where(lane == 0, own, 0.0))
    h_row = pltpu.roll(jnp.where(lane < H, h_row, 0.0), 1, 1)
    h_row = jnp.where(lane == 0, own + old, h_row + cross)
    lanes = iota((H, LANES), 1)
    first = iota((H, LANES), 0) == 0
    gram = jnp.where(first, cross, jnp.where(lanes == 0, as_col(cross), shifted))
    ridge = RIDGE * (trace + own) / H + TINY
    gram = gram + jnp.where(square, ridge, 0.0)
    gram = jnp.where(lanes == H, as_col(h_row), gram)
    coeffs = -eliminate(gram, H)[:, H : H + 1]
    rest = pltpu.roll(coeffs * jnp.ones((H, LANES), F32), H - 1, 0)[:, 0:1]
    rest = jnp.where(iota((H, 1), 0) < H - 1, rest, 0.0)
    state = combine(rest, jnp.zeros((6, IF), F32))
    all_arrived(a_back2, BACK2)
    out2 = jnp.concatenate([solid2, -unpack(a_back2) * nrm], axis=0)
    state_out[...] = out2 + coeffs[0:1, :] * (out2 - out1) + state

    for arrived, r in (
        (a_cells, CELLS),
        (a_weights, WEIGHTS),
        (a_solid, SOLID),
        (a_first, FIRST),
        (a_back, BACK),
        (a_moved, MOVED),
        (a_wall1, WALL1),
        (a_wall2, WALL2),
        (a_back2, BACK2),
        (a_last, LAST),
    ):
        all_sent(arrived, r)
    for ch in range(NCH):
        for copy in halo(pb, SWEEPS * COUPLE - 1, ch):
            copy.wait_send()
    for part, r in ((g_one.at[pl.ds(0, LO - 1)], 0), (g_two.at[pl.ds(0, HI - 1)], 1)):
        remote(part, part, tree_send.at[r], tree_recv.at[r], right).wait_send()
    save.wait()


def finish(*refs):
    sources, targets, stages, sem = refs[:3], refs[3:6], refs[6:9], refs[9]
    triples = []
    for source, stage, target in zip(sources, stages, targets, strict=True):
        if len(source.shape) == 3:
            triples += [(source.at[i], stage.at[i], target.at[i]) for i in range(source.shape[0])]
        else:
            triples.append((source, stage, target))
    come = [pltpu.make_async_copy(a, b, sem.at[0, i]) for i, (a, b, _) in enumerate(triples)]
    leave = [pltpu.make_async_copy(b, c, sem.at[1, i]) for i, (_, b, c) in enumerate(triples)]
    for copy in come:
        copy.start()
    for a, b in zip(come, leave, strict=True):
        a.wait()
        b.start()
    for copy in leave:
        copy.wait()


def local(cfg, *args):
    (D, SP, LO, CX, NY, NZ, L3, W1, S2, IF, H, NCH, RC) = cfg
    (p, coef, rhs, ws, stiff, load, normals, owner, cell, x, vres, vout) = args
    vres, vout = vres.transpose(1, 0, 2), vout.transpose(1, 0, 2)
    R, K = CX * NY, SLOTS * D
    EX = SWEEPS * COUPLE
    wide = LANES
    G = 8

    def vmem(*shape, dtype=F32):
        return pltpu.VMEM(shape, dtype)

    dma = pltpu.SemaphoreType.DMA
    scratch = [
        vmem(CX, NY + 16, NZ), vmem(CX, NY + 16, NZ), vmem(CX, NY, NZ), vmem(R, NZ), vmem(R, NZ),
        vmem(EX, NY, NZ), vmem(EX, NY, NZ),
        vmem(R, K, dtype=BF16), vmem(K, R, dtype=BF16), vmem(K, NZ, dtype=BF16), vmem(K, NZ, dtype=BF16),
        vmem(R, NZ, dtype=BF16), vmem(R, NZ, dtype=BF16),
        vmem(3, L3, W1, S2), vmem(L3, W1, S2), vmem(3, L3, W1, S2),
        vmem(3, IF), vmem(1, IF, dtype=jnp.int32), vmem(1, IF, dtype=jnp.int32), vmem(6, IF),
        vmem(6, H, IF), vmem(6, H, IF),
        vmem(D, IF), vmem(LANES, IF),
        vmem(D, 1, wide), vmem(D, 1, wide), vmem(D, 8, wide), vmem(D, 8, wide),
        vmem(D, 1, wide), vmem(D, 1, wide), vmem(D, 1, wide), vmem(D, 1, wide), vmem(D, 1, wide), vmem(D, 1, wide),
        vmem(D, 1, wide), vmem(D, 1, wide),
        vmem(1, wide), vmem(D, 1, wide), vmem(1, wide), vmem(D, 1, wide),
        vmem(W1 + 2, 3, L3, S2), vmem(W1 + 2, L3, S2), vmem(W1 + 4, 3, L3, S2), vmem(W1 + 4, 3, L3, S2),
        vmem(W1, 3, L3, S2), vmem(W1, 3, L3, S2),
        vmem(G, wide), vmem(LO, G, wide), vmem(G, wide), vmem(D // LO, G, wide),
        vmem(1, wide), vmem(D, 1, wide), vmem(1, wide), vmem(D, 1, wide),
        vmem(LANES, IF), vmem(D, SLOTS, dtype=jnp.int32),
        dma((11 + 2 * CX,)), dma((ROUNDS,)), dma((ROUNDS,)), dma((EX, 2, NCH)), dma((EX, 2, NCH)),
        dma((4, 2)), dma((4, 2)), dma((4,)), dma((4,)), dma(()),
    ]
    anywhere = pl.BlockSpec(memory_space=pl.ANY)
    inside = pl.BlockSpec(memory_space=pltpu.VMEM)
    shapes = (
        jax.ShapeDtypeStruct((6, IF), F32),
        jax.ShapeDtypeStruct((CX, NY, NZ), F32),
        jax.ShapeDtypeStruct((3, L3, W1, S2), F32),
    )
    results = pl.pallas_call(
        functools.partial(kernel, cfg),
        out_shape=shapes,
        in_specs=[anywhere] * 12,
        out_specs=(inside, anywhere, inside),
        scratch_shapes=scratch,
        compiler_params=pltpu.CompilerParams(
            collective_id=0, has_side_effects=True, vmem_limit_bytes=60 * 2**20
        ),
    )(
        p, coef, rhs.reshape(R, NZ), ws, stiff, load, normals,
        owner.reshape(1, IF), cell.reshape(1, IF), x, vres, vout,
    )
    return pl.pallas_call(
        finish,
        out_shape=shapes,
        in_specs=[anywhere] * 3,
        out_specs=(anywhere,) * 3,
        scratch_shapes=[vmem(6, IF), vmem(CX, NY, NZ), vmem(3, L3, W1, S2), dma((2, CX + 2))],
    )(*results)


def solution(mesh):
    sp = mesh.shape["space"]
    devices = mesh.shape["solver"] * sp

    def run(*args):
        CX, NY, NZ = args[0].shape
        _, L3, W1, S2 = args[3].shape
        IF, H = args[8].shape[0], args[10].shape[0]
        lo = 8 if devices > 8 else 4
        cfg = (devices, sp, lo, CX, NY, NZ, L3, W1, S2, IF, H, 4, min(32, NY // 4))
        return local(cfg, *args)

    in_specs = (
        P(BOTH, None, None),
        P(BOTH, None, None),
        P(BOTH, None, None),
        P(None, None, BOTH, None),
        P(None, BOTH, None),
        P(None, None, BOTH, None),
        P(None, BOTH),
        P(BOTH, None),
        P(BOTH),
        P(None, BOTH),
        P(None, None, BOTH),
        P(None, None, BOTH),
    )
    out_specs = (P(None, BOTH), P(BOTH, None, None), P(None, None, BOTH, None))
    return jax.shard_map(run, mesh=mesh, in_specs=in_specs, out_specs=out_specs, check_vma=False)
```
